32 devices in a mesh: gx: 2 (over x), gy: 4 (over y, core), gz: 4 (over z).
Axes of the slice: x: 2, y: 2, z: 4, core: 2. Of those that a mesh axis runs over, the one named last changes fastest.
Arguments:
- velocity: float32 [3, 32, 64, 512], P(None, 'gx', 'gy', 'gz'), may hold values from -6 to 6
- gradients: bfloat16 [2, 3, 32, 64, 512], P(None, None, 'gx', 'gy', 'gz'), may hold values from -6 to 6
- shift_x: int32 [2, 4, 8, 4], P(None, 'gx', 'gy', 'gz'), may hold values from -6 to 6
- shift_y: int32 [2, 4, 8, 4], P(None, 'gx', 'gy', 'gz'), may hold values from -6 to 6
- shift_z: int32 [2, 4, 8, 4], P(None, 'gx', 'gy', 'gz'), may hold values from -14 to 14
- fractions: int32 [2, 3, 4, 8, 4], P(None, None, 'gx', 'gy', 'gz'), may hold values from 0 to 7
Outputs:
- hess_vec: float32 [3, 32, 64, 512], P(None, 'gx', 'gy', 'gz')
The draws below stay inside these ranges and needn't reach their ends.
All inputs are finite; a program needn't handle non-finite values.
Results may differ from the reference program's by a relative error of at most 0.0003.
Values sent between devices are 32-bit elements; how exact they have to be, the bound alone decides.
A program may use at most 64 MiB of HBM per device.

```python
import jax
import jax.numpy as jnp
from jax import lax

BX = 8
BY = 8
BZ = 128
RX = 6
RY = 6
RZ = 14
STEPS = 2
NX = 32
NY = 64
NZ = 512
NBX = 4
NBY = 8
NBZ = 4


def set_ends(array, rng, smallest, largest):
    place = [jax.random.randint(jax.random.fold_in(rng, axis), (), 0, length) for axis, length in enumerate(array.shape)]
    main_axis = array.shape.index(max(array.shape))
    neighbour = place[:main_axis] + [(place[main_axis] + 1) % array.shape[main_axis]] + place[main_axis + 1:]
    return array.at[tuple(place)].set(smallest).at[tuple(neighbour)].set(largest)


def level_of(rng, dims, pieces, least, high):
    loudness = 1.0
    for axis_at, blocks in pieces:
        heights = jax.random.uniform(jax.random.fold_in(jax.random.fold_in(rng, 6), axis_at), (blocks,), jnp.float32, least / len(pieces), high / len(pieces))
        loudness = loudness * jnp.repeat(jnp.exp(heights), dims[axis_at] // blocks).reshape((-1,) + (1,) * (len(dims) - 1 - axis_at))
    return loudness


def gaussian(own_key, shape, spread, bound, cuts=(), kind=jnp.bfloat16):
    array = jax.random.normal(own_key, shape, jnp.float32) * spread
    if len(cuts) > 0:
        array = level_of(own_key, shape, cuts, -0.22, 0.18) * array
    return jnp.clip(array, min=-bound, max=bound).astype(kind)


def setup_inputs(seed: int = 0) -> dict:
    seeds = jax.random.split(jax.random.key(seed), 7)
    velocity = gaussian(seeds[0], (3, NX, NY, NZ), 1.0, 6.0, ((1, 2), (2, 4), (3, 4)), jnp.float32)
    gradients = gaussian(seeds[1], (STEPS, 3, NX, NY, NZ), 1.0, 6.0, ((2, 2), (3, 4), (4, 4)))
    shift_x = set_ends(jax.random.randint(seeds[2], (STEPS, NBX, NBY, NBZ), 0 - RX, RX + 1), jax.random.fold_in(seeds[2], 1), 0 - RX, RX).astype(jnp.int32)
    shift_y = set_ends(jax.random.randint(seeds[3], (STEPS, NBX, NBY, NBZ), 0 - RY, RY + 1), jax.random.fold_in(seeds[3], 1), 0 - RY, RY).astype(jnp.int32)
    shift_z = set_ends(jax.random.randint(seeds[4], (STEPS, NBX, NBY, NBZ), 0 - RZ, RZ + 1), jax.random.fold_in(seeds[4], 1), 0 - RZ, RZ).astype(jnp.int32)
    fractions = set_ends(jax.random.randint(seeds[5], (STEPS, 3, NBX, NBY, NBZ), 0, 8), jax.random.fold_in(seeds[5], 1), 0, 7).astype(jnp.int32)
    return {"velocity": velocity, "gradients": gradients, "shift_x": shift_x, "shift_y": shift_y, "shift_z": shift_z, "fractions": fractions}


STEP_SIZE = 0.5
REG_WEIGHT = 0.1
LAPLACE_TAPS = (-205.0 / 72.0, 8.0 / 5.0, -1.0 / 5.0, 8.0 / 315.0, -1.0 / 560.0)


def cubic_weights(fractions):
    fraction = fractions.astype(jnp.float32) / 8.0
    squared = fraction * fraction
    cubed = squared * fraction
    taps = jnp.stack([0.5 * (2.0 * squared - cubed - fraction), 0.5 * (3.0 * cubed - 5.0 * squared + 2.0), 0.5 * (4.0 * squared - 3.0 * cubed + fraction), 0.5 * (cubed - squared)], axis=-1)
    return taps.reshape(3, -1, 4)


def block_starts(shift_x, shift_y, shift_z):
    count_x, count_y, count_z = shift_x.shape
    base_x = jnp.arange(count_x, dtype=jnp.int32)[:, None, None] * BX
    base_y = jnp.arange(count_y, dtype=jnp.int32)[None, :, None] * BY
    base_z = jnp.arange(count_z, dtype=jnp.int32)[None, None, :] * BZ
    start_x = (base_x + shift_x + (RX + 1)).astype(jnp.int32).reshape(-1)
    start_y = (base_y + shift_y + (RY + 1)).astype(jnp.int32).reshape(-1)
    start_z = (base_z + shift_z + (RZ + 1)).astype(jnp.int32).reshape(-1)
    return start_x, start_y, start_z


def apply_cubic(window, weight_x, weight_y, weight_z):
    span_z = window.shape[2] - 3
    along_z = sum(weight_z[a] * window[:, :, a:a + span_z] for a in range(4))
    span_y = window.shape[1] - 3
    along_y = sum(weight_y[a] * along_z[:, a:a + span_y, :] for a in range(4))
    span_x = window.shape[0] - 3
    return sum(weight_x[a] * along_y[a:a + span_x] for a in range(4))


def transpose_cubic(values, weight_x, weight_y, weight_z):
    along_x = sum(weight_x[a] * jnp.pad(values, ((a, 3 - a), (0, 0), (0, 0))) for a in range(4))
    along_y = sum(weight_y[a] * jnp.pad(along_x, ((0, 0), (a, 3 - a), (0, 0))) for a in range(4))
    return sum(weight_z[a] * jnp.pad(along_y, ((0, 0), (0, 0), (a, 3 - a))) for a in range(4))


def to_blocks(field):
    tile_x, tile_y, tile_z = field.shape
    split = field.reshape(tile_x // BX, BX, tile_y // BY, BY, tile_z // BZ, BZ)
    return split.transpose(0, 2, 4, 1, 3, 5).reshape(-1, BX, BY, BZ)


def from_blocks(blocks, tile_x, tile_y, tile_z):
    split = blocks.reshape(tile_x // BX, tile_y // BY, tile_z // BZ, BX, BY, BZ)
    return split.transpose(0, 3, 1, 4, 2, 5).reshape(tile_x, tile_y, tile_z)


def spread_blocks(field, start_x, start_y, start_z, weights):
    values = to_blocks(field)
    accumulated = jnp.zeros((field.shape[0] + 2 * (RX + 2), field.shape[1] + 2 * (RY + 2), field.shape[2] + 2 * (RZ + 2)), jnp.float32)

    def add_block(b, accumulated):
        window = transpose_cubic(values[b], weights[0, b], weights[1, b], weights[2, b])
        corner = (start_x[b], start_y[b], start_z[b])
        current = lax.dynamic_slice(accumulated, corner, window.shape)
        return lax.dynamic_update_slice(accumulated, current + window, corner)

    return lax.fori_loop(0, values.shape[0], add_block, accumulated)


def neg_laplacian(padded):
    tile_x = padded.shape[1] - 8
    tile_y = padded.shape[2] - 8
    tile_z = padded.shape[3] - 8

    def shifted(off_x, off_y, off_z):
        return padded[:, 4 + off_x:4 + off_x + tile_x, 4 + off_y:4 + off_y + tile_y, 4 + off_z:4 + off_z + tile_z]

    result = (3.0 * LAPLACE_TAPS[0]) * shifted(0, 0, 0)
    for k in range(1, 5):
        result = result + LAPLACE_TAPS[k] * (shifted(k, 0, 0) + shifted(-k, 0, 0) + shifted(0, k, 0) + shifted(0, -k, 0) + shifted(0, 0, k) + shifted(0, 0, -k))
    return -result


def advect(field, shift_x, shift_y, shift_z, fractions):
    padded = jnp.pad(field, ((RX + 2, RX + 2), (RY + 2, RY + 2), (RZ + 2, RZ + 2)))
    start_x, start_y, start_z = block_starts(shift_x, shift_y, shift_z)
    weights = cubic_weights(fractions)

    def one_block(block_items):
        corner_x, corner_y, corner_z, weight_x, weight_y, weight_z = block_items
        window = lax.dynamic_slice(padded, (corner_x, corner_y, corner_z), (BX + 3, BY + 3, BZ + 3))
        return apply_cubic(window, weight_x, weight_y, weight_z)

    blocks = lax.map(one_block, (start_x, start_y, start_z, weights[0], weights[1], weights[2]))
    return from_blocks(blocks, field.shape[0], field.shape[1], field.shape[2])


def advect_transposed(field, shift_x, shift_y, shift_z, fractions):
    start_x, start_y, start_z = block_starts(shift_x, shift_y, shift_z)
    weights = cubic_weights(fractions)
    accumulated = spread_blocks(field, start_x, start_y, start_z, weights)
    return accumulated[RX + 2:RX + 2 + field.shape[0], RY + 2:RY + 2 + field.shape[1], RZ + 2:RZ + 2 + field.shape[2]]


def reference(velocity, gradients, shift_x, shift_y, shift_z, fractions):
    state = jnp.zeros(velocity.shape[1:], jnp.float32)
    for k in range(STEPS):
        source = state + STEP_SIZE * jnp.sum(gradients[k].astype(jnp.float32) * velocity, axis=0)
        state = advect(source, shift_x[k], shift_y[k], shift_z[k], fractions[k])
    adjoint = state
    gauss_term = jnp.zeros_like(velocity)
    for k in reversed(range(STEPS)):
        adjoint = advect_transposed(adjoint, shift_x[k], shift_y[k], shift_z[k], fractions[k])
        gauss_term = gauss_term + STEP_SIZE * gradients[k].astype(jnp.float32) * adjoint[None]
    faces = jnp.pad(velocity, ((0, 0), (4, 4), (4, 4), (4, 4)))
    regular = REG_WEIGHT * neg_laplacian(faces)
    return regular + gauss_term
```

```python
import functools

import jax
import jax.numpy as jnp
from jax import lax
from jax.experimental import pallas as pl
from jax.experimental.pallas import tpu as pltpu
from jax.sharding import PartitionSpec as P

BX = 8
BY = 8
BZ = 128
RX = 6
RY = 6
RZ = 14
STEPS = 2

STEP_SIZE = 0.5
REG_WEIGHT = 0.1
LAPLACE_TAPS = (-205.0 / 72.0, 8.0 / 5.0, -1.0 / 5.0, 8.0 / 315.0, -1.0 / 560.0)

HX = RX + 2
HY = RY + 2
HZ = RZ + 2
LANES = 128
PK = LANES // HZ
XG = HX // PK
LH = 4
VPK = LANES // (2 * LH)
WX = BX + 2 * HX
WY = BY + 2 * HY
TILE = 8
MESH = pl.DeviceIdType.MESH
AXES = ("gx", "gy", "gz")
WAYS = sorted(((i, j, k) for i in (-1, 0, 1) for j in (-1, 0, 1) for k in (-1, 0, 1) if (i, j, k) != (0, 0, 0)),
              key=lambda d: (not d[0], sum(map(abs, d))))


def piece(way, own, halo):
    return {-1: (0, halo), 0: (halo, halo + own), 1: (halo + own, 2 * halo + own)}[way]


def border(way, own, halo):
    return {-1: (halo, 2 * halo), 0: (halo, halo + own), 1: (own, halo + own)}[way]


def kernel(shape, vel_in, grad_in, shx_in, shy_in, shz_in, frac_in, out,
           vel, grad, shx, shy, shz, frac, arrive,
           E0, E1, LX, U, YP, XP, ACC0, ACC1, BK0, BK1, ADJ, SP,
           VE, YSU, YSD, YVD, YVU, SV, VRD, VRU, BULK, send, recv):
    TX, TY, TZ = vel.shape[1:]
    NBX, NBY = TX // BX, TY // BY
    EX = TX + 2 * HX
    EY = TY + 2 * HY
    EG = EX // PK
    G = TX // PK
    OX = slice(HX, HX + TX)
    OY = slice(HY, HY + TY)
    NT = TY // TILE

    at = {a: lax.axis_index(a) for a in AXES}

    def has(way):
        ok = None
        for a, w in zip(AXES, way):
            if w:
                one = at[a] < shape[a] - 1 if w > 0 else at[a] > 0
                ok = one if ok is None else jnp.logical_and(ok, one)
        return ok

    def device(way):
        return {a: at[a] + w for a, w in zip(AXES, way) if w}

    up = (at["gx"] == 0).astype(jnp.int32)

    def column(i):
        return i * up + (NBX - 1 - i) * (1 - up)

    def group_of(q):
        return q * up + (EG - 1 - q) * (1 - up)

    loads = []

    def load(src, dst):
        loads.append(pltpu.make_async_copy(src, dst, arrive.at[len(loads)]))
        loads[-1].start()
        return loads[-1]

    def part(ref, i):
        return ref.at[:, pl.ds(column(i) * BX, BX)]

    sources = [(load(part(vel_in, i), part(vel, i)), load(part(grad_in.at[0], i), part(grad.at[0], i)))
               for i in reversed(range(NBX))]
    later = [load(a, b) for a, b in ((shx_in, shx), (shy_in, shy), (shz_in, shz), (frac_in, frac),
                                     (grad_in.at[1], grad.at[1]))]

    barrier = pltpu.get_barrier_semaphore()
    total = jnp.int32(0)
    for way in WAYS:
        @pl.when(has(way))
        def _(way=way):
            pl.semaphore_signal(barrier, inc=1, device_id=device(way), device_id_type=MESH)
        total = total + has(way).astype(jnp.int32)

    def counts(a):
        n = (at[a] > 0).astype(jnp.int32) + (at[a] < shape[a] - 1).astype(jnp.int32)
        return [(v, n == v if shape[a] > 2 else None) for v in ((0,), (1,), (1, 2))[min(shape[a], 3) - 1]]

    def wait_for(sem, tiles, axes, also=None):
        combos = [((), also)]
        for a in axes:
            combos = [(vs + (v,), c if ok is None else ok if c is None else jnp.logical_and(c, ok))
                      for vs, c in combos for v, ok in counts(a)]
        for vs, ok in combos:
            n = tiles(*vs)
            if not n:
                continue
            wait = pltpu.make_async_copy(BULK.at[0:n], BULK.at[0:n], sem).wait
            if ok is None:
                wait()
            else:
                pl.when(ok)(wait)

    def tiles_of(x, y, z):
        return x * y * z // (TILE * LANES)

    def wait_rest(n):
        wait_for(recv.at[3 * n], lambda y, z: tiles_of(TX, TY + HY * y, LANES + HZ * z) - tiles_of(TX, TY, LANES),
                 ("gy", "gz"))

    def wait_x(n, side, also=None):
        ok = has((side, 0, 0))
        wait_for(recv.at[3 * n + (1 if side < 0 else 2)], lambda y, z: tiles_of(HX, TY + HY * y, LANES + HZ * z),
                 ("gy", "gz"), ok if also is None else jnp.logical_and(ok, also))

    def wait_far(n):
        if shape["gx"] > 2:
            wait_x(n, 1, up == 0)

    def wait_near(n):
        wait_x(n, -1)
        wait_x(n, 1, up == 1 if shape["gx"] > 2 else None)

    def wait_sent(n):
        wait_for(send.at[n], lambda x, y, z: tiles_of(TX + HX * x, TY + HY * y, LANES + HZ * z) - tiles_of(TX, TY, LANES),
                 AXES)

    def start(src, dst, way, sent, came):
        desc = pltpu.make_async_remote_copy(
            src_ref=src, dst_ref=dst, send_sem=send.at[sent], recv_sem=recv.at[came],
            device_id=device(way), device_id_type=MESH)
        pl.when(has(way))(desc.start)

    lane2 = lax.broadcasted_iota(jnp.int32, (1, LANES), 1)
    group = lane2 // HZ
    edge = jnp.logical_or(lane2 < HZ, lane2 >= LANES - HZ)

    def packed(layer):
        first = last = None
        for j in range(PK):
            turned = pltpu.roll(layer(j), HZ * j, 1) if j else layer(0)
            first = turned if j == 0 else jnp.where(group == j, turned, first)
            last = turned if j == 0 else jnp.where(group == j - 1, turned, last)
        return first, last

    def unpacked(first, last, j):
        both = jnp.where(group == j, first, last)
        return pltpu.roll(both, LANES - HZ * j, 1) if j else both

    def region(way, dim_of):
        (x0, x1) = dim_of(way[0], G if way[2] else TX, XG if way[2] else HX)
        (y0, y1) = dim_of(way[1], TY, HY)
        return slice(x0, x1), slice(y0, y1)

    def rim(ref, way):
        xs, ys = region(way, piece)
        base = {0: 0, -1: EX, 1: EX + EG}[way[2]]
        return ref.at[slice(base + xs.start, base + xs.stop), ys, :]

    def landing(k, way):
        x = {0: slice(0, HX), -1: slice(HX, HX + XG), 1: slice(HX + XG, HX + 2 * XG)}[way[2]]
        return LX.at[k, (way[0] + 1) // 2, x, region(way, piece)[1], :]

    def forward_send(E, k, n, ways):
        for way in ways:
            xs, ys = region(way, border)
            src = SP.at[k, 0 if way[2] < 0 else 1, xs, ys, :] if way[2] else E.at[xs, ys, :]
            other = tuple(-w for w in way)
            start(src, landing(k, other) if way[0] else rim(E, other), way, n, 3 * n + (0, 1, 2)[way[0]])

    def return_send(ACC, BK, n, ways):
        for way in ways:
            other = tuple(-w for w in way)
            start(rim(ACC, way), rim(BK, other), way, n, 3 * n + (0, 1, 2)[way[0]])

    X_WAYS = [w for w in WAYS if w[0]]
    REST = [w for w in WAYS if not w[0]]

    def pack_column(E, k, bx):
        SP[k, 0, XG + bx, OY, :], SP[k, 1, XG + bx, OY, :] = packed(lambda j: E[HX + bx * BX + j, OY, :])

    def unpack(below, above, g):
        for j in range(PK):
            U[PK * g + j] = unpacked(above, below, j)

    def taps(k, d, bx, by):
        e = frac[k, bx, by, 0, d].astype(jnp.float32) * 0.125
        e2 = e * e
        e3 = e2 * e
        return (0.5 * (2.0 * e2 - e3 - e), 0.5 * (3.0 * e3 - 5.0 * e2 + 2.0),
                0.5 * (4.0 * e2 - 3.0 * e3 + e), 0.5 * (e3 - e2))

    def total_of(terms):
        return functools.reduce(lambda a, b: a + b, terms)

    def gather_block(E, k, bx, by):
        a, b, c = shx[k, bx, 0, by], shy[k, bx, 0, by], shz[k, bx, 0, by]
        wx, wy, wz = (taps(k, d, bx, by) for d in range(3))
        x0 = bx * BX + (a + HX - 1)
        y0 = by * BY + (b + HY - 1)
        along = []
        for ref in (E, U):
            rows = [total_of(wy[v] * ref[x0 + m, pl.ds(y0 + v, BY), :] for v in range(4)) for m in range(BX + 3)]
            along.append([total_of(wx[u] * rows[m + u] for u in range(4)) for m in range(BX)])
        own, rest = (jnp.concatenate(p, axis=0) for p in along)
        res = None
        for w in range(4):
            s = c + (w - 1)
            inside = jnp.logical_and(lane2 >= s, lane2 < LANES + s)
            term = wz[w] * pltpu.roll(jnp.where(inside, own, rest), lax.rem(LANES - s, LANES), 1)
            res = term if res is None else res + term
        return [res[BY * m:BY * (m + 1)] for m in range(BX)]

    def spread_block(vals, k, i, bx, by):
        n = i * NBY + by
        c = shz[k, bx, 0, by]
        wx, wy, wz = (taps(k, d, bx, by) for d in range(3))
        flat = jnp.concatenate(vals, axis=0)
        own = rest = None
        for w in range(4):
            s = c + (w - 1)
            inside = jnp.logical_and(lane2 >= s, lane2 < LANES + s)
            term = wz[w] * pltpu.roll(flat, lax.rem(LANES + s, LANES), 1)
            o, r = jnp.where(inside, term, 0.0), jnp.where(inside, 0.0, term)
            own, rest = (o, r) if own is None else (own + o, rest + r)
        for p, zs in enumerate((own, rest)):
            z = [zs[BY * m:BY * (m + 1)] for m in range(BX)]
            for m in range(BX + 3):
                YP[n, p, m, TILE:TILE + BY, :] = total_of(wx[u] * z[m - u] for u in range(4) if 0 <= m - u < BX)
            for m in range(BX + 3):
                XP[n, p, 2 * HX + m, 2 * TILE:2 * TILE + 2 * BY, :] = total_of(
                    wy[v] * YP[n, p, m, TILE - v:TILE - v + 2 * BY, :] for v in range(4))

    def collect(ACC, k, q):
        g = group_of(q)
        found = []
        for i in range(NBX):
            if 0 <= q - i <= 2:
                bx = column(i)
                offset = BX * ((q - i) * up + (2 - q + i) * (1 - up))
                for by in range(NBY):
                    found.append((i * NBY + by, by, (HX + 1) - shx[k, bx, 0, by] + offset,
                                  (2 * TILE - HY + 1) - shy[k, bx, 0, by]))

        def layer(p, j):
            tiles = [None] * (EY // TILE)
            for n, by, x0, y0 in found:
                rows = XP[n, p, x0 + j, pl.ds(y0, WY), :]
                for r in range(WY // TILE):
                    one = rows[r * TILE:(r + 1) * TILE]
                    old = tiles[by + r]
                    tiles[by + r] = one if old is None else old + one
            return jnp.concatenate(tiles, axis=0)

        for j in range(PK):
            ACC[PK * g + j] = layer(0, j)
        rims = [layer(1, j) for j in range(PK)]
        ACC[EX + EG + g], ACC[EX + g] = packed(lambda j: rims[j])

    def received(ACC, BK, i):
        bx = column(i)
        halos = ([0] if i == 0 and shape["gx"] > 2 else []) + ([EG - 1] if i == NBX - 1 else [])
        halos = [group_of(q) for q in halos]

        def rows(center, L):
            tiles = [center[L, HY + TILE * t:HY + TILE * (t + 1), :] for t in range(NT)]
            tiles[0] = tiles[0] + BK[L, 0:HY, :]
            tiles[-1] = tiles[-1] + BK[L, HY + TY:, :]
            return jnp.concatenate(tiles, axis=0)

        rims = []
        for base in (EX, EX + EG):
            rims.append(total_of([rows(BK, base + XG + bx)] + [rows(BK, base + g) for g in halos]))
        first, last = rims
        res = []
        for j in range(BX):
            one = total_of([rows(ACC, HX + bx * BX + j)] + [rows(BK, PK * g + j) for g in halos])
            res.append(one + jnp.where(edge, unpacked(first, last, j), 0.0))
        return res

    def blocks(layers, by):
        return [one[by * BY:(by + 1) * BY] for one in layers]

    def product(k, bx, j):
        return STEP_SIZE * total_of(grad[k, c, bx * BX + j].astype(jnp.float32) * vel[c, bx * BX + j] for c in range(3))

    def clear(a, first, last):
        for end, views in ((0, first), (shape[a] - 1, last)):
            @pl.when(at[a] == end)
            def _(views=views):
                for ref in views:
                    ref[...] = jnp.zeros_like(ref)

    def clear_missing():
        sides = ((slice(0, HX), slice(EX, EX + XG), slice(EX + EG, EX + EG + XG)),
                 (slice(HX + TX, EX), slice(EX + XG + G, EX + EG), slice(EX + EG + XG + G, EX + 2 * EG)))
        low, high = ([BK.at[x] for BK in (BK0, BK1) for x in side] for side in sides)
        clear("gx", low + [LX.at[:, 0], VE.at[:, 0:LH]], high + [LX.at[:, 1], VE.at[:, LH + TX:]])
        ends = slice(0, HY), slice(HY + TY, EY)
        low, high = ([ref.at[:, y] for ref in (E0, E1, BK0, BK1)] + [LX.at[:, :, :, y]] for y in ends)
        clear("gy", low + [YVD], high + [YVU])
        low, high = ([ref.at[x] for ref in (E0, E1, BK0, BK1)] for x in (slice(EX, EX + EG), slice(EX + EG, EX + 2 * EG)))
        clear("gz", low + [LX.at[:, :, HX:HX + XG], VRD], high + [LX.at[:, :, HX + XG:], VRU])

    def send_faces():
        n = 4
        copies = [((1, 0, 0), vel.at[:, TX - LH:TX], VE.at[:, 0:LH, OY, :]),
                  ((-1, 0, 0), vel.at[:, 0:LH], VE.at[:, LH + TX:2 * LH + TX, OY, :])]
        for way, src, dst in copies:
            start(src, dst, way, n, 3 * n)
        VE[:, LH:LH + TX, OY, :] = vel[...]
        for c in range(3):
            for i in range(TX // 2):
                for h in range(2):
                    YSU[c, i, LH * h:LH * (h + 1), :] = vel[c, 2 * i + h, TY - LH:TY, :]
                    YSD[c, i, LH * h:LH * (h + 1), :] = vel[c, 2 * i + h, 0:LH, :]
            for g in range(TX // VPK):
                row = None
                for j in range(VPK):
                    turned = pltpu.roll(vel[c, VPK * g + j], (2 * LH * j + LH) % LANES, 1)
                    row = turned if row is None else jnp.where(lane2 // (2 * LH) == j, turned, row)
                SV[c, g] = row
        for way, src, dst in (((0, 1, 0), YSU, YVD), ((0, -1, 0), YSD, YVU),
                              ((0, 0, 1), SV, VRD), ((0, 0, -1), SV, VRU)):
            start(src, dst, way, n, 3 * n)

    def face_tiles(x, y, z):
        return (x * tiles_of(3 * LH, TY, LANES) + y * tiles_of(3 * TX // 2, 2 * LH, LANES)
                + z * tiles_of(3 * TX // VPK, TY, LANES))

    def regular():
        wait_for(recv.at[12], face_tiles, AXES)
        for c in range(3):
            for i in range(TX // 2):
                for h in range(2):
                    VE[c, LH + 2 * i + h, HY - LH:HY, :] = YVD[c, i, LH * h:LH * (h + 1), :]
                    VE[c, LH + 2 * i + h, HY + TY:HY + TY + LH, :] = YVU[c, i, LH * h:LH * (h + 1), :]
        rows = lax.broadcasted_iota(jnp.int32, (2 * LANES, LANES), 0)
        cols = lax.broadcasted_iota(jnp.int32, (2 * LANES, LANES), 1)
        r = rows - LANES
        place = jnp.where(rows < LANES, rows, jnp.where(r < LH, r + LANES, r - LANES))
        known = jnp.logical_or(rows < LANES, jnp.logical_or(r < LH, r >= LANES - LH))
        gap = jnp.abs(place - cols)
        band = jnp.zeros((2 * LANES, LANES), jnp.float32)
        for k in range(5):
            tap = (3.0 if k == 0 else 1.0) * LAPLACE_TAPS[k]
            band = jnp.where(jnp.logical_and(known, gap == k), tap, band)
        for c in range(3):
            rims = []
            for g in range(TX // VPK):
                row = jnp.where(lane2 % (2 * LH) < LH, VRD[c, g], VRU[c, g])
                for j in range(VPK):
                    rims.append(pltpu.roll(row, (LANES - (2 * LH * j + LH)) % LANES, 1))
            rims = jnp.concatenate(rims, axis=0)
            own = vel[c].reshape(TX * TY, LANES)
            res = jnp.dot(jnp.concatenate([own, rims], axis=1), band,
                          preferred_element_type=jnp.float32,
                          precision=lax.Precision.HIGHEST).reshape(TX, TY, LANES)
            for k in range(1, 5):
                res = res + LAPLACE_TAPS[k] * (
                    VE[c, LH + k:LH + k + TX, OY, :] + VE[c, LH - k:LH - k + TX, OY, :]
                    + VE[c, LH:LH + TX, HY + k:HY + k + TY, :]
                    + VE[c, LH:LH + TX, HY - k:HY - k + TY, :])
            out[c] = (-REG_WEIGHT) * res

    met = False
    for i in reversed(range(NBX)):
        for copy in sources[NBX - 1 - i]:
            copy.wait()
        bx = column(i)
        for j in range(BX):
            E0[HX + bx * BX + j, OY, :] = product(0, bx, j)
        pack_column(E0, 0, bx)
        if not met and (i == NBX - 1 and shape["gx"] <= 2 or i == 0):
            pl.semaphore_wait(barrier, total)
            forward_send(E0, 0, 0, X_WAYS)
            met = True
    forward_send(E0, 0, 0, REST)

    clear_missing()
    send_faces()
    for copy in later:
        copy.wait()
    for i in range(NBX):
        for j in range(BX):
            E1[HX + column(i) * BX + j, OY, :] = product(1, column(i), j)
    YP[:, :, :, 0:TILE] = jnp.zeros_like(YP[:, :, :, 0:TILE])
    YP[:, :, :, TILE + BY:] = jnp.zeros_like(YP[:, :, :, TILE + BY:])
    XP[...] = jnp.zeros_like(XP)

    def enter(E, k, g, side):
        for j in range(HX):
            E[PK * g + j] = LX[k, side, j]
        unpack(LX[k, side, HX], LX[k, side, HX + XG], g)

    def forward(E, n, each):
        wait_rest(n)
        for i in range(NBX):
            g = XG + column(i)
            unpack(E[EX + g], E[EX + EG + g], g)
        for i in range(NBX):
            if i == 0:
                wait_far(n)
                enter(E, n, group_of(0), 1 - up)
            if i == NBX - 1:
                wait_near(n)
                enter(E, n, group_of(EG - 1), up)
            each(i, column(i))

    def first(i, bx):
        for by in range(NBY):
            res = gather_block(E0, 0, bx, by)
            for m in range(BX):
                rows = slice(HY + by * BY, HY + (by + 1) * BY)
                E1[HX + bx * BX + m, rows, :] = E1[HX + bx * BX + m, rows, :] + res[m]
        pack_column(E1, 1, bx)

    forward(E0, 0, first)
    forward_send(E1, 1, 1, X_WAYS)
    forward_send(E1, 1, 1, REST)

    def second(i, bx):
        for by in range(NBY):
            spread_block(gather_block(E1, 1, bx, by), 1, i, bx, by)

    forward(E1, 1, second)

    def give_back(ACC, BK, k, n):
        collect(ACC, k, EG - 1)
        if shape["gx"] > 2:
            collect(ACC, k, 0)
        return_send(ACC, BK, n, X_WAYS)
        for q in range(XG, XG + G):
            collect(ACC, k, q)
        return_send(ACC, BK, n, REST)

    def backward(ACC, BK, n, each):
        wait_rest(n)
        for i in range(NBX):
            if i == 0:
                wait_far(n)
            if i == NBX - 1:
                wait_near(n)
            each(i, column(i), received(ACC, BK, i))

    give_back(ACC1, BK1, 1, 2)
    regular()

    def third(i, bx, layers):
        for j in range(BX):
            ADJ[bx * BX + j] = layers[j]
        for by in range(NBY):
            spread_block(blocks(layers, by), 0, i, bx, by)

    backward(ACC1, BK1, 2, third)
    give_back(ACC0, BK0, 0, 3)

    for c in range(3):
        out[c] = out[c] + STEP_SIZE * grad[1, c].astype(jnp.float32) * ADJ[...]
    for n in range(3):
        wait_sent(n)
    wait_for(send.at[4], face_tiles, AXES)

    def fourth(i, bx, layers):
        for c in range(3):
            for j in range(BX):
                x = bx * BX + j
                out[c, x] = out[c, x] + STEP_SIZE * grad[0, c, x].astype(jnp.float32) * layers[j]

    backward(ACC0, BK0, 3, fourth)
    wait_sent(3)


def body(shape, velocity, gradients, shift_x, shift_y, shift_z, fractions):
    TX, TY, TZ = velocity.shape[1:]
    assert TZ == BZ == LANES and TX % VPK == 0 and TX % BX == 0 and TY % BY == 0
    assert BX == HX == PK and BY == HY == TILE and XG == 1
    EX, EY = TX + 2 * HX, TY + 2 * HY
    EG = EX // PK
    NB = (TX // BX) * (TY // BY)
    most = EX * EY * (LANES + 2 * HZ) // (TILE * LANES)

    vm = lambda *s: pltpu.VMEM(s, jnp.float32)
    vmem = pl.BlockSpec(memory_space=pltpu.VMEM)
    hbm = pl.BlockSpec(memory_space=pltpu.HBM)
    shift_x, shift_y, shift_z = (s.transpose(0, 1, 3, 2) for s in (shift_x, shift_y, shift_z))
    fractions = fractions.transpose(0, 2, 3, 4, 1)
    return pl.pallas_call(
        functools.partial(kernel, shape),
        out_shape=jax.ShapeDtypeStruct(velocity.shape, jnp.float32),
        in_specs=[hbm] * 6,
        out_specs=vmem,
        scratch_shapes=[
            pltpu.VMEM(velocity.shape, velocity.dtype), pltpu.VMEM(gradients.shape, gradients.dtype),
            *[pltpu.SMEM(s.shape, s.dtype) for s in (shift_x, shift_y, shift_z, fractions)],
            pltpu.SemaphoreType.DMA((2 * (TX // BX) + 5,)),
            vm(EX + 2 * EG, EY, LANES), vm(EX + 2 * EG, EY, LANES),
            vm(2, 2, HX + 2 * XG, EY, LANES), vm(EX, EY, LANES),
            vm(NB, 2, BX + 3, 3 * TILE, LANES), vm(NB, 2, 2 * WX - BX, 5 * TILE, LANES),
            *[vm(EX + 2 * EG, EY, LANES) for _ in range(4)],
            vm(TX, TY, LANES),
            vm(2, 2, EG, EY, LANES),
            vm(3, TX + 2 * LH, EY, LANES),
            vm(3, TX // 2, 2 * LH, LANES), vm(3, TX // 2, 2 * LH, LANES),
            vm(3, TX // 2, 2 * LH, LANES), vm(3, TX // 2, 2 * LH, LANES),
            vm(3, TX // VPK, TY, LANES), vm(3, TX // VPK, TY, LANES), vm(3, TX // VPK, TY, LANES),
            vm(most, TILE, LANES),
            pltpu.SemaphoreType.DMA((5,)), pltpu.SemaphoreType.DMA((13,)),
        ],
        compiler_params=pltpu.CompilerParams(collective_id=0, has_side_effects=True,
                                             vmem_limit_bytes=24 << 20),
    )(*(pltpu.with_memory_space_constraint(x, pltpu.HBM) for x in (velocity, gradients, shift_x, shift_y, shift_z, fractions)))


def solution(mesh):
    in_specs = (
        P(None, "gx", "gy", "gz"),
        P(None, None, "gx", "gy", "gz"),
        P(None, "gx", "gy", "gz"),
        P(None, "gx", "gy", "gz"),
        P(None, "gx", "gy", "gz"),
        P(None, None, "gx", "gy", "gz"),
    )
    out_specs = P(None, "gx", "gy", "gz")
    return jax.shard_map(functools.partial(body, dict(mesh.shape)), mesh=mesh, in_specs=in_specs,
                         out_specs=out_specs, check_vma=False)
```

```python
import functools

import jax
import jax.numpy as jnp
from jax import lax
from jax.experimental import pallas as pl
from jax.experimental.pallas import tpu as pltpu
from jax.sharding import PartitionSpec as P

BX = 8
BY = 8
BZ = 128
RX = 6
RY = 6
RZ = 14
STEPS = 2

STEP_SIZE = 0.5
REG_WEIGHT = 0.1
LAPLACE_TAPS = (-205.0 / 72.0, 8.0 / 5.0, -1.0 / 5.0, 8.0 / 315.0, -1.0 / 560.0)

HX = RX + 2
HY = RY + 2
HZ = RZ + 2
LANES = 128
PK = LANES // HZ
XG = HX // PK
LH = 4
VPK = LANES // (2 * LH)
WX = BX + 2 * HX
WY = BY + 2 * HY
TILE = 8
MESH = pl.DeviceIdType.MESH
AXES = ("gx", "gy", "gz")
WAYS = sorted(((i, j, k) for i in (-1, 0, 1) for j in (-1, 0, 1) for k in (-1, 0, 1) if (i, j, k) != (0, 0, 0)),
              key=lambda d: (not d[0], sum(map(abs, d))))


def piece(way, own, halo):
    return {-1: (0, halo), 0: (halo, halo + own), 1: (halo + own, 2 * halo + own)}[way]


def border(way, own, halo):
    return {-1: (halo, 2 * halo), 0: (halo, halo + own), 1: (own, halo + own)}[way]


def kernel(shape, vel_in, grad_in, shx_in, shy_in, shz_in, frac_in, out,
           vel, grad, shx, shy, shz, frac, arrive,
           E0, E1, LX, HA, RL, U, YP, XP, ACC0, ACC1, BK0, BK1, ADJ, SP,
           VE, YSU, YSD, YVD, YVU, SV, VRD, VRU, BULK, send, recv):
    TX, TY, TZ = vel.shape[1:]
    NBX, NBY = TX // BX, TY // BY
    EX = TX + 2 * HX
    EY = TY + 2 * HY
    EG = EX // PK
    G = TX // PK
    OX = slice(HX, HX + TX)
    OY = slice(HY, HY + TY)
    NT = TY // TILE

    at = {a: lax.axis_index(a) for a in AXES}

    def has(way):
        ok = None
        for a, w in zip(AXES, way):
            if w:
                one = at[a] < shape[a] - 1 if w > 0 else at[a] > 0
                ok = one if ok is None else jnp.logical_and(ok, one)
        return ok

    def device(way):
        return {a: at[a] + w for a, w in zip(AXES, way) if w}

    up = (at["gx"] == 0).astype(jnp.int32)

    NS = 2 if shape["gx"] > 2 else 1
    even = 1 - lax.rem(at["gy"], 2)
    off = jnp.where(even == 1, at["gy"] > 0, at["gy"] < shape["gy"] - 1)

    def place(h):
        return h if NS == 2 else 0

    def multiple(x):
        return pl.multiple_of(x, TILE)

    A = pl.ds(multiple(HY + even * (TY - HY)), HY)
    B = pl.ds(multiple(HY + (1 - even) * HY), TY - HY)
    OFF = pl.ds(multiple(HY + (1 - even) * (TY - HY)), HY)
    INNER = pl.ds(multiple(even * (HY + TY)), HY)
    OUTER = pl.ds(multiple((1 - even) * (HY + TY)), HY)

    def column(i):
        return i * up + (NBX - 1 - i) * (1 - up)

    def group_of(q):
        return q * up + (EG - 1 - q) * (1 - up)

    loads = []

    def load(src, dst):
        loads.append(pltpu.make_async_copy(src, dst, arrive.at[len(loads)]))
        loads[-1].start()
        return loads[-1]

    def part(ref, i):
        return ref.at[:, pl.ds(column(i) * BX, BX)]

    sources = [(load(part(vel_in, i), part(vel, i)), load(part(grad_in.at[0], i), part(grad.at[0], i)))
               for i in reversed(range(NBX))]
    later = [load(a, b) for a, b in ((shx_in, shx), (shy_in, shy), (shz_in, shz), (frac_in, frac),
                                     (grad_in.at[1], grad.at[1]))]

    barrier = pltpu.get_barrier_semaphore()
    total = jnp.int32(0)
    for way in WAYS:
        @pl.when(has(way))
        def _(way=way):
            pl.semaphore_signal(barrier, inc=1, device_id=device(way), device_id_type=MESH)
        total = total + has(way).astype(jnp.int32)

    def counts(a):
        if a == "off":
            return [(v, off if v else jnp.logical_not(off)) for v in range(2)] if shape["gy"] > 2 else [(0, None)]
        n = (at[a] > 0).astype(jnp.int32) + (at[a] < shape[a] - 1).astype(jnp.int32)
        return [(v, n == v if shape[a] > 2 else None) for v in ((0,), (1,), (1, 2))[min(shape[a], 3) - 1]]

    def wait_for(sem, tiles, axes, also=None):
        combos = [((), also)]
        for a in axes:
            combos = [(vs + (v,), c if ok is None else ok if c is None else jnp.logical_and(c, ok))
                      for vs, c in combos for v, ok in counts(a)]
        for vs, ok in combos:
            n = tiles(*vs)
            if not n:
                continue
            wait = pltpu.make_async_copy(BULK.at[0:n], BULK.at[0:n], sem).wait
            if ok is None:
                wait()
            else:
                pl.when(ok)(wait)

    def tiles_of(x, y, z):
        return x * y * z // (TILE * LANES)

    EACH = 1 + 2 * NS
    SIDES = [] if shape["gx"] == 1 else [(up, None)] if NS == 1 else [(0, has((-1, 0, 0))), (1, has((1, 0, 0)))]

    def wait_rest(n):
        wait_for(recv.at[EACH * n], lambda y, z: tiles_of(TX, TY + HY * y, LANES + HZ * z) - tiles_of(TX, TY, LANES),
                 ("gy", "gz"))

    def wait_early(n, h, ok):
        wait_for(recv.at[EACH * n + 1 + place(h)], lambda z: tiles_of(HX, HY, LANES) + tiles_of(HX, TY, HZ * z), ("gz",), ok)

    def wait_late(n, h, ok):
        wait_for(recv.at[EACH * n + 1 + NS + place(h)], lambda y, z: tiles_of(HX, TY - HY, LANES)
                 + tiles_of(HX + 2 * XG, HY, LANES) + y * tiles_of(HX, HY, LANES + HZ * z), ("off", "gz"), ok)

    def wait_back(n, h, ok):
        wait_for(recv.at[EACH * n + 1 + place(h)], lambda y, z: tiles_of(HX, TY + HY * y, LANES + HZ * z), ("off", "gz"), ok)

    def wait_pair(n, h, ok):
        wait_for(recv.at[EACH * n + 1 + NS + place(h)], lambda: tiles_of(HX + 2 * XG, HY, LANES), (), ok)

    def far_of(wait, n):
        if NS == 2:
            wait(n, 1, jnp.logical_and(SIDES[1][1], up == 0))

    def near_of(wait, n):
        for h, ok in SIDES:
            wait(n, h, jnp.logical_and(ok, up == 1) if NS == 2 and h else ok)

    def wait_sent(n):
        wait_for(send.at[n], lambda x, y, z: tiles_of(TX, TY + HY * (1 + y), LANES + HZ * z) - tiles_of(TX, TY, LANES)
                 + x * (tiles_of(HX, TY + HY * y, LANES + HZ * z) + tiles_of(HX + 2 * XG, HY, LANES)),
                 ("gx", "off", "gz"))

    def start(src, dst, way, sent, came):
        to_device(src, dst, device(way), has(way), sent, came)

    def to_device(src, dst, where, ok, sent, came):
        desc = pltpu.make_async_remote_copy(
            src_ref=src, dst_ref=dst, send_sem=send.at[sent], recv_sem=recv.at[came],
            device_id=where, device_id_type=MESH)
        if ok is None:
            desc.start()
        else:
            pl.when(ok)(desc.start)

    def both(*oks):
        oks = [ok for ok in oks if ok is not None]
        return functools.reduce(jnp.logical_and, oks) if oks else None

    def beside(h, y=0, z=0):
        where = {"gx": at["gx"] + 2 * h - 1}
        if y:
            where["gy"] = at["gy"] + (1 - 2 * even if y < 0 else 2 * even - 1)
        if z:
            where["gz"] = at["gz"] + z
        return where

    partner = {"gy": at["gy"] + 2 * even - 1}

    lane2 = lax.broadcasted_iota(jnp.int32, (1, LANES), 1)
    group = lane2 // HZ
    edge = jnp.logical_or(lane2 < HZ, lane2 >= LANES - HZ)

    def packed(layer):
        first = last = None
        for j in range(PK):
            turned = pltpu.roll(layer(j), HZ * j, 1) if j else layer(0)
            first = turned if j == 0 else jnp.where(group == j, turned, first)
            last = turned if j == 0 else jnp.where(group == j - 1, turned, last)
        return first, last

    def unpacked(first, last, j):
        both = jnp.where(group == j, first, last)
        return pltpu.roll(both, LANES - HZ * j, 1) if j else both

    def region(way, dim_of):
        (x0, x1) = dim_of(way[0], G if way[2] else TX, XG if way[2] else HX)
        (y0, y1) = dim_of(way[1], TY, HY)
        return slice(x0, x1), slice(y0, y1)

    def rim(ref, way):
        xs, ys = region(way, piece)
        base = {0: 0, -1: EX, 1: EX + EG}[way[2]]
        return ref.at[slice(base + xs.start, base + xs.stop), ys, :]

    def forward_x(E, k, n):
        for h, ok in SIDES:
            mine, g, into = pl.ds(HX + h * (TX - HX), HX), XG + h * (G - XG), LX.at[k, place(1 - h)]
            early, late = EACH * n + 1 + place(1 - h), EACH * n + 1 + NS + place(1 - h)
            to_device(E.at[mine, A, :], into.at[0:HX, A, :], beside(h), ok, n, early)
            for z in (-1, 1):
                to_device(SP.at[k, (z + 1) // 2, g, OY, :], into.at[HX + (1 - z) // 2, OY, :],
                          beside(h, 0, z), both(ok, has((0, 0, z))), n, early)
            to_device(E.at[mine, OFF, :], into.at[0:HX, INNER, :], beside(h, -1), both(ok, off), n, late)
            for z in (-1, 1):
                to_device(SP.at[k, (z + 1) // 2, g, OFF, :], into.at[HX + (1 - z) // 2, INNER, :],
                          beside(h, -1, z), both(ok, off, has((0, 0, z))), n, late)
            to_device(E.at[mine, B, :], into.at[0:HX, B, :], beside(h), ok, n, late)

    def forward_pair(k, n):
        for h, ok in SIDES:
            wait_early(n, h, ok)
            to_device(LX.at[k, place(h), :, A, :], LX.at[k, place(h), :, OUTER, :], partner, ok, n,
                      EACH * n + 1 + NS + place(h))

    def forward_rest(E, k, n):
        for way in REST:
            xs, ys = region(way, border)
            src = SP.at[k, 0 if way[2] < 0 else 1, xs, ys, :] if way[2] else E.at[xs, ys, :]
            start(src, rim(E, tuple(-w for w in way)), way, n, EACH * n)

    def return_x(k, BK, n, part):
        for h, ok in SIDES:
            mine, came = HA.at[k, place(h)], EACH * n + 1 + place(1 - h)
            first = (1 - h) * (HX + TX)
            g = (1 - h) * (EG - 1)

            def send_rows(rows, into, y, ok):
                to_device(mine.at[0:HX, rows, :], BK.at[pl.ds(first, HX), into, :], beside(h, y), ok, n, came)
                for z in (-1, 1):
                    to_device(mine.at[HX + (z + 1) // 2, rows, :], BK.at[EX + EG * ((1 - z) // 2) + g, into, :],
                              beside(h, y, z), both(ok, has((0, 0, z))), n, came)

            if part == 0:
                to_device(mine.at[:, INNER, :], RL.at[k, place(h)], partner, ok, n, EACH * n + 1 + NS + place(h))
                send_rows(OUTER, INNER, -1, both(ok, off))
                send_rows(B, B, 0, ok)
            else:
                wait_pair(n, h, ok)
                for L in range(HX + 2 * XG):
                    HA[k, place(h), L, A, :] = HA[k, place(h), L, A, :] + RL[k, place(h), L]
                send_rows(A, A, 0, ok)

    def return_rest(ACC, BK, n):
        for way in REST:
            start(rim(ACC, way), rim(BK, tuple(-w for w in way)), way, n, EACH * n)

    REST = [w for w in WAYS if not w[0]]

    def pack_column(E, k, bx):
        SP[k, 0, XG + bx, OY, :], SP[k, 1, XG + bx, OY, :] = packed(lambda j: E[HX + bx * BX + j, OY, :])

    def unpack(below, above, g):
        for j in range(PK):
            U[PK * g + j] = unpacked(above, below, j)

    def taps(k, d, bx, by):
        e = frac[k, bx, by, 0, d].astype(jnp.float32) * 0.125
        e2 = e * e
        e3 = e2 * e
        return (0.5 * (2.0 * e2 - e3 - e), 0.5 * (3.0 * e3 - 5.0 * e2 + 2.0),
                0.5 * (4.0 * e2 - 3.0 * e3 + e), 0.5 * (e3 - e2))

    def total_of(terms):
        return functools.reduce(lambda a, b: a + b, terms)

    def gather_block(E, k, bx, by):
        a, b, c = shx[k, bx, 0, by], shy[k, bx, 0, by], shz[k, bx, 0, by]
        wx, wy, wz = (taps(k, d, bx, by) for d in range(3))
        x0 = bx * BX + (a + HX - 1)
        y0 = by * BY + (b + HY - 1)
        along = []
        for ref in (E, U):
            rows = [total_of(wy[v] * ref[x0 + m, pl.ds(y0 + v, BY), :] for v in range(4)) for m in range(BX + 3)]
            along.append([total_of(wx[u] * rows[m + u] for u in range(4)) for m in range(BX)])
        own, rest = (jnp.concatenate(p, axis=0) for p in along)
        res = None
        for w in range(4):
            s = c + (w - 1)
            inside = jnp.logical_and(lane2 >= s, lane2 < LANES + s)
            term = wz[w] * pltpu.roll(jnp.where(inside, own, rest), lax.rem(LANES - s, LANES), 1)
            res = term if res is None else res + term
        return [res[BY * m:BY * (m + 1)] for m in range(BX)]

    def spread_block(vals, k, i, bx, by):
        n = i * NBY + by
        c = shz[k, bx, 0, by]
        wx, wy, wz = (taps(k, d, bx, by) for d in range(3))
        flat = jnp.concatenate(vals, axis=0)
        own = rest = None
        for w in range(4):
            s = c + (w - 1)
            inside = jnp.logical_and(lane2 >= s, lane2 < LANES + s)
            term = wz[w] * pltpu.roll(flat, lax.rem(LANES + s, LANES), 1)
            o, r = jnp.where(inside, term, 0.0), jnp.where(inside, 0.0, term)
            own, rest = (o, r) if own is None else (own + o, rest + r)
        for p, zs in enumerate((own, rest)):
            z = [zs[BY * m:BY * (m + 1)] for m in range(BX)]
            for m in range(BX + 3):
                YP[n, p, m, TILE:TILE + BY, :] = total_of(wx[u] * z[m - u] for u in range(4) if 0 <= m - u < BX)
            for m in range(BX + 3):
                XP[n, p, 2 * HX + m, 2 * TILE:2 * TILE + 2 * BY, :] = total_of(
                    wy[v] * YP[n, p, m, TILE - v:TILE - v + 2 * BY, :] for v in range(4))

    def collect(k, q, ACC=None, halo=None):
        g = group_of(q)
        found = []
        for i in range(NBX):
            if 0 <= q - i <= 2:
                bx = column(i)
                offset = BX * ((q - i) * up + (2 - q + i) * (1 - up))
                for by in range(NBY):
                    found.append((i * NBY + by, by, (HX + 1) - shx[k, bx, 0, by] + offset,
                                  (2 * TILE - HY + 1) - shy[k, bx, 0, by]))

        def layer(p, j):
            tiles = [None] * (EY // TILE)
            for n, by, x0, y0 in found:
                rows = XP[n, p, x0 + j, pl.ds(y0, WY), :]
                for r in range(WY // TILE):
                    one = rows[r * TILE:(r + 1) * TILE]
                    old = tiles[by + r]
                    tiles[by + r] = one if old is None else old + one
            return jnp.concatenate(tiles, axis=0)

        rims = [layer(1, j) for j in range(PK)]
        above, below = packed(lambda j: rims[j])
        for j in range(PK):
            if halo is not None:
                HA[k, halo, j] = layer(0, j)
            else:
                ACC[PK * g + j] = layer(0, j)
        if halo is not None:
            HA[k, halo, HX], HA[k, halo, HX + XG] = below, above
        else:
            ACC[EX + EG + g], ACC[EX + g] = above, below

    def received(ACC, BK, i):
        bx = column(i)
        halos = ([0] if i == 0 and NS == 2 else []) + ([EG - 1] if i == NBX - 1 else [])
        halos = [group_of(q) for q in halos]

        def rows(center, L):
            tiles = [center[L, HY + TILE * t:HY + TILE * (t + 1), :] for t in range(NT)]
            tiles[0] = tiles[0] + BK[L, 0:HY, :]
            tiles[-1] = tiles[-1] + BK[L, HY + TY:, :]
            return jnp.concatenate(tiles, axis=0)

        rims = []
        for base in (EX, EX + EG):
            rims.append(total_of([rows(BK, base + XG + bx)] + [rows(BK, base + g) for g in halos]))
        first, last = rims
        res = []
        for j in range(BX):
            one = total_of([rows(ACC, HX + bx * BX + j)] + [rows(BK, PK * g + j) for g in halos])
            res.append(one + jnp.where(edge, unpacked(first, last, j), 0.0))
        return res

    def blocks(layers, by):
        return [one[by * BY:(by + 1) * BY] for one in layers]

    def product(k, bx, j):
        return STEP_SIZE * total_of(grad[k, c, bx * BX + j].astype(jnp.float32) * vel[c, bx * BX + j] for c in range(3))

    def clear(a, first, last):
        for end, views in ((0, first), (shape[a] - 1, last)):
            @pl.when(at[a] == end)
            def _(views=views):
                for ref in views:
                    ref[...] = jnp.zeros_like(ref)

    def clear_missing():
        sides = ((slice(0, HX), slice(EX, EX + XG), slice(EX + EG, EX + EG + XG)),
                 (slice(HX + TX, EX), slice(EX + XG + G, EX + EG), slice(EX + EG + XG + G, EX + 2 * EG)))
        low, high = ([BK.at[x] for BK in (BK0, BK1) for x in side] for side in sides)
        if NS == 2:
            low, high = low + [LX.at[:, 0]], high + [LX.at[:, 1]]
        clear("gx", low + [E.at[x] for E in (E0, E1) for x in sides[0]] + [VE.at[:, 0:LH]],
              high + [E.at[x] for E in (E0, E1) for x in sides[1]] + [VE.at[:, LH + TX:]])
        for BK in (BK0, BK1):
            for x in sides[0] + sides[1]:
                BK[x, INNER, :] = jnp.zeros_like(BK[x, INNER, :])
        ends = slice(0, HY), slice(HY + TY, EY)
        low, high = ([ref.at[:, y] for ref in (E0, E1, BK0, BK1)] + [LX.at[:, :, :, y]] for y in ends)
        clear("gy", low + [YVD], high + [YVU])
        low, high = ([ref.at[x] for ref in (E0, E1, BK0, BK1)] for x in (slice(EX, EX + EG), slice(EX + EG, EX + 2 * EG)))
        clear("gz", low + [LX.at[:, :, HX, y] for y in (OY, OUTER)] + [VRD],
              high + [LX.at[:, :, HX + XG, y] for y in (OY, OUTER)] + [VRU])

    def send_faces():
        n = 4
        copies = [((1, 0, 0), vel.at[:, TX - LH:TX], VE.at[:, 0:LH, OY, :]),
                  ((-1, 0, 0), vel.at[:, 0:LH], VE.at[:, LH + TX:2 * LH + TX, OY, :])]
        for way, src, dst in copies:
            start(src, dst, way, n, EACH * n)
        VE[:, LH:LH + TX, OY, :] = vel[...]
        for c in range(3):
            for i in range(TX // 2):
                for h in range(2):
                    YSU[c, i, LH * h:LH * (h + 1), :] = vel[c, 2 * i + h, TY - LH:TY, :]
                    YSD[c, i, LH * h:LH * (h + 1), :] = vel[c, 2 * i + h, 0:LH, :]
            for g in range(TX // VPK):
                row = None
                for j in range(VPK):
                    turned = pltpu.roll(vel[c, VPK * g + j], (2 * LH * j + LH) % LANES, 1)
                    row = turned if row is None else jnp.where(lane2 // (2 * LH) == j, turned, row)
                SV[c, g] = row
        for way, src, dst in (((0, 1, 0), YSU, YVD), ((0, -1, 0), YSD, YVU),
                              ((0, 0, 1), SV, VRD), ((0, 0, -1), SV, VRU)):
            start(src, dst, way, n, EACH * n)

    def face_tiles(x, y, z):
        return (x * tiles_of(3 * LH, TY, LANES) + y * tiles_of(3 * TX // 2, 2 * LH, LANES)
                + z * tiles_of(3 * TX // VPK, TY, LANES))

    def regular():
        wait_for(recv.at[4 * EACH], face_tiles, AXES)
        for c in range(3):
            for i in range(TX // 2):
                for h in range(2):
                    VE[c, LH + 2 * i + h, HY - LH:HY, :] = YVD[c, i, LH * h:LH * (h + 1), :]
                    VE[c, LH + 2 * i + h, HY + TY:HY + TY + LH, :] = YVU[c, i, LH * h:LH * (h + 1), :]
        rows = lax.broadcasted_iota(jnp.int32, (2 * LANES, LANES), 0)
        cols = lax.broadcasted_iota(jnp.int32, (2 * LANES, LANES), 1)
        r = rows - LANES
        place = jnp.where(rows < LANES, rows, jnp.where(r < LH, r + LANES, r - LANES))
        known = jnp.logical_or(rows < LANES, jnp.logical_or(r < LH, r >= LANES - LH))
        gap = jnp.abs(place - cols)
        band = jnp.zeros((2 * LANES, LANES), jnp.float32)
        for k in range(5):
            tap = (3.0 if k == 0 else 1.0) * LAPLACE_TAPS[k]
            band = jnp.where(jnp.logical_and(known, gap == k), tap, band)
        for c in range(3):
            rims = []
            for g in range(TX // VPK):
                row = jnp.where(lane2 % (2 * LH) < LH, VRD[c, g], VRU[c, g])
                for j in range(VPK):
                    rims.append(pltpu.roll(row, (LANES - (2 * LH * j + LH)) % LANES, 1))
            rims = jnp.concatenate(rims, axis=0)
            own = vel[c].reshape(TX * TY, LANES)
            res = jnp.dot(jnp.concatenate([own, rims], axis=1), band,
                          preferred_element_type=jnp.float32,
                          precision=lax.Precision.HIGHEST).reshape(TX, TY, LANES)
            for k in range(1, 5):
                res = res + LAPLACE_TAPS[k] * (
                    VE[c, LH + k:LH + k + TX, OY, :] + VE[c, LH - k:LH - k + TX, OY, :]
                    + VE[c, LH:LH + TX, HY + k:HY + k + TY, :]
                    + VE[c, LH:LH + TX, HY - k:HY - k + TY, :])
            out[c] = (-REG_WEIGHT) * res

    met = False
    for i in reversed(range(NBX)):
        for copy in sources[NBX - 1 - i]:
            copy.wait()
        bx = column(i)
        for j in range(BX):
            E0[HX + bx * BX + j, OY, :] = product(0, bx, j)
        pack_column(E0, 0, bx)
        if not met and (i == NBX - 1 and NS == 1 or i == 0):
            pl.semaphore_wait(barrier, total)
            forward_x(E0, 0, 0)
            met = True
    forward_rest(E0, 0, 0)

    clear_missing()
    send_faces()
    for copy in later:
        copy.wait()
    for i in range(NBX):
        for j in range(BX):
            E1[HX + column(i) * BX + j, OY, :] = product(1, column(i), j)
    YP[:, :, :, 0:TILE] = jnp.zeros_like(YP[:, :, :, 0:TILE])
    YP[:, :, :, TILE + BY:] = jnp.zeros_like(YP[:, :, :, TILE + BY:])
    XP[...] = jnp.zeros_like(XP)

    def enter(E, k, g, side):
        for j in range(HX):
            E[PK * g + j] = LX[k, side, j]
        unpack(LX[k, side, HX], LX[k, side, HX + XG], g)

    def forward(E, n, each):
        forward_pair(n, n)
        wait_rest(n)
        for i in range(NBX):
            g = XG + column(i)
            unpack(E[EX + g], E[EX + EG + g], g)
        for i in range(NBX):
            if i == 0:
                g = group_of(0)
                if NS == 2:
                    far_of(wait_late, n)
                    enter(E, n, g, 1 - up)
                else:
                    unpack(E[EX + g], E[EX + EG + g], g)
            if i == NBX - 1:
                near_of(wait_late, n)
                enter(E, n, group_of(EG - 1), place(up))
            each(i, column(i))

    def first(i, bx):
        for by in range(NBY):
            res = gather_block(E0, 0, bx, by)
            for m in range(BX):
                rows = slice(HY + by * BY, HY + (by + 1) * BY)
                E1[HX + bx * BX + m, rows, :] = E1[HX + bx * BX + m, rows, :] + res[m]
        pack_column(E1, 1, bx)

    forward(E0, 0, first)
    forward_x(E1, 1, 1)
    forward_rest(E1, 1, 1)

    def second(i, bx):
        for by in range(NBY):
            spread_block(gather_block(E1, 1, bx, by), 1, i, bx, by)

    forward(E1, 1, second)

    def give_back(ACC, BK, k, n, meanwhile):
        collect(k, EG - 1, halo=place(up))
        if NS == 2:
            collect(k, 0, halo=1 - up)
        return_x(k, BK, n, 0)
        for q in range(XG, XG + G):
            collect(k, q, ACC)
        return_rest(ACC, BK, n)
        meanwhile()
        return_x(k, BK, n, 1)

    def backward(ACC, BK, n, each):
        wait_rest(n)
        for i in range(NBX):
            if i == 0:
                far_of(wait_back, n)
            if i == NBX - 1:
                near_of(wait_back, n)
            each(i, column(i), received(ACC, BK, i))

    give_back(ACC1, BK1, 1, 2, regular)

    def third(i, bx, layers):
        for j in range(BX):
            ADJ[bx * BX + j] = layers[j]
        for by in range(NBY):
            spread_block(blocks(layers, by), 0, i, bx, by)

    backward(ACC1, BK1, 2, third)
    def gauss():
        for c in range(3):
            out[c] = out[c] + STEP_SIZE * grad[1, c].astype(jnp.float32) * ADJ[...]
        for n in range(3):
            wait_sent(n)
        wait_for(send.at[4], face_tiles, AXES)

    give_back(ACC0, BK0, 0, 3, gauss)

    def fourth(i, bx, layers):
        for c in range(3):
            for j in range(BX):
                x = bx * BX + j
                out[c, x] = out[c, x] + STEP_SIZE * grad[0, c, x].astype(jnp.float32) * layers[j]

    backward(ACC0, BK0, 3, fourth)
    wait_sent(3)


def body(shape, velocity, gradients, shift_x, shift_y, shift_z, fractions):
    TX, TY, TZ = velocity.shape[1:]
    assert TZ == BZ == LANES and TX % VPK == 0 and TX % BX == 0 and TY % BY == 0
    assert shape["gy"] % 2 == 0 and TX // BX > 1
    assert BX == HX == PK and BY == HY == TILE and XG == 1
    EX, EY = TX + 2 * HX, TY + 2 * HY
    EG = EX // PK
    NS = 2 if shape["gx"] > 2 else 1
    NB = (TX // BX) * (TY // BY)
    most = EX * EY * (LANES + 2 * HZ) // (TILE * LANES)

    vm = lambda *s: pltpu.VMEM(s, jnp.float32)
    vmem = pl.BlockSpec(memory_space=pltpu.VMEM)
    hbm = pl.BlockSpec(memory_space=pltpu.HBM)
    shift_x, shift_y, shift_z = (s.transpose(0, 1, 3, 2) for s in (shift_x, shift_y, shift_z))
    fractions = fractions.transpose(0, 2, 3, 4, 1)
    return pl.pallas_call(
        functools.partial(kernel, shape),
        out_shape=jax.ShapeDtypeStruct(velocity.shape, jnp.float32),
        in_specs=[hbm] * 6,
        out_specs=vmem,
        scratch_shapes=[
            pltpu.VMEM(velocity.shape, velocity.dtype), pltpu.VMEM(gradients.shape, gradients.dtype),
            *[pltpu.SMEM(s.shape, s.dtype) for s in (shift_x, shift_y, shift_z, fractions)],
            pltpu.SemaphoreType.DMA((2 * (TX // BX) + 5,)),
            vm(EX + 2 * EG, EY, LANES), vm(EX + 2 * EG, EY, LANES),
            vm(2, NS, HX + 2 * XG, EY, LANES), vm(2, NS, HX + 2 * XG, EY, LANES),
            vm(2, NS, HX + 2 * XG, HY, LANES), vm(EX, EY, LANES),
            vm(NB, 2, BX + 3, 3 * TILE, LANES), vm(NB, 2, 2 * WX - BX, 5 * TILE, LANES),
            *[vm(EX + 2 * EG, EY, LANES) for _ in range(4)],
            vm(TX, TY, LANES),
            vm(2, 2, EG, EY, LANES),
            vm(3, TX + 2 * LH, EY, LANES),
            vm(3, TX // 2, 2 * LH, LANES), vm(3, TX // 2, 2 * LH, LANES),
            vm(3, TX // 2, 2 * LH, LANES), vm(3, TX // 2, 2 * LH, LANES),
            vm(3, TX // VPK, TY, LANES), vm(3, TX // VPK, TY, LANES), vm(3, TX // VPK, TY, LANES),
            vm(most, TILE, LANES),
            pltpu.SemaphoreType.DMA((5,)), pltpu.SemaphoreType.DMA((4 * (1 + 2 * NS) + 1,)),
        ],
        compiler_params=pltpu.CompilerParams(collective_id=0, has_side_effects=True,
                                             vmem_limit_bytes=24 << 20),
    )(*(pltpu.with_memory_space_constraint(x, pltpu.HBM) for x in (velocity, gradients, shift_x, shift_y, shift_z, fractions)))


def solution(mesh):
    in_specs = (
        P(None, "gx", "gy", "gz"),
        P(None, None, "gx", "gy", "gz"),
        P(None, "gx", "gy", "gz"),
        P(None, "gx", "gy", "gz"),
        P(None, "gx", "gy", "gz"),
        P(None, None, "gx", "gy", "gz"),
    )
    out_specs = P(None, "gx", "gy", "gz")
    return jax.shard_map(functools.partial(body, dict(mesh.shape)), mesh=mesh, in_specs=in_specs,
                         out_specs=out_specs, check_vma=False)
```

```python
import functools

import jax
import jax.numpy as jnp
from jax import lax
from jax.experimental import pallas as pl
from jax.experimental.pallas import tpu as pltpu
from jax.sharding import PartitionSpec as P

BX = 8
BY = 8
BZ = 128
RX = 6
RY = 6
RZ = 14
STEPS = 2

STEP_SIZE = 0.5
REG_WEIGHT = 0.1
LAPLACE_TAPS = (-205.0 / 72.0, 8.0 / 5.0, -1.0 / 5.0, 8.0 / 315.0, -1.0 / 560.0)

HX = RX + 2
HY = RY + 2
HZ = RZ + 2
LANES = 128
PK = LANES // HZ
XG = HX // PK
LH = 4
VPK = LANES // (2 * LH)
WX = BX + 2 * HX
WY = BY + 2 * HY
TILE = 8
MESH = pl.DeviceIdType.MESH
AXES = ("gx", "gy", "gz")
WAYS = sorted(((i, j, k) for i in (-1, 0, 1) for j in (-1, 0, 1) for k in (-1, 0, 1) if (i, j, k) != (0, 0, 0)),
              key=lambda d: (not d[0], sum(map(abs, d))))


def piece(way, own, halo):
    return {-1: (0, halo), 0: (halo, halo + own), 1: (halo + own, 2 * halo + own)}[way]


def border(way, own, halo):
    return {-1: (halo, 2 * halo), 0: (halo, halo + own), 1: (own, halo + own)}[way]


def kernel(shape, vel_in, grad_in, shx_in, shy_in, shz_in, frac_in, out,
           vel, grad, shx, shy, shz, frac, arrive,
           E0, E1, LX, HA, RL, U, YP, XP, ACC0, ACC1, BK0, BK1, ADJ, SP,
           VE, YSU, YSD, YVD, YVU, SV, VRD, VRU, BULK, send, recv):
    TX, TY, TZ = vel.shape[1:]
    NBX, NBY = TX // BX, TY // BY
    EX = TX + 2 * HX
    EY = TY + 2 * HY
    EG = EX // PK
    G = TX // PK
    OX = slice(HX, HX + TX)
    OY = slice(HY, HY + TY)
    NT = TY // TILE

    at = {a: lax.axis_index(a) for a in AXES}

    def has(way):
        ok = None
        for a, w in zip(AXES, way):
            if w:
                one = at[a] < shape[a] - 1 if w > 0 else at[a] > 0
                ok = one if ok is None else jnp.logical_and(ok, one)
        return ok

    def device(way):
        return {a: at[a] + w for a, w in zip(AXES, way) if w}

    up = (at["gx"] == 0).astype(jnp.int32)

    NS = 2 if shape["gx"] > 2 else 1
    even = 1 - lax.rem(at["gy"], 2)
    off = jnp.where(even == 1, at["gy"] > 0, at["gy"] < shape["gy"] - 1)

    def place(h):
        return h if NS == 2 else 0

    def multiple(x):
        return pl.multiple_of(x, TILE)

    A = pl.ds(multiple(HY + even * (TY - HY)), HY)
    B = pl.ds(multiple(HY + (1 - even) * HY), TY - HY)
    OFF = pl.ds(multiple(HY + (1 - even) * (TY - HY)), HY)
    INNER = pl.ds(multiple(even * (HY + TY)), HY)
    OUTER = pl.ds(multiple((1 - even) * (HY + TY)), HY)

    def column(i):
        return i * up + (NBX - 1 - i) * (1 - up)

    def group_of(q):
        return q * up + (EG - 1 - q) * (1 - up)

    def block(j):
        return (NBY - 1 - j) * even + j * (1 - even)

    def rows_of(t):
        return pl.ds(multiple(TILE * ((NT + 1 - t) * even + t * (1 - even))), TILE)

    loads = []

    def load(src, dst):
        loads.append(pltpu.make_async_copy(src, dst, arrive.at[len(loads)]))
        loads[-1].start()
        return loads[-1]

    def part(ref, i):
        return ref.at[:, pl.ds(column(i) * BX, BX)]

    sources = [(load(part(vel_in, i), part(vel, i)), load(part(grad_in.at[0], i), part(grad.at[0], i)))
               for i in reversed(range(NBX))]
    later = [load(a, b) for a, b in ((shx_in, shx), (shy_in, shy), (shz_in, shz), (frac_in, frac),
                                     (grad_in.at[1], grad.at[1]))]

    barrier = pltpu.get_barrier_semaphore()
    total = jnp.int32(0)
    for way in WAYS:
        @pl.when(has(way))
        def _(way=way):
            pl.semaphore_signal(barrier, inc=1, device_id=device(way), device_id_type=MESH)
        total = total + has(way).astype(jnp.int32)

    def counts(a):
        if a == "off":
            return [(v, off if v else jnp.logical_not(off)) for v in range(2)] if shape["gy"] > 2 else [(0, None)]
        n = (at[a] > 0).astype(jnp.int32) + (at[a] < shape[a] - 1).astype(jnp.int32)
        return [(v, n == v if shape[a] > 2 else None) for v in ((0,), (1,), (1, 2))[min(shape[a], 3) - 1]]

    def wait_for(sem, tiles, axes, also=None):
        combos = [((), also)]
        for a in axes:
            combos = [(vs + (v,), c if ok is None else ok if c is None else jnp.logical_and(c, ok))
                      for vs, c in combos for v, ok in counts(a)]
        for vs, ok in combos:
            n = tiles(*vs)
            if not n:
                continue
            wait = pltpu.make_async_copy(BULK.at[0:n], BULK.at[0:n], sem).wait
            if ok is None:
                wait()
            else:
                pl.when(ok)(wait)

    def tiles_of(x, y, z):
        return x * y * z // (TILE * LANES)

    EACH = 1 + 3 * NS
    SIDES = [] if shape["gx"] == 1 else [(up, None)] if NS == 1 else [(0, has((-1, 0, 0))), (1, has((1, 0, 0)))]

    def sem(n, kind=None, h=0):
        return EACH * (n % 2) + (0 if kind is None else 1 + kind * NS + place(h))

    def wait_rest(n):
        wait_for(recv.at[sem(n)], lambda y, z: tiles_of(TX, TY + HY * y, LANES + HZ * z) - tiles_of(TX, TY, LANES),
                 ("gy", "gz"))

    def wait_early(n, h, ok):
        wait_for(recv.at[sem(n, 0, h)], lambda z: tiles_of(HX, HY, LANES + HZ * z), ("gz",), ok)

    def wait_late(n, h, ok):
        wait_for(recv.at[sem(n, 1, h)], lambda z: tiles_of(HX, TY - HY, LANES + HZ * z) + tiles_of(HX + 2 * XG, HY, LANES),
                 ("gz",), ok)

    def wait_off(n, h, ok):
        wait_for(recv.at[sem(n, 2, h)], lambda y, z: y * tiles_of(HX, HY, LANES + HZ * z), ("off", "gz"), ok)

    def wait_back(n, h, ok):
        wait_for(recv.at[sem(n, 0, h)], lambda y, z: tiles_of(HX, TY - HY + HY * y, LANES + HZ * z), ("off", "gz"), ok)

    def wait_last(n, h, ok):
        wait_for(recv.at[sem(n, 1, h)], lambda z: tiles_of(HX, HY, LANES + HZ * z), ("gz",), ok)

    def wait_pair(n, h, ok):
        wait_for(recv.at[sem(n, 2, h)], lambda: tiles_of(HX + 2 * XG, HY, LANES), (), ok)

    def far_of(wait, n):
        if NS == 2:
            wait(n, 1, jnp.logical_and(SIDES[1][1], up == 0))

    def near_of(wait, n):
        for h, ok in SIDES:
            wait(n, h, jnp.logical_and(ok, up == 1) if NS == 2 and h else ok)

    def wait_sent(n):
        wait_for(send.at[n], lambda x, y, z: tiles_of(TX, TY + HY * (1 + y), LANES + HZ * z) - tiles_of(TX, TY, LANES)
                 + x * (tiles_of(HX, TY + HY * y, LANES + HZ * z) + tiles_of(HX + 2 * XG, HY, LANES)),
                 ("gx", "off", "gz"))

    def start(src, dst, way, sent, came):
        to_device(src, dst, device(way), has(way), sent, came)

    def to_device(src, dst, where, ok, sent, came):
        desc = pltpu.make_async_remote_copy(
            src_ref=src, dst_ref=dst, send_sem=send.at[sent], recv_sem=recv.at[came],
            device_id=where, device_id_type=MESH)
        if ok is None:
            desc.start()
        else:
            pl.when(ok)(desc.start)

    def both(*oks):
        oks = [ok for ok in oks if ok is not None]
        return functools.reduce(jnp.logical_and, oks) if oks else None

    def beside(h, y=0, z=0):
        where = {"gx": at["gx"] + 2 * h - 1}
        if y:
            where["gy"] = at["gy"] + (1 - 2 * even if y < 0 else 2 * even - 1)
        if z:
            where["gz"] = at["gz"] + z
        return where

    partner = {"gy": at["gy"] + 2 * even - 1}

    lane2 = lax.broadcasted_iota(jnp.int32, (1, LANES), 1)
    group = lane2 // HZ
    edge = jnp.logical_or(lane2 < HZ, lane2 >= LANES - HZ)

    def packed(layer):
        first = last = None
        for j in range(PK):
            turned = pltpu.roll(layer(j), HZ * j, 1) if j else layer(0)
            first = turned if j == 0 else jnp.where(group == j, turned, first)
            last = turned if j == 0 else jnp.where(group == j - 1, turned, last)
        return first, last

    def unpacked(first, last, j):
        both = jnp.where(group == j, first, last)
        return pltpu.roll(both, LANES - HZ * j, 1) if j else both

    def region(way, dim_of):
        (x0, x1) = dim_of(way[0], G if way[2] else TX, XG if way[2] else HX)
        (y0, y1) = dim_of(way[1], TY, HY)
        return slice(x0, x1), slice(y0, y1)

    def rim(ref, way):
        xs, ys = region(way, piece)
        base = {0: 0, -1: EX, 1: EX + EG}[way[2]]
        return ref.at[slice(base + xs.start, base + xs.stop), ys, :]

    def forward_x(E, k, n, part):
        for h, ok in SIDES:
            mine, g, into = pl.ds(HX + h * (TX - HX), HX), XG + h * (G - XG), LX.at[k, place(1 - h)]

            def send_rows(rows, where, y, ok, came):
                to_device(E.at[mine, rows, :], into.at[0:HX, where, :], beside(h, y), ok, n, came)
                for z in (-1, 1):
                    to_device(SP.at[k, (z + 1) // 2, g, rows, :], into.at[HX + (1 - z) // 2, where, :],
                              beside(h, y, z), both(ok, has((0, 0, z))), n, came)

            if part == 0:
                send_rows(A, A, 0, ok, sem(n, 0, 1 - h))
            else:
                send_rows(OFF, INNER, -1, both(ok, off), sem(n, 2, 1 - h))
                send_rows(B, B, 0, ok, sem(n, 1, 1 - h))

    def forward_pair(k, n):
        for h, ok in SIDES:
            wait_early(n, h, ok)
            to_device(LX.at[k, place(h), :, A, :], LX.at[k, place(h), :, OUTER, :], partner, ok, n, sem(n, 1, h))

    def forward_rest(E, k, n):
        for way in REST:
            xs, ys = region(way, border)
            src = SP.at[k, 0 if way[2] < 0 else 1, xs, ys, :] if way[2] else E.at[xs, ys, :]
            start(src, rim(E, tuple(-w for w in way)), way, n, sem(n))

    def return_x(k, BK, n, part):
        for h, ok in SIDES:
            mine = HA.at[k, place(h)]
            first = (1 - h) * (HX + TX)
            g = (1 - h) * (EG - 1)

            def send_rows(rows, into, y, ok, came):
                to_device(mine.at[0:HX, rows, :], BK.at[pl.ds(first, HX), into, :], beside(h, y), ok, n, came)
                for z in (-1, 1):
                    to_device(mine.at[HX + (z + 1) // 2, rows, :], BK.at[EX + EG * ((1 - z) // 2) + g, into, :],
                              beside(h, y, z), both(ok, has((0, 0, z))), n, came)

            if part == "pair":
                to_device(mine.at[:, INNER, :], RL.at[k, place(h)], partner, ok, n, sem(n, 2, h))
            elif part == "off":
                send_rows(OUTER, INNER, -1, both(ok, off), sem(n, 0, 1 - h))
            elif part == "own":
                send_rows(B, B, 0, ok, sem(n, 0, 1 - h))
            else:
                wait_pair(n, h, ok)
                for L in range(HX + 2 * XG):
                    HA[k, place(h), L, A, :] = HA[k, place(h), L, A, :] + RL[k, place(h), L]
                send_rows(A, A, 0, ok, sem(n, 1, 1 - h))

    def return_rest(ACC, BK, n):
        for way in REST:
            start(rim(ACC, way), rim(BK, tuple(-w for w in way)), way, n, sem(n))

    REST = [w for w in WAYS if not w[0]]

    def pack(E, k, bx, rows):
        SP[k, 0, XG + bx, rows, :], SP[k, 1, XG + bx, rows, :] = packed(lambda j: E[HX + bx * BX + j, rows, :])

    def unpack(below, above, g, rows=slice(None)):
        for j in range(PK):
            U[PK * g + j, rows, :] = unpacked(above, below, j)

    def taps(k, d, bx, by):
        e = frac[k, bx, by, 0, d].astype(jnp.float32) * 0.125
        e2 = e * e
        e3 = e2 * e
        return (0.5 * (2.0 * e2 - e3 - e), 0.5 * (3.0 * e3 - 5.0 * e2 + 2.0),
                0.5 * (4.0 * e2 - 3.0 * e3 + e), 0.5 * (e3 - e2))

    def total_of(terms):
        return functools.reduce(lambda a, b: a + b, terms)

    def gather_block(E, k, bx, by):
        a, b, c = shx[k, bx, 0, by], shy[k, bx, 0, by], shz[k, bx, 0, by]
        wx, wy, wz = (taps(k, d, bx, by) for d in range(3))
        x0 = bx * BX + (a + HX - 1)
        y0 = by * BY + (b + HY - 1)
        along = []
        for ref in (E, U):
            rows = [total_of(wy[v] * ref[x0 + m, pl.ds(y0 + v, BY), :] for v in range(4)) for m in range(BX + 3)]
            along.append([total_of(wx[u] * rows[m + u] for u in range(4)) for m in range(BX)])
        own, rest = (jnp.concatenate(p, axis=0) for p in along)
        res = None
        for w in range(4):
            s = c + (w - 1)
            inside = jnp.logical_and(lane2 >= s, lane2 < LANES + s)
            term = wz[w] * pltpu.roll(jnp.where(inside, own, rest), lax.rem(LANES - s, LANES), 1)
            res = term if res is None else res + term
        return [res[BY * m:BY * (m + 1)] for m in range(BX)]

    def spread_block(vals, k, n, bx, by):
        c = shz[k, bx, 0, by]
        wx, wy, wz = (taps(k, d, bx, by) for d in range(3))
        flat = jnp.concatenate(vals, axis=0)
        own = rest = None
        for w in range(4):
            s = c + (w - 1)
            inside = jnp.logical_and(lane2 >= s, lane2 < LANES + s)
            term = wz[w] * pltpu.roll(flat, lax.rem(LANES + s, LANES), 1)
            o, r = jnp.where(inside, term, 0.0), jnp.where(inside, 0.0, term)
            own, rest = (o, r) if own is None else (own + o, rest + r)
        for p, zs in enumerate((own, rest)):
            z = [zs[BY * m:BY * (m + 1)] for m in range(BX)]
            for m in range(BX + 3):
                YP[n, p, m, TILE:TILE + BY, :] = total_of(wx[u] * z[m - u] for u in range(4) if 0 <= m - u < BX)
            for m in range(BX + 3):
                XP[n, p, 2 * HX + m, 2 * TILE:2 * TILE + 2 * BY, :] = total_of(
                    wy[v] * YP[n, p, m, TILE - v:TILE - v + 2 * BY, :] for v in range(4))

    def collect(k, q, ts, into):
        for t in ts:
            found = []
            for i in range(NBX):
                for j in range(NBY):
                    if 0 <= q - i <= 2 and 0 <= t - j <= 2:
                        bx, by = column(i), block(j)
                        found.append((i * NBY + j,
                                      (HX + 1) - shx[k, bx, 0, by] + BX * ((q - i) * up + (2 - q + i) * (1 - up)),
                                      (2 * TILE - HY + 1) - shy[k, bx, 0, by]
                                      + TILE * ((2 - t + j) * even + (t - j) * (1 - even))))

            def layer(p, m):
                return total_of(XP[n, p, x0 + m, pl.ds(y0, TILE), :] for n, x0, y0 in found)

            rims = [layer(1, m) for m in range(PK)]
            above, below = packed(lambda m: rims[m])
            into(rows_of(t), [layer(0, m) for m in range(PK)], below, above)

    def collect_own(ACC, k):
        for q in range(XG, XG + G):
            g = group_of(q)

            def into(rows, layers, below, above):
                for m in range(PK):
                    ACC[PK * g + m, rows, :] = layers[m]
                ACC[EX + g, rows, :], ACC[EX + EG + g, rows, :] = below, above

            collect(k, q, range(NT + 2), into)

    def collect_halo(k, ts):
        for q, side in ((EG - 1, place(up)),) + (((0, 1 - up),) if NS == 2 else ()):
            def into(rows, layers, below, above):
                for m, one in enumerate(layers + [below, above]):
                    HA[k, side, m, rows, :] = one

            collect(k, q, ts, into)

    def received(ACC, BK, i, t):
        bx = column(i)
        halos = ([0] if i == 0 and NS == 2 else []) + ([EG - 1] if i == NBX - 1 else [])
        halos = [group_of(q) for q in halos]

        def rows(center, L, pair):
            terms = [center[L, rows_of(t), :]]
            if t == 1 and pair:
                terms.append(BK[L, INNER, :])
            if t == NT:
                terms.append(BK[L, OUTER, :])
            return total_of(terms)

        first, last = (total_of([rows(BK, base + XG + bx, True)] + [rows(BK, base + g, False) for g in halos])
                       for base in (EX, EX + EG))
        return [total_of([rows(ACC, HX + bx * BX + m, True)] + [rows(BK, PK * g + m, False) for g in halos])
                + jnp.where(edge, unpacked(first, last, m), 0.0) for m in range(BX)]

    def product(k, bx, j):
        return STEP_SIZE * total_of(grad[k, c, bx * BX + j].astype(jnp.float32) * vel[c, bx * BX + j] for c in range(3))

    def clear(a, first, last):
        for end, views in ((0, first), (shape[a] - 1, last)):
            @pl.when(at[a] == end)
            def _(views=views):
                for ref in views:
                    ref[...] = jnp.zeros_like(ref)

    def clear_missing():
        sides = ((slice(0, HX), slice(EX, EX + XG), slice(EX + EG, EX + EG + XG)),
                 (slice(HX + TX, EX), slice(EX + XG + G, EX + EG), slice(EX + EG + XG + G, EX + 2 * EG)))
        low, high = ([BK.at[x] for BK in (BK0, BK1) for x in side] for side in sides)
        if NS == 2:
            low, high = low + [LX.at[:, 0]], high + [LX.at[:, 1]]
        clear("gx", low + [E.at[x] for E in (E0, E1) for x in sides[0]] + [VE.at[:, 0:LH]],
              high + [E.at[x] for E in (E0, E1) for x in sides[1]] + [VE.at[:, LH + TX:]])
        ends = slice(0, HY), slice(HY + TY, EY)
        low, high = ([ref.at[:, y] for ref in (E0, E1, BK0, BK1)] + [LX.at[:, :, :, y]] for y in ends)
        clear("gy", low + [YVD], high + [YVU])
        low, high = ([ref.at[x] for ref in (E0, E1, BK0, BK1)] for x in (slice(EX, EX + EG), slice(EX + EG, EX + 2 * EG)))
        clear("gz", low + [LX.at[:, :, HX, y] for y in (OY, OUTER)] + [VRD],
              high + [LX.at[:, :, HX + XG, y] for y in (OY, OUTER)] + [VRU])

    def send_faces():
        n = 4
        copies = [((1, 0, 0), vel.at[:, TX - LH:TX], VE.at[:, 0:LH, OY, :]),
                  ((-1, 0, 0), vel.at[:, 0:LH], VE.at[:, LH + TX:2 * LH + TX, OY, :])]
        for way, src, dst in copies:
            start(src, dst, way, n, 2 * EACH)
        VE[:, LH:LH + TX, OY, :] = vel[...]
        for c in range(3):
            for i in range(TX // 2):
                for h in range(2):
                    YSU[c, i, LH * h:LH * (h + 1), :] = vel[c, 2 * i + h, TY - LH:TY, :]
                    YSD[c, i, LH * h:LH * (h + 1), :] = vel[c, 2 * i + h, 0:LH, :]
            for g in range(TX // VPK):
                row = None
                for j in range(VPK):
                    turned = pltpu.roll(vel[c, VPK * g + j], (2 * LH * j + LH) % LANES, 1)
                    row = turned if row is None else jnp.where(lane2 // (2 * LH) == j, turned, row)
                SV[c, g] = row
        for way, src, dst in (((0, 1, 0), YSU, YVD), ((0, -1, 0), YSD, YVU),
                              ((0, 0, 1), SV, VRD), ((0, 0, -1), SV, VRU)):
            start(src, dst, way, n, 2 * EACH)

    def face_tiles(x, y, z):
        return (x * tiles_of(3 * LH, TY, LANES) + y * tiles_of(3 * TX // 2, 2 * LH, LANES)
                + z * tiles_of(3 * TX // VPK, TY, LANES))

    def regular():
        wait_for(recv.at[2 * EACH], face_tiles, AXES)
        for c in range(3):
            for i in range(TX // 2):
                for h in range(2):
                    VE[c, LH + 2 * i + h, HY - LH:HY, :] = YVD[c, i, LH * h:LH * (h + 1), :]
                    VE[c, LH + 2 * i + h, HY + TY:HY + TY + LH, :] = YVU[c, i, LH * h:LH * (h + 1), :]
        rows = lax.broadcasted_iota(jnp.int32, (2 * LANES, LANES), 0)
        cols = lax.broadcasted_iota(jnp.int32, (2 * LANES, LANES), 1)
        r = rows - LANES
        place = jnp.where(rows < LANES, rows, jnp.where(r < LH, r + LANES, r - LANES))
        known = jnp.logical_or(rows < LANES, jnp.logical_or(r < LH, r >= LANES - LH))
        gap = jnp.abs(place - cols)
        band = jnp.zeros((2 * LANES, LANES), jnp.float32)
        for k in range(5):
            tap = (3.0 if k == 0 else 1.0) * LAPLACE_TAPS[k]
            band = jnp.where(jnp.logical_and(known, gap == k), tap, band)
        for c in range(3):
            rims = []
            for g in range(TX // VPK):
                row = jnp.where(lane2 % (2 * LH) < LH, VRD[c, g], VRU[c, g])
                for j in range(VPK):
                    rims.append(pltpu.roll(row, (LANES - (2 * LH * j + LH)) % LANES, 1))
            rims = jnp.concatenate(rims, axis=0)
            own = vel[c].reshape(TX * TY, LANES)
            res = jnp.dot(jnp.concatenate([own, rims], axis=1), band,
                          preferred_element_type=jnp.float32,
                          precision=lax.Precision.HIGHEST).reshape(TX, TY, LANES)
            for k in range(1, 5):
                res = res + LAPLACE_TAPS[k] * (
                    VE[c, LH + k:LH + k + TX, OY, :] + VE[c, LH - k:LH - k + TX, OY, :]
                    + VE[c, LH:LH + TX, HY + k:HY + k + TY, :]
                    + VE[c, LH:LH + TX, HY - k:HY - k + TY, :])
            out[c] = (-REG_WEIGHT) * res

    met = False
    for i in reversed(range(NBX)):
        for copy in sources[NBX - 1 - i]:
            copy.wait()
        bx = column(i)
        for j in range(BX):
            E0[HX + bx * BX + j, OY, :] = product(0, bx, j)
        pack(E0, 0, bx, OY)
        if not met and (i == NBX - 1 and NS == 1 or i == 0):
            pl.semaphore_wait(barrier, total)
            forward_x(E0, 0, 0, 0)
            forward_x(E0, 0, 0, 1)
            met = True
    forward_rest(E0, 0, 0)

    clear_missing()
    send_faces()
    for copy in later:
        copy.wait()
    for i in range(NBX):
        for j in range(BX):
            E1[HX + column(i) * BX + j, OY, :] = product(1, column(i), j)
    YP[:, :, :, 0:TILE] = jnp.zeros_like(YP[:, :, :, 0:TILE])
    YP[:, :, :, TILE + BY:] = jnp.zeros_like(YP[:, :, :, TILE + BY:])
    XP[...] = jnp.zeros_like(XP)

    def enter(E, k, g, side, rows):
        for j in range(HX):
            E[PK * g + j, rows, :] = LX[k, side, j, rows, :]
        unpack(LX[k, side, HX, rows, :], LX[k, side, HX + XG, rows, :], g, rows)

    def forward(E, n, each, after):
        forward_pair(n, n)
        wait_rest(n)
        for i in range(NBX):
            g = XG + column(i)
            unpack(E[EX + g], E[EX + EG + g], g)
        for i in range(NBX):
            if i == 0:
                g = group_of(0)
                if NS == 2:
                    far_of(wait_late, n)
                    far_of(wait_off, n)
                    enter(E, n, g, 1 - up, slice(None))
                else:
                    unpack(E[EX + g], E[EX + EG + g], g)
            if i == NBX - 1:
                g = group_of(EG - 1)
                near_of(wait_late, n)
                enter(E, n, g, place(up), OY)
                enter(E, n, g, place(up), INNER)
            for j in range(NBY):
                if i == NBX - 1 and j == NBY - 1:
                    near_of(wait_off, n)
                    enter(E, n, g, place(up), OUTER)
                each(i * NBY + j, column(i), block(j), rows_of(1 + j))
                if i == NBX - 1 and j in (0, NBY - 1):
                    after(j)

    def first(n, bx, by, rows):
        res = gather_block(E0, 0, bx, by)
        for m in range(BX):
            E1[HX + bx * BX + m, rows, :] = E1[HX + bx * BX + m, rows, :] + res[m]
        pack(E1, 1, bx, rows)

    def first_sent(j):
        forward_x(E1, 1, 1, min(j, 1))

    forward(E0, 0, first, first_sent)
    forward_rest(E1, 1, 1)

    def second(n, bx, by, rows):
        spread_block(gather_block(E1, 1, bx, by), 1, n, bx, by)

    def second_sent(j):
        if j == 0:
            collect_halo(1, [0])
            return_x(1, BK1, 2, "pair")
        else:
            collect_halo(1, [NT + 1])
            return_x(1, BK1, 2, "off")

    forward(E1, 1, second, second_sent)

    def give_back(ACC, BK, k, n, meanwhile):
        collect_halo(k, range(1, NT + 1))
        return_x(k, BK, n, "own")
        collect_own(ACC, k)
        return_rest(ACC, BK, n)
        meanwhile()
        return_x(k, BK, n, "sum")

    def backward(ACC, BK, n, each, after):
        wait_rest(n)
        for i in range(NBX):
            if i == 0:
                far_of(wait_back, n)
                far_of(wait_last, n)
            if i == NBX - 1:
                near_of(wait_back, n)
            for j in reversed(range(NBY)):
                if i == NBX - 1 and j == 0:
                    near_of(wait_last, n)
                each(i * NBY + j, column(i), block(j), 1 + j, received(ACC, BK, i, 1 + j))
                if i == NBX - 1 and j in (0, NBY - 1):
                    after(j)

    give_back(ACC1, BK1, 1, 2, regular)

    def own_rows(t):
        return pl.ds(multiple(TILE * ((NT - t) * even + (t - 1) * (1 - even))), TILE)

    def third(n, bx, by, t, layers):
        for m in range(BX):
            ADJ[bx * BX + m, own_rows(t), :] = layers[m]
        spread_block(layers, 0, n, bx, by)

    def third_sent(j):
        if j == 0:
            collect_halo(0, [0])
            return_x(0, BK0, 3, "pair")
        else:
            collect_halo(0, [NT + 1])
            return_x(0, BK0, 3, "off")

    backward(ACC1, BK1, 2, third, third_sent)

    def gauss():
        for c in range(3):
            out[c] = out[c] + STEP_SIZE * grad[1, c].astype(jnp.float32) * ADJ[...]
        for n in range(3):
            wait_sent(n)
        wait_for(send.at[4], face_tiles, AXES)

    give_back(ACC0, BK0, 0, 3, gauss)

    def fourth(n, bx, by, t, layers):
        for m in range(BX):
            ADJ[bx * BX + m, own_rows(t), :] = layers[m]
        if t == 1:
            for c in range(3):
                for m in range(BX):
                    x = bx * BX + m
                    out[c, x] = out[c, x] + STEP_SIZE * grad[0, c, x].astype(jnp.float32) * ADJ[x]

    backward(ACC0, BK0, 3, fourth, lambda j: None)
    wait_sent(3)


def body(shape, velocity, gradients, shift_x, shift_y, shift_z, fractions):
    TX, TY, TZ = velocity.shape[1:]
    assert TZ == BZ == LANES and TX % VPK == 0 and TX % BX == 0 and TY % BY == 0
    assert shape["gy"] % 2 == 0 and TX // BX > 1 and TY // BY > 1
    assert BX == HX == PK and BY == HY == TILE and XG == 1
    EX, EY = TX + 2 * HX, TY + 2 * HY
    EG = EX // PK
    NS = 2 if shape["gx"] > 2 else 1
    NB = (TX // BX) * (TY // BY)
    most = EX * EY * (LANES + 2 * HZ) // (TILE * LANES)

    vm = lambda *s: pltpu.VMEM(s, jnp.float32)
    vmem = pl.BlockSpec(memory_space=pltpu.VMEM)
    hbm = pl.BlockSpec(memory_space=pltpu.HBM)
    shift_x, shift_y, shift_z = (s.transpose(0, 1, 3, 2) for s in (shift_x, shift_y, shift_z))
    fractions = fractions.transpose(0, 2, 3, 4, 1)
    return pl.pallas_call(
        functools.partial(kernel, shape),
        out_shape=jax.ShapeDtypeStruct(velocity.shape, jnp.float32),
        in_specs=[hbm] * 6,
        out_specs=vmem,
        scratch_shapes=[
            pltpu.VMEM(velocity.shape, velocity.dtype), pltpu.VMEM(gradients.shape, gradients.dtype),
            *[pltpu.SMEM(s.shape, s.dtype) for s in (shift_x, shift_y, shift_z, fractions)],
            pltpu.SemaphoreType.DMA((2 * (TX // BX) + 5,)),
            vm(EX + 2 * EG, EY, LANES), vm(EX + 2 * EG, EY, LANES),
            vm(2, NS, HX + 2 * XG, EY, LANES), vm(2, NS, HX + 2 * XG, EY, LANES),
            vm(2, NS, HX + 2 * XG, HY, LANES), vm(EX, EY, LANES),
            vm(NB, 2, BX + 3, 3 * TILE, LANES), vm(NB, 2, 2 * WX - BX, 5 * TILE, LANES),
            *[vm(EX + 2 * EG, EY, LANES) for _ in range(4)],
            vm(TX, TY, LANES),
            vm(2, 2, EG, EY, LANES),
            vm(3, TX + 2 * LH, EY, LANES),
            vm(3, TX // 2, 2 * LH, LANES), vm(3, TX // 2, 2 * LH, LANES),
            vm(3, TX // 2, 2 * LH, LANES), vm(3, TX // 2, 2 * LH, LANES),
            vm(3, TX // VPK, TY, LANES), vm(3, TX // VPK, TY, LANES), vm(3, TX // VPK, TY, LANES),
            vm(most, TILE, LANES),
            pltpu.SemaphoreType.DMA((5,)), pltpu.SemaphoreType.DMA((2 * (1 + 3 * NS) + 1,)),
        ],
        compiler_params=pltpu.CompilerParams(collective_id=0, has_side_effects=True,
                                             vmem_limit_bytes=24 << 20),
    )(*(pltpu.with_memory_space_constraint(x, pltpu.HBM) for x in (velocity, gradients, shift_x, shift_y, shift_z, fractions)))


def solution(mesh):
    in_specs = (
        P(None, "gx", "gy", "gz"),
        P(None, None, "gx", "gy", "gz"),
        P(None, "gx", "gy", "gz"),
        P(None, "gx", "gy", "gz"),
        P(None, "gx", "gy", "gz"),
        P(None, None, "gx", "gy", "gz"),
    )
    out_specs = P(None, "gx", "gy", "gz")
    return jax.shard_map(functools.partial(body, dict(mesh.shape)), mesh=mesh, in_specs=in_specs,
                         out_specs=out_specs, check_vma=False)
```

```python
import functools

import jax
import jax.numpy as jnp
from jax import lax
from jax.experimental import pallas as pl
from jax.experimental.pallas import tpu as pltpu
from jax.sharding import PartitionSpec as P

BX = 8
BY = 8
BZ = 128
RX = 6
RY = 6
RZ = 14
STEPS = 2

STEP_SIZE = 0.5
REG_WEIGHT = 0.1
LAPLACE_TAPS = (-205.0 / 72.0, 8.0 / 5.0, -1.0 / 5.0, 8.0 / 315.0, -1.0 / 560.0)

HX = RX + 2
HY = RY + 2
HZ = RZ + 2
LANES = 128
PK = LANES // HZ
XG = HX // PK
LH = 4
VPK = LANES // (2 * LH)
WX = BX + 2 * HX
WY = BY + 2 * HY
TILE = 8
MESH = pl.DeviceIdType.MESH
AXES = ("gx", "gy", "gz")
WAYS = sorted(((i, j, k) for i in (-1, 0, 1) for j in (-1, 0, 1) for k in (-1, 0, 1) if (i, j, k) != (0, 0, 0)),
              key=lambda d: (not d[0], sum(map(abs, d))))


def piece(way, own, halo):
    return {-1: (0, halo), 0: (halo, halo + own), 1: (halo + own, 2 * halo + own)}[way]


def border(way, own, halo):
    return {-1: (halo, 2 * halo), 0: (halo, halo + own), 1: (own, halo + own)}[way]


def kernel(shape, vel_in, grad_in, shx_in, shy_in, shz_in, frac_in, out,
           vel, grad, shx, shy, shz, frac, arrive,
           E0, E1, LX, HA, RL, U, YP, XP, ACC0, ACC1, BK0, BK1, ADJ, SP,
           VE, YSU, YSD, YVD, YVU, SV, VRD, VRU, BULK, send, recv):
    TX, TY, TZ = vel.shape[1:]
    NBX, NBY = TX // BX, TY // BY
    EX = TX + 2 * HX
    EY = TY + 2 * HY
    EG = EX // PK
    G = TX // PK
    OX = slice(HX, HX + TX)
    OY = slice(HY, HY + TY)
    NT = TY // TILE

    at = {a: lax.axis_index(a) for a in AXES}

    def has(way):
        ok = None
        for a, w in zip(AXES, way):
            if w:
                one = at[a] < shape[a] - 1 if w > 0 else at[a] > 0
                ok = one if ok is None else jnp.logical_and(ok, one)
        return ok

    def device(way):
        return {a: at[a] + w for a, w in zip(AXES, way) if w}

    up = (at["gx"] == 0).astype(jnp.int32)

    NS = 2 if shape["gx"] > 2 else 1
    even = 1 - lax.rem(at["gy"], 2)
    off = jnp.where(even == 1, at["gy"] > 0, at["gy"] < shape["gy"] - 1)

    def place(h):
        return h if NS == 2 else 0

    def multiple(x):
        return pl.multiple_of(x, TILE)

    A = pl.ds(multiple(HY + even * (TY - HY)), HY)
    B = pl.ds(multiple(HY + (1 - even) * HY), TY - HY)
    OFF = pl.ds(multiple(HY + (1 - even) * (TY - HY)), HY)
    INNER = pl.ds(multiple(even * (HY + TY)), HY)
    OUTER = pl.ds(multiple((1 - even) * (HY + TY)), HY)

    def column(i):
        return i * up + (NBX - 1 - i) * (1 - up)

    def group_of(q):
        return q * up + (EG - 1 - q) * (1 - up)

    def part(ref, i):
        return ref.at[:, pl.ds(column(i) * BX, BX)]

    for i in reversed(range(NBX)):
        for src, dst in ((vel_in, vel), (grad_in.at[0], grad.at[0])):
            pltpu.make_async_copy(part(src, i), part(dst, i), arrive.at[i]).start()
    later = [pltpu.make_async_copy(a, b, arrive.at[NBX + m]) for m, (a, b) in enumerate((
        (shx_in, shx), (shy_in, shy), (shz_in, shz), (frac_in, frac), (grad_in.at[1], grad.at[1])))]
    for copy in later:
        copy.start()

    barrier = pltpu.get_barrier_semaphore()
    total = jnp.int32(0)
    for way in WAYS:
        @pl.when(has(way))
        def _(way=way):
            pl.semaphore_signal(barrier, inc=1, device_id=device(way), device_id_type=MESH)
        total = total + has(way).astype(jnp.int32)

    def counts(a):
        if a == "off":
            return [(v, off if v else jnp.logical_not(off)) for v in range(2)] if shape["gy"] > 2 else [(0, None)]
        n = (at[a] > 0).astype(jnp.int32) + (at[a] < shape[a] - 1).astype(jnp.int32)
        return [(v, n == v if shape[a] > 2 else None) for v in ((0,), (1,), (1, 2))[min(shape[a], 3) - 1]]

    def wait_for(sem, tiles, axes, also=None):
        combos = [((), also)]
        for a in axes:
            combos = [(vs + (v,), c if ok is None else ok if c is None else jnp.logical_and(c, ok))
                      for vs, c in combos for v, ok in counts(a)]
        for vs, ok in combos:
            n = tiles(*vs)
            if not n:
                continue
            wait = pltpu.make_async_copy(BULK.at[0:n], BULK.at[0:n], sem).wait
            if ok is None:
                wait()
            else:
                pl.when(ok)(wait)

    def tiles_of(x, y, z):
        return x * y * z // (TILE * LANES)

    EACH = 1 + 2 * NS
    SIDES = [] if shape["gx"] == 1 else [(up, None)] if NS == 1 else [(0, has((-1, 0, 0))), (1, has((1, 0, 0)))]

    def sem(n, kind=None, h=0):
        return EACH * (n % 2) + (0 if kind is None else 1 + kind * NS + place(h))

    def wait_rest(n):
        wait_for(recv.at[sem(n)], lambda y, z: tiles_of(TX, TY + HY * y, LANES + HZ * z) - tiles_of(TX, TY, LANES),
                 ("gy", "gz"))

    def wait_early(n, h, ok):
        wait_for(recv.at[sem(n, 0, h)], lambda z: tiles_of(HX, HY, LANES + HZ * z), ("gz",), ok)

    def wait_late(n, h, ok):
        wait_for(recv.at[sem(n, 1, h)], lambda y, z: tiles_of(HX, TY - HY + HY * y, LANES + HZ * z)
                 + tiles_of(HX + 2 * XG, HY, LANES), ("off", "gz"), ok)

    def wait_back(n, h, ok):
        wait_for(recv.at[sem(n, 0, h)], lambda y, z: tiles_of(HX, TY + HY * y, LANES + HZ * z), ("off", "gz"), ok)

    def wait_pair(n, h, ok):
        wait_for(recv.at[sem(n, 1, h)], lambda: tiles_of(HX + 2 * XG, HY, LANES), (), ok)

    def far_of(wait, n):
        if NS == 2:
            wait(n, 1, jnp.logical_and(SIDES[1][1], up == 0))

    def near_of(wait, n):
        for h, ok in SIDES:
            wait(n, h, jnp.logical_and(ok, up == 1) if NS == 2 and h else ok)

    def wait_sent():
        def tiles(x, y, z):
            one = (tiles_of(TX, TY + HY * (1 + y), LANES + HZ * z) - tiles_of(TX, TY, LANES)
                   + x * (tiles_of(HX, TY + HY * y, LANES + HZ * z) + tiles_of(HX + 2 * XG, HY, LANES)))
            return 2 * STEPS * one + face_tiles(x, 1 + y, z)

        wait_for(send.at[0], tiles, ("gx", "off", "gz"))

    def start(src, dst, way, came):
        to_device(src, dst, device(way), has(way), came)

    def to_device(src, dst, where, ok, came):
        desc = pltpu.make_async_remote_copy(
            src_ref=src, dst_ref=dst, send_sem=send.at[0], recv_sem=recv.at[came],
            device_id=where, device_id_type=MESH)
        if ok is None:
            desc.start()
        else:
            pl.when(ok)(desc.start)

    def both(*oks):
        oks = [ok for ok in oks if ok is not None]
        return functools.reduce(jnp.logical_and, oks) if oks else None

    def beside(h, y=0, z=0):
        where = {"gx": at["gx"] + 2 * h - 1}
        if y:
            where["gy"] = at["gy"] + (1 - 2 * even if y < 0 else 2 * even - 1)
        if z:
            where["gz"] = at["gz"] + z
        return where

    partner = {"gy": at["gy"] + 2 * even - 1}

    lane2 = lax.broadcasted_iota(jnp.int32, (1, LANES), 1)
    group = lane2 // HZ
    edge = jnp.logical_or(lane2 < HZ, lane2 >= LANES - HZ)

    def packed(layer):
        first = last = None
        for j in range(PK):
            turned = pltpu.roll(layer(j), HZ * j, 1) if j else layer(0)
            first = turned if j == 0 else jnp.where(group == j, turned, first)
            last = turned if j == 0 else jnp.where(group == j - 1, turned, last)
        return first, last

    def unpacked(first, last, j):
        both = jnp.where(group == j, first, last)
        return pltpu.roll(both, LANES - HZ * j, 1) if j else both

    def region(way, dim_of):
        (x0, x1) = dim_of(way[0], G if way[2] else TX, XG if way[2] else HX)
        (y0, y1) = dim_of(way[1], TY, HY)
        return slice(x0, x1), slice(y0, y1)

    def rim(ref, way):
        xs, ys = region(way, piece)
        base = {0: 0, -1: EX, 1: EX + EG}[way[2]]
        return ref.at[slice(base + xs.start, base + xs.stop), ys, :]

    def forward_x(E, k, n):
        for h, ok in SIDES:
            mine, g, into = pl.ds(HX + h * (TX - HX), HX), XG + h * (G - XG), LX.at[k, place(1 - h)]

            def send_rows(rows, where, y, ok, came):
                to_device(E.at[mine, rows, :], into.at[0:HX, where, :], beside(h, y), ok, came)
                for z in (-1, 1):
                    to_device(SP.at[k, (z + 1) // 2, g, rows, :], into.at[HX + (1 - z) // 2, where, :],
                              beside(h, y, z), both(ok, has((0, 0, z))), came)

            send_rows(A, A, 0, ok, sem(n, 0, 1 - h))
            send_rows(OFF, INNER, -1, both(ok, off), sem(n, 1, 1 - h))
            send_rows(B, B, 0, ok, sem(n, 1, 1 - h))

    def forward_pair(k, n):
        for h, ok in SIDES:
            wait_early(n, h, ok)
            to_device(LX.at[k, place(h), :, A, :], LX.at[k, place(h), :, OUTER, :], partner, ok, sem(n, 1, h))

    def forward_rest(E, k, n, bx):
        for way in REST:
            ys, into = region(way, border)[1], region(tuple(-w for w in way), piece)[1]
            base = {0: HX, -1: EX + EG, 1: EX}[way[2]]
            if way[2]:
                src, dst = SP.at[k, (way[2] + 1) // 2, XG + bx, ys, :], E.at[base + XG + bx, into, :]
            else:
                src, dst = (E.at[pl.ds(HX + bx * BX, BX), rows, :] for rows in (ys, into))
            start(src, dst, way, sem(n))

    def return_x(k, BK, n, part):
        for h, ok in SIDES:
            mine, came = HA.at[k, place(h)], sem(n, 0, 1 - h)
            first = (1 - h) * (HX + TX)
            g = (1 - h) * (EG - 1)

            def send_rows(rows, into, y, ok):
                to_device(mine.at[0:HX, rows, :], BK.at[pl.ds(first, HX), into, :], beside(h, y), ok, came)
                for z in (-1, 1):
                    to_device(mine.at[HX + (z + 1) // 2, rows, :], BK.at[EX + EG * ((1 - z) // 2) + g, into, :],
                              beside(h, y, z), both(ok, has((0, 0, z))), came)

            if part == 0:
                to_device(mine.at[:, INNER, :], RL.at[k, place(h)], partner, ok, sem(n, 1, h))
                send_rows(OUTER, INNER, -1, both(ok, off))
                send_rows(B, B, 0, ok)
            else:
                wait_pair(n, h, ok)
                for L in range(HX + 2 * XG):
                    HA[k, place(h), L, A, :] = HA[k, place(h), L, A, :] + RL[k, place(h), L]
                send_rows(A, A, 0, ok)

    def return_rest(ACC, BK, n):
        for way in REST:
            start(rim(ACC, way), rim(BK, tuple(-w for w in way)), way, sem(n))

    REST = [w for w in WAYS if not w[0]]

    def pack_column(E, k, bx):
        SP[k, 0, XG + bx, OY, :], SP[k, 1, XG + bx, OY, :] = packed(lambda j: E[HX + bx * BX + j, OY, :])

    def unpack(below, above, g):
        for j in range(PK):
            U[PK * g + j] = unpacked(above, below, j)

    def taps(k, d, bx, by):
        e = frac[k, bx, by, 0, d].astype(jnp.float32) * 0.125
        e2 = e * e
        e3 = e2 * e
        return (0.5 * (2.0 * e2 - e3 - e), 0.5 * (3.0 * e3 - 5.0 * e2 + 2.0),
                0.5 * (4.0 * e2 - 3.0 * e3 + e), 0.5 * (e3 - e2))

    def total_of(terms):
        return functools.reduce(lambda a, b: a + b, terms)

    def gather_block(E, k, bx, by):
        a, b, c = shx[k, bx, 0, by], shy[k, bx, 0, by], shz[k, bx, 0, by]
        wx, wy, wz = (taps(k, d, bx, by) for d in range(3))
        x0 = bx * BX + (a + HX - 1)
        y0 = by * BY + (b + HY - 1)
        along = []
        for ref in (E, U):
            rows = [total_of(wy[v] * ref[x0 + m, pl.ds(y0 + v, BY), :] for v in range(4)) for m in range(BX + 3)]
            along.append([total_of(wx[u] * rows[m + u] for u in range(4)) for m in range(BX)])
        own, rest = (jnp.concatenate(p, axis=0) for p in along)
        res = None
        for w in range(4):
            s = c + (w - 1)
            inside = jnp.logical_and(lane2 >= s, lane2 < LANES + s)
            term = wz[w] * pltpu.roll(jnp.where(inside, own, rest), lax.rem(LANES - s, LANES), 1)
            res = term if res is None else res + term
        return [res[BY * m:BY * (m + 1)] for m in range(BX)]

    def spread_block(vals, k, i, bx, by):
        n = i * NBY + by
        c = shz[k, bx, 0, by]
        wx, wy, wz = (taps(k, d, bx, by) for d in range(3))
        flat = jnp.concatenate(vals, axis=0)
        own = rest = None
        for w in range(4):
            s = c + (w - 1)
            inside = jnp.logical_and(lane2 >= s, lane2 < LANES + s)
            term = wz[w] * pltpu.roll(flat, lax.rem(LANES + s, LANES), 1)
            o, r = jnp.where(inside, term, 0.0), jnp.where(inside, 0.0, term)
            own, rest = (o, r) if own is None else (own + o, rest + r)
        for p, zs in enumerate((own, rest)):
            z = [zs[BY * m:BY * (m + 1)] for m in range(BX)]
            for m in range(BX + 3):
                YP[n, p, m, TILE:TILE + BY, :] = total_of(wx[u] * z[m - u] for u in range(4) if 0 <= m - u < BX)
            for m in range(BX + 3):
                XP[n, p, 2 * HX + m, 2 * TILE:2 * TILE + 2 * BY, :] = total_of(
                    wy[v] * YP[n, p, m, TILE - v:TILE - v + 2 * BY, :] for v in range(4))

    def collect(k, q, ACC=None, halo=None):
        g = group_of(q)
        found = []
        for i in range(NBX):
            if 0 <= q - i <= 2:
                bx = column(i)
                offset = BX * ((q - i) * up + (2 - q + i) * (1 - up))
                for by in range(NBY):
                    found.append((i * NBY + by, by, (HX + 1) - shx[k, bx, 0, by] + offset,
                                  (2 * TILE - HY + 1) - shy[k, bx, 0, by]))

        def layer(p, j):
            tiles = [None] * (EY // TILE)
            for n, by, x0, y0 in found:
                rows = XP[n, p, x0 + j, pl.ds(y0, WY), :]
                for r in range(WY // TILE):
                    one = rows[r * TILE:(r + 1) * TILE]
                    old = tiles[by + r]
                    tiles[by + r] = one if old is None else old + one
            return jnp.concatenate(tiles, axis=0)

        rims = [layer(1, j) for j in range(PK)]
        above, below = packed(lambda j: rims[j])
        for j in range(PK):
            if halo is not None:
                HA[k, halo, j] = layer(0, j)
            else:
                ACC[PK * g + j] = layer(0, j)
        if halo is not None:
            HA[k, halo, HX], HA[k, halo, HX + XG] = below, above
        else:
            ACC[EX + EG + g], ACC[EX + g] = above, below

    def received(ACC, BK, i):
        bx = column(i)
        halos = ([0] if i == 0 and NS == 2 else []) + ([EG - 1] if i == NBX - 1 else [])
        halos = [group_of(q) for q in halos]

        def rows(center, L):
            tiles = [center[L, HY + TILE * t:HY + TILE * (t + 1), :] for t in range(NT)]
            tiles[0] = tiles[0] + BK[L, 0:HY, :]
            tiles[-1] = tiles[-1] + BK[L, HY + TY:, :]
            return jnp.concatenate(tiles, axis=0)

        rims = []
        for base in (EX, EX + EG):
            rims.append(total_of([rows(BK, base + XG + bx)] + [rows(BK, base + g) for g in halos]))
        first, last = rims
        res = []
        for j in range(BX):
            one = total_of([rows(ACC, HX + bx * BX + j)] + [rows(BK, PK * g + j) for g in halos])
            res.append(one + jnp.where(edge, unpacked(first, last, j), 0.0))
        return res

    def blocks(layers, by):
        return [one[by * BY:(by + 1) * BY] for one in layers]

    def product(k, bx, j):
        return STEP_SIZE * total_of(grad[k, c, bx * BX + j].astype(jnp.float32) * vel[c, bx * BX + j] for c in range(3))

    def clear(a, first, last):
        for end, views in ((0, first), (shape[a] - 1, last)):
            @pl.when(at[a] == end)
            def _(views=views):
                for ref in views:
                    ref[...] = jnp.zeros_like(ref)

    def clear_missing():
        sides = ((slice(0, HX), slice(EX, EX + XG), slice(EX + EG, EX + EG + XG)),
                 (slice(HX + TX, EX), slice(EX + XG + G, EX + EG), slice(EX + EG + XG + G, EX + 2 * EG)))
        low, high = ([BK.at[x] for BK in (BK0, BK1) for x in side] for side in sides)
        if NS == 2:
            low, high = low + [LX.at[:, 0]], high + [LX.at[:, 1]]
        clear("gx", low + [E.at[x] for E in (E0, E1) for x in sides[0]] + [VE.at[:, 0:LH]],
              high + [E.at[x] for E in (E0, E1) for x in sides[1]] + [VE.at[:, LH + TX:]])
        for BK in (BK0, BK1):
            for x in sides[0] + sides[1]:
                BK[x, INNER, :] = jnp.zeros_like(BK[x, INNER, :])
        ends = slice(0, HY), slice(HY + TY, EY)
        low, high = ([ref.at[:, y] for ref in (E0, E1, BK0, BK1)] + [LX.at[:, :, :, y]] for y in ends)
        clear("gy", low + [YVD], high + [YVU])
        low, high = ([ref.at[x] for ref in (E0, E1, BK0, BK1)] for x in (slice(EX, EX + EG), slice(EX + EG, EX + 2 * EG)))
        clear("gz", low + [LX.at[:, :, HX, y] for y in (OY, OUTER)] + [VRD],
              high + [LX.at[:, :, HX + XG, y] for y in (OY, OUTER)] + [VRU])

    def send_faces():
        copies = [((1, 0, 0), vel.at[:, TX - LH:TX], VE.at[:, 0:LH, OY, :]),
                  ((-1, 0, 0), vel.at[:, 0:LH], VE.at[:, LH + TX:2 * LH + TX, OY, :])]
        for way, src, dst in copies:
            start(src, dst, way, 2 * EACH)
        VE[:, LH:LH + TX, OY, :] = vel[...]
        for c in range(3):
            for i in range(TX // 2):
                for h in range(2):
                    YSU[c, i, LH * h:LH * (h + 1), :] = vel[c, 2 * i + h, TY - LH:TY, :]
                    YSD[c, i, LH * h:LH * (h + 1), :] = vel[c, 2 * i + h, 0:LH, :]
            for g in range(TX // VPK):
                row = None
                for j in range(VPK):
                    turned = pltpu.roll(vel[c, VPK * g + j], (2 * LH * j + LH) % LANES, 1)
                    row = turned if row is None else jnp.where(lane2 // (2 * LH) == j, turned, row)
                SV[c, g] = row
        for way, src, dst in (((0, 1, 0), YSU, YVD), ((0, -1, 0), YSD, YVU),
                              ((0, 0, 1), SV, VRD), ((0, 0, -1), SV, VRU)):
            start(src, dst, way, 2 * EACH)

    def face_tiles(x, y, z):
        return (x * tiles_of(3 * LH, TY, LANES) + y * tiles_of(3 * TX // 2, 2 * LH, LANES)
                + z * tiles_of(3 * TX // VPK, TY, LANES))

    def regular():
        wait_for(recv.at[2 * EACH], face_tiles, AXES)
        for c in range(3):
            for i in range(TX // 2):
                for h in range(2):
                    VE[c, LH + 2 * i + h, HY - LH:HY, :] = YVD[c, i, LH * h:LH * (h + 1), :]
                    VE[c, LH + 2 * i + h, HY + TY:HY + TY + LH, :] = YVU[c, i, LH * h:LH * (h + 1), :]
        rows = lax.broadcasted_iota(jnp.int32, (2 * LANES, LANES), 0)
        cols = lax.broadcasted_iota(jnp.int32, (2 * LANES, LANES), 1)
        r = rows - LANES
        place = jnp.where(rows < LANES, rows, jnp.where(r < LH, r + LANES, r - LANES))
        known = jnp.logical_or(rows < LANES, jnp.logical_or(r < LH, r >= LANES - LH))
        gap = jnp.abs(place - cols)
        band = jnp.zeros((2 * LANES, LANES), jnp.float32)
        for k in range(5):
            tap = (3.0 if k == 0 else 1.0) * LAPLACE_TAPS[k]
            band = jnp.where(jnp.logical_and(known, gap == k), tap, band)
        for c in range(3):
            rims = []
            for g in range(TX // VPK):
                row = jnp.where(lane2 % (2 * LH) < LH, VRD[c, g], VRU[c, g])
                for j in range(VPK):
                    rims.append(pltpu.roll(row, (LANES - (2 * LH * j + LH)) % LANES, 1))
            rims = jnp.concatenate(rims, axis=0)
            own = vel[c].reshape(TX * TY, LANES)
            res = jnp.dot(jnp.concatenate([own, rims], axis=1), band,
                          preferred_element_type=jnp.float32,
                          precision=lax.Precision.HIGHEST).reshape(TX, TY, LANES)
            for k in range(1, 5):
                res = res + LAPLACE_TAPS[k] * (
                    VE[c, LH + k:LH + k + TX, OY, :] + VE[c, LH - k:LH - k + TX, OY, :]
                    + VE[c, LH:LH + TX, HY + k:HY + k + TY, :]
                    + VE[c, LH:LH + TX, HY - k:HY - k + TY, :])
            out[c] = (-REG_WEIGHT) * res

    met = False
    for i in reversed(range(NBX)):
        wait_for(arrive.at[i], lambda: tiles_of(3 * BX, TY, LANES) * 3 // 2, ())
        bx = column(i)
        for j in range(BX):
            E0[HX + bx * BX + j, OY, :] = product(0, bx, j)
        pack_column(E0, 0, bx)
        if not met and (i == NBX - 1 and NS == 1 or i == 0):
            pl.semaphore_wait(barrier, total)
            forward_x(E0, 0, 0)
            met = True
    for i in range(NBX):
        forward_rest(E0, 0, 0, column(i))

    clear_missing()
    send_faces()
    for copy in later:
        copy.wait()
    for i in range(NBX):
        for j in range(BX):
            E1[HX + column(i) * BX + j, OY, :] = product(1, column(i), j)
    YP[:, :, :, 0:TILE] = jnp.zeros_like(YP[:, :, :, 0:TILE])
    YP[:, :, :, TILE + BY:] = jnp.zeros_like(YP[:, :, :, TILE + BY:])
    XP[...] = jnp.zeros_like(XP)

    def enter(E, k, g, side):
        for j in range(HX):
            E[PK * g + j] = LX[k, side, j]
        unpack(LX[k, side, HX], LX[k, side, HX + XG], g)

    def forward(E, n, each):
        forward_pair(n, n)
        wait_rest(n)
        for i in range(NBX):
            g = XG + column(i)
            unpack(E[EX + g], E[EX + EG + g], g)
        for i in range(NBX):
            if i == 0:
                g = group_of(0)
                if NS == 2:
                    far_of(wait_late, n)
                    enter(E, n, g, 1 - up)
                else:
                    unpack(E[EX + g], E[EX + EG + g], g)
            if i == NBX - 1:
                near_of(wait_late, n)
                enter(E, n, group_of(EG - 1), place(up))
            each(i, column(i))

    def first(i, bx):
        for by in range(NBY):
            res = gather_block(E0, 0, bx, by)
            for m in range(BX):
                rows = slice(HY + by * BY, HY + (by + 1) * BY)
                E1[HX + bx * BX + m, rows, :] = E1[HX + bx * BX + m, rows, :] + res[m]
        pack_column(E1, 1, bx)
        if i == NBX - 1:
            forward_x(E1, 1, 1)
        forward_rest(E1, 1, 1, bx)

    forward(E0, 0, first)

    def second(i, bx):
        for by in range(NBY):
            spread_block(gather_block(E1, 1, bx, by), 1, i, bx, by)

    forward(E1, 1, second)

    def give_back(ACC, BK, k, n, meanwhile):
        collect(k, EG - 1, halo=place(up))
        if NS == 2:
            collect(k, 0, halo=1 - up)
        return_x(k, BK, n, 0)
        for q in range(XG, XG + G):
            collect(k, q, ACC)
        return_rest(ACC, BK, n)
        meanwhile()
        return_x(k, BK, n, 1)

    def backward(ACC, BK, n, each):
        wait_rest(n)
        for i in range(NBX):
            if i == 0:
                far_of(wait_back, n)
            if i == NBX - 1:
                near_of(wait_back, n)
            each(i, column(i), received(ACC, BK, i))

    give_back(ACC1, BK1, 1, 2, regular)

    def third(i, bx, layers):
        for j in range(BX):
            ADJ[bx * BX + j] = layers[j]
        for by in range(NBY):
            spread_block(blocks(layers, by), 0, i, bx, by)

    backward(ACC1, BK1, 2, third)
    def gauss():
        for c in range(3):
            out[c] = out[c] + STEP_SIZE * grad[1, c].astype(jnp.float32) * ADJ[...]

    give_back(ACC0, BK0, 0, 3, gauss)

    def fourth(i, bx, layers):
        for c in range(3):
            for j in range(BX):
                x = bx * BX + j
                out[c, x] = out[c, x] + STEP_SIZE * grad[0, c, x].astype(jnp.float32) * layers[j]

    backward(ACC0, BK0, 3, fourth)
    wait_sent()


def body(shape, velocity, gradients, shift_x, shift_y, shift_z, fractions):
    TX, TY, TZ = velocity.shape[1:]
    assert TZ == BZ == LANES and TX % VPK == 0 and TX % BX == 0 and TY % BY == 0
    assert shape["gy"] % 2 == 0 and TX // BX > 1
    assert BX == HX == PK and BY == HY == TILE and XG == 1
    EX, EY = TX + 2 * HX, TY + 2 * HY
    EG = EX // PK
    NS = 2 if shape["gx"] > 2 else 1
    NB = (TX // BX) * (TY // BY)
    most = (2 * STEPS + 1) * EX * EY * (LANES + 2 * HZ) // (TILE * LANES)

    vm = lambda *s: pltpu.VMEM(s, jnp.float32)
    vmem = pl.BlockSpec(memory_space=pltpu.VMEM)
    hbm = pl.BlockSpec(memory_space=pltpu.HBM)
    shift_x, shift_y, shift_z = (s.transpose(0, 1, 3, 2) for s in (shift_x, shift_y, shift_z))
    fractions = fractions.transpose(0, 2, 3, 4, 1)
    return pl.pallas_call(
        functools.partial(kernel, shape),
        out_shape=jax.ShapeDtypeStruct(velocity.shape, jnp.float32),
        in_specs=[hbm] * 6,
        out_specs=vmem,
        scratch_shapes=[
            pltpu.VMEM(velocity.shape, velocity.dtype), pltpu.VMEM(gradients.shape, gradients.dtype),
            *[pltpu.SMEM(s.shape, s.dtype) for s in (shift_x, shift_y, shift_z, fractions)],
            pltpu.SemaphoreType.DMA((TX // BX + 5,)),
            vm(EX + 2 * EG, EY, LANES), vm(EX + 2 * EG, EY, LANES),
            vm(2, NS, HX + 2 * XG, EY, LANES), vm(2, NS, HX + 2 * XG, EY, LANES),
            vm(2, NS, HX + 2 * XG, HY, LANES), vm(EX, EY, LANES),
            vm(NB, 2, BX + 3, 3 * TILE, LANES), vm(NB, 2, 2 * WX - BX, 5 * TILE, LANES),
            *[vm(EX + 2 * EG, EY, LANES) for _ in range(4)],
            vm(TX, TY, LANES),
            vm(2, 2, EG, EY, LANES),
            vm(3, TX + 2 * LH, EY, LANES),
            vm(3, TX // 2, 2 * LH, LANES), vm(3, TX // 2, 2 * LH, LANES),
            vm(3, TX // 2, 2 * LH, LANES), vm(3, TX // 2, 2 * LH, LANES),
            vm(3, TX // VPK, TY, LANES), vm(3, TX // VPK, TY, LANES), vm(3, TX // VPK, TY, LANES),
            vm(most, TILE, LANES),
            pltpu.SemaphoreType.DMA((1,)), pltpu.SemaphoreType.DMA((2 * (1 + 2 * NS) + 1,)),
        ],
        compiler_params=pltpu.CompilerParams(collective_id=0, has_side_effects=True,
                                             vmem_limit_bytes=24 << 20),
    )(*(pltpu.with_memory_space_constraint(x, pltpu.HBM) for x in (velocity, gradients, shift_x, shift_y, shift_z, fractions)))


def solution(mesh):
    in_specs = (
        P(None, "gx", "gy", "gz"),
        P(None, None, "gx", "gy", "gz"),
        P(None, "gx", "gy", "gz"),
        P(None, "gx", "gy", "gz"),
        P(None, "gx", "gy", "gz"),
        P(None, None, "gx", "gy", "gz"),
    )
    out_specs = P(None, "gx", "gy", "gz")
    return jax.shard_map(functools.partial(body, dict(mesh.shape)), mesh=mesh, in_specs=in_specs,
                         out_specs=out_specs, check_vma=False)
```

```python
import functools

import jax
import jax.numpy as jnp
from jax import lax
from jax.experimental import pallas as pl
from jax.experimental.pallas import tpu as pltpu
from jax.sharding import PartitionSpec as P

BX = 8
BY = 8
BZ = 128
RX = 6
RY = 6
RZ = 14
STEPS = 2

STEP_SIZE = 0.5
REG_WEIGHT = 0.1
LAPLACE_TAPS = (-205.0 / 72.0, 8.0 / 5.0, -1.0 / 5.0, 8.0 / 315.0, -1.0 / 560.0)

HX = RX + 2
HY = RY + 2
HZ = RZ + 2
LANES = 128
PK = LANES // HZ
XG = HX // PK
LH = 4
VPK = LANES // (2 * LH)
WX = BX + 2 * HX
WY = BY + 2 * HY
TILE = 8
MESH = pl.DeviceIdType.MESH
AXES = ("gx", "gy", "gz")
WAYS = sorted(((i, j, k) for i in (-1, 0, 1) for j in (-1, 0, 1) for k in (-1, 0, 1) if (i, j, k) != (0, 0, 0)),
              key=lambda d: (not d[0], sum(map(abs, d))))


def piece(way, own, halo):
    return {-1: (0, halo), 0: (halo, halo + own), 1: (halo + own, 2 * halo + own)}[way]


def border(way, own, halo):
    return {-1: (halo, 2 * halo), 0: (halo, halo + own), 1: (own, halo + own)}[way]


def kernel(shape, vel_in, grad_in, shx_in, shy_in, shz_in, frac_in, out,
           vel, grad, shx, shy, shz, frac, arrive,
           E0, E1, LX, HA, RL, U, YP, XP, ACC0, ACC1, BK0, BK1, ADJ, SP,
           VE, YSU, YSD, YVD, YVU, SV, VRD, VRU, BULK, send, recv):
    TX, TY, TZ = vel.shape[1:]
    NBX, NBY = TX // BX, TY // BY
    EX = TX + 2 * HX
    EY = TY + 2 * HY
    EG = EX // PK
    G = TX // PK
    OX = slice(HX, HX + TX)
    OY = slice(HY, HY + TY)
    NT = TY // TILE

    at = {a: lax.axis_index(a) for a in AXES}

    def has(way):
        ok = None
        for a, w in zip(AXES, way):
            if w:
                one = at[a] < shape[a] - 1 if w > 0 else at[a] > 0
                ok = one if ok is None else jnp.logical_and(ok, one)
        return ok

    def device(way):
        return {a: at[a] + w for a, w in zip(AXES, way) if w}

    up = (at["gx"] == 0).astype(jnp.int32)

    NS = 2 if shape["gx"] > 2 else 1
    even = 1 - lax.rem(at["gy"], 2)
    off = jnp.where(even == 1, at["gy"] > 0, at["gy"] < shape["gy"] - 1)

    odd = even == 0
    SEAM = pl.ds(0, 2 * HY), pl.ds(TY, 2 * HY)

    def place(h):
        return h if NS == 2 else 0

    def multiple(x):
        return pl.multiple_of(x, TILE)

    A = pl.ds(multiple(HY + even * (TY - HY)), HY)
    B = pl.ds(multiple(HY + (1 - even) * HY), TY - HY)
    OFF = pl.ds(multiple(HY + (1 - even) * (TY - HY)), HY)
    INNER = pl.ds(multiple(even * (HY + TY)), HY)
    OUTER = pl.ds(multiple((1 - even) * (HY + TY)), HY)

    def column(i):
        return i * up + (NBX - 1 - i) * (1 - up)

    def group_of(q):
        return q * up + (EG - 1 - q) * (1 - up)

    def part(ref, i):
        return ref.at[:, pl.ds(column(i) * BX, BX)]

    for i in reversed(range(NBX)):
        for src, dst in ((vel_in, vel), (grad_in.at[0], grad.at[0])):
            pltpu.make_async_copy(part(src, i), part(dst, i), arrive.at[i]).start()
    later = [pltpu.make_async_copy(a, b, arrive.at[NBX + m]) for m, (a, b) in enumerate((
        (shx_in, shx), (shy_in, shy), (shz_in, shz), (frac_in, frac), (grad_in.at[1], grad.at[1])))]
    for copy in later:
        copy.start()

    barrier = pltpu.get_barrier_semaphore()
    total = jnp.int32(0)
    for way in WAYS:
        @pl.when(has(way))
        def _(way=way):
            pl.semaphore_signal(barrier, inc=1, device_id=device(way), device_id_type=MESH)
        total = total + has(way).astype(jnp.int32)

    def counts(a):
        if a == "even":
            return [(v, even == v) for v in range(2)]
        if a == "off":
            return [(v, off if v else jnp.logical_not(off)) for v in range(2)] if shape["gy"] > 2 else [(0, None)]
        n = (at[a] > 0).astype(jnp.int32) + (at[a] < shape[a] - 1).astype(jnp.int32)
        return [(v, n == v if shape[a] > 2 else None) for v in ((0,), (1,), (1, 2))[min(shape[a], 3) - 1]]

    def wait_for(sem, tiles, axes, also=None):
        combos = [((), also)]
        for a in axes:
            combos = [(vs + (v,), c if ok is None else ok if c is None else jnp.logical_and(c, ok))
                      for vs, c in combos for v, ok in counts(a)]
        for vs, ok in combos:
            n = tiles(*vs)
            if not n:
                continue
            wait = pltpu.make_async_copy(BULK.at[0:n], BULK.at[0:n], sem).wait
            if ok is None:
                wait()
            else:
                pl.when(ok)(wait)

    def tiles_of(x, y, z):
        return x * y * z // (TILE * LANES)

    EACH = 1 + 2 * NS
    SIDES = [] if shape["gx"] == 1 else [(up, None)] if NS == 1 else [(0, has((-1, 0, 0))), (1, has((1, 0, 0)))]

    def sem(n, kind=None, h=0):
        return EACH * (n % 2) + (0 if kind is None else 1 + kind * NS + place(h))

    def wait_rest(n):
        wait_for(recv.at[sem(n)], lambda y, z: tiles_of(TX, TY + HY * y, LANES + HZ * z) - tiles_of(TX, TY, LANES),
                 ("gy", "gz"))

    def wait_early(n, h, ok):
        wait_for(recv.at[sem(n, 0, h)], lambda z: 2 * tiles_of(HX, HY, LANES + HZ * z), ("gz",), both(ok, odd))

    def wait_late(n, h, ok):
        wait_for(recv.at[sem(n, 1, h)], lambda e, y, z: tiles_of(HX, TY - HY + HY * y, LANES + HZ * z)
                 + e * tiles_of(HX + 2 * XG, 2 * HY, LANES), ("even", "off", "gz"), ok)

    def wait_back(n, h, ok):
        wait_for(recv.at[sem(n, 0, h)], lambda y, z: tiles_of(HX, TY + HY * y, LANES + HZ * z), ("off", "gz"), ok)

    def wait_pair(n, h, ok):
        wait_for(recv.at[sem(n, 1, h)], lambda: tiles_of(HX + 2 * XG, 2 * HY, LANES), (), both(ok, odd))

    def far_of(wait, n):
        if NS == 2:
            wait(n, 1, jnp.logical_and(SIDES[1][1], up == 0))

    def near_of(wait, n):
        for h, ok in SIDES:
            wait(n, h, jnp.logical_and(ok, up == 1) if NS == 2 and h else ok)

    def wait_sent():
        def tiles(x, e, y, z):
            seam = tiles_of(HX + 2 * XG, 2 * HY, LANES)
            along = seam + tiles_of(HX, 2 * (TY + HY * y) + (-HY if e else HY), LANES + HZ * z)
            one = tiles_of(TX, TY + HY * (1 + y), LANES + HZ * z) - tiles_of(TX, TY, LANES)
            return STEPS * (2 * one + x * along) + face_tiles(x, 1 + y, z)

        wait_for(send.at[0], tiles, ("gx", "even", "off", "gz"))

    def start(src, dst, way, came):
        to_device(src, dst, device(way), has(way), came)

    def to_device(src, dst, where, ok, came):
        desc = pltpu.make_async_remote_copy(
            src_ref=src, dst_ref=dst, send_sem=send.at[0], recv_sem=recv.at[came],
            device_id=where, device_id_type=MESH)
        if ok is None:
            desc.start()
        else:
            pl.when(ok)(desc.start)

    def both(*oks):
        oks = [ok for ok in oks if ok is not None]
        return functools.reduce(jnp.logical_and, oks) if oks else None

    def beside(h, y=0, z=0):
        where = {"gx": at["gx"] + 2 * h - 1}
        if y is even:
            where["gy"] = at["gy"] + even
        elif y:
            where["gy"] = at["gy"] + (1 - 2 * even if y < 0 else 2 * even - 1)
        if z:
            where["gz"] = at["gz"] + z
        return where

    partner = {"gy": at["gy"] + 2 * even - 1}

    lane2 = lax.broadcasted_iota(jnp.int32, (1, LANES), 1)
    group = lane2 // HZ
    edge = jnp.logical_or(lane2 < HZ, lane2 >= LANES - HZ)

    def packed(layer):
        first = last = None
        for j in range(PK):
            turned = pltpu.roll(layer(j), HZ * j, 1) if j else layer(0)
            first = turned if j == 0 else jnp.where(group == j, turned, first)
            last = turned if j == 0 else jnp.where(group == j - 1, turned, last)
        return first, last

    def unpacked(first, last, j):
        both = jnp.where(group == j, first, last)
        return pltpu.roll(both, LANES - HZ * j, 1) if j else both

    def region(way, dim_of):
        (x0, x1) = dim_of(way[0], G if way[2] else TX, XG if way[2] else HX)
        (y0, y1) = dim_of(way[1], TY, HY)
        return slice(x0, x1), slice(y0, y1)

    def rim(ref, way):
        xs, ys = region(way, piece)
        base = {0: 0, -1: EX, 1: EX + EG}[way[2]]
        return ref.at[slice(base + xs.start, base + xs.stop), ys, :]

    def forward_x(E, k, n):
        for h, ok in SIDES:
            mine, g, into = pl.ds(HX + h * (TX - HX), HX), XG + h * (G - XG), LX.at[k, place(1 - h)]

            def send_rows(rows, where, y, ok, came):
                to_device(E.at[mine, rows, :], into.at[0:HX, where, :], beside(h, y), ok, came)
                for z in (-1, 1):
                    to_device(SP.at[k, (z + 1) // 2, g, rows, :], into.at[HX + (1 - z) // 2, where, :],
                              beside(h, y, z), both(ok, has((0, 0, z))), came)

            send_rows(A, pl.ds(multiple(HY * (1 - even)), HY), even, ok, sem(n, 0, 1 - h))
            send_rows(OFF, INNER, -1, both(ok, off), sem(n, 1, 1 - h))
            send_rows(B, B, 0, ok, sem(n, 1, 1 - h))

    def forward_pair(k, n):
        for h, ok in SIDES:
            wait_early(n, h, ok)
            to_device(LX.at[k, place(h), :, SEAM[0], :], LX.at[k, place(h), :, SEAM[1], :], partner, both(ok, odd),
                      sem(n, 1, h))

    def forward_rest(E, k, n, bx):
        for way in REST:
            ys, into = region(way, border)[1], region(tuple(-w for w in way), piece)[1]
            base = {0: HX, -1: EX + EG, 1: EX}[way[2]]
            if way[2]:
                src, dst = SP.at[k, (way[2] + 1) // 2, XG + bx, ys, :], E.at[base + XG + bx, into, :]
            else:
                src, dst = (E.at[pl.ds(HX + bx * BX, BX), rows, :] for rows in (ys, into))
            start(src, dst, way, sem(n))

    def return_x(k, BK, n, part):
        for h, ok in SIDES:
            mine, came = HA.at[k, place(h)], sem(n, 0, 1 - h)
            first = (1 - h) * (HX + TX)
            g = (1 - h) * (EG - 1)

            def send_rows(rows, into, y, ok):
                to_device(mine.at[0:HX, rows, :], BK.at[pl.ds(first, HX), into, :], beside(h, y), ok, came)
                for z in (-1, 1):
                    to_device(mine.at[HX + (z + 1) // 2, rows, :], BK.at[EX + EG * ((1 - z) // 2) + g, into, :],
                              beside(h, y, z), both(ok, has((0, 0, z))), came)

            if part == 0:
                to_device(mine.at[:, SEAM[1], :], RL.at[k, place(h)], partner, both(ok, even == 1), sem(n, 1, h))
                send_rows(OUTER, INNER, -1, both(ok, off))
                send_rows(B, B, 0, ok)
            else:
                wait_pair(n, h, ok)

                @pl.when(odd)
                def _(h=h):
                    for L in range(HX + 2 * XG):
                        HA[k, place(h), L, SEAM[0], :] = HA[k, place(h), L, SEAM[0], :] + RL[k, place(h), L]

                send_rows(pl.ds(0, HY), pl.ds(TY, HY), 1, both(ok, odd))
                send_rows(pl.ds(HY, HY), pl.ds(HY, HY), 0, both(ok, odd))

    def return_rest(ACC, BK, n):
        for way in REST:
            start(rim(ACC, way), rim(BK, tuple(-w for w in way)), way, sem(n))

    REST = [w for w in WAYS if not w[0]]

    def pack_column(E, k, bx):
        SP[k, 0, XG + bx, OY, :], SP[k, 1, XG + bx, OY, :] = packed(lambda j: E[HX + bx * BX + j, OY, :])

    def unpack(below, above, g):
        for j in range(PK):
            U[PK * g + j] = unpacked(above, below, j)

    def taps(k, d, bx, by):
        e = frac[k, bx, by, 0, d].astype(jnp.float32) * 0.125
        e2 = e * e
        e3 = e2 * e
        return (0.5 * (2.0 * e2 - e3 - e), 0.5 * (3.0 * e3 - 5.0 * e2 + 2.0),
                0.5 * (4.0 * e2 - 3.0 * e3 + e), 0.5 * (e3 - e2))

    def total_of(terms):
        return functools.reduce(lambda a, b: a + b, terms)

    def gather_block(E, k, bx, by):
        a, b, c = shx[k, bx, 0, by], shy[k, bx, 0, by], shz[k, bx, 0, by]
        wx, wy, wz = (taps(k, d, bx, by) for d in range(3))
        x0 = bx * BX + (a + HX - 1)
        y0 = by * BY + (b + HY - 1)
        along = []
        for ref in (E, U):
            rows = [total_of(wy[v] * ref[x0 + m, pl.ds(y0 + v, BY), :] for v in range(4)) for m in range(BX + 3)]
            along.append([total_of(wx[u] * rows[m + u] for u in range(4)) for m in range(BX)])
        own, rest = (jnp.concatenate(p, axis=0) for p in along)
        res = None
        for w in range(4):
            s = c + (w - 1)
            inside = jnp.logical_and(lane2 >= s, lane2 < LANES + s)
            term = wz[w] * pltpu.roll(jnp.where(inside, own, rest), lax.rem(LANES - s, LANES), 1)
            res = term if res is None else res + term
        return [res[BY * m:BY * (m + 1)] for m in range(BX)]

    def spread_block(vals, k, i, bx, by):
        n = i * NBY + by
        c = shz[k, bx, 0, by]
        wx, wy, wz = (taps(k, d, bx, by) for d in range(3))
        flat = jnp.concatenate(vals, axis=0)
        own = rest = None
        for w in range(4):
            s = c + (w - 1)
            inside = jnp.logical_and(lane2 >= s, lane2 < LANES + s)
            term = wz[w] * pltpu.roll(flat, lax.rem(LANES + s, LANES), 1)
            o, r = jnp.where(inside, term, 0.0), jnp.where(inside, 0.0, term)
            own, rest = (o, r) if own is None else (own + o, rest + r)
        for p, zs in enumerate((own, rest)):
            z = [zs[BY * m:BY * (m + 1)] for m in range(BX)]
            for m in range(BX + 3):
                YP[n, p, m, TILE:TILE + BY, :] = total_of(wx[u] * z[m - u] for u in range(4) if 0 <= m - u < BX)
            for m in range(BX + 3):
                XP[n, p, 2 * HX + m, 2 * TILE:2 * TILE + 2 * BY, :] = total_of(
                    wy[v] * YP[n, p, m, TILE - v:TILE - v + 2 * BY, :] for v in range(4))

    def collect(k, q, ACC=None, halo=None):
        g = group_of(q)
        found = []
        for i in range(NBX):
            if 0 <= q - i <= 2:
                bx = column(i)
                offset = BX * ((q - i) * up + (2 - q + i) * (1 - up))
                for by in range(NBY):
                    found.append((i * NBY + by, by, (HX + 1) - shx[k, bx, 0, by] + offset,
                                  (2 * TILE - HY + 1) - shy[k, bx, 0, by]))

        def layer(p, j):
            tiles = [None] * (EY // TILE)
            for n, by, x0, y0 in found:
                rows = XP[n, p, x0 + j, pl.ds(y0, WY), :]
                for r in range(WY // TILE):
                    one = rows[r * TILE:(r + 1) * TILE]
                    old = tiles[by + r]
                    tiles[by + r] = one if old is None else old + one
            return jnp.concatenate(tiles, axis=0)

        rims = [layer(1, j) for j in range(PK)]
        above, below = packed(lambda j: rims[j])
        for j in range(PK):
            if halo is not None:
                HA[k, halo, j] = layer(0, j)
            else:
                ACC[PK * g + j] = layer(0, j)
        if halo is not None:
            HA[k, halo, HX], HA[k, halo, HX + XG] = below, above
        else:
            ACC[EX + EG + g], ACC[EX + g] = above, below

    def received(ACC, BK, i):
        bx = column(i)
        halos = ([0] if i == 0 and NS == 2 else []) + ([EG - 1] if i == NBX - 1 else [])
        halos = [group_of(q) for q in halos]

        def rows(center, L):
            tiles = [center[L, HY + TILE * t:HY + TILE * (t + 1), :] for t in range(NT)]
            tiles[0] = tiles[0] + BK[L, 0:HY, :]
            tiles[-1] = tiles[-1] + BK[L, HY + TY:, :]
            return jnp.concatenate(tiles, axis=0)

        rims = []
        for base in (EX, EX + EG):
            rims.append(total_of([rows(BK, base + XG + bx)] + [rows(BK, base + g) for g in halos]))
        first, last = rims
        res = []
        for j in range(BX):
            one = total_of([rows(ACC, HX + bx * BX + j)] + [rows(BK, PK * g + j) for g in halos])
            res.append(one + jnp.where(edge, unpacked(first, last, j), 0.0))
        return res

    def blocks(layers, by):
        return [one[by * BY:(by + 1) * BY] for one in layers]

    def product(k, bx, j):
        return STEP_SIZE * total_of(grad[k, c, bx * BX + j].astype(jnp.float32) * vel[c, bx * BX + j] for c in range(3))

    def clear(a, first, last):
        for end, views in ((0, first), (shape[a] - 1, last)):
            @pl.when(at[a] == end)
            def _(views=views):
                for ref in views:
                    ref[...] = jnp.zeros_like(ref)

    def clear_missing():
        sides = ((slice(0, HX), slice(EX, EX + XG), slice(EX + EG, EX + EG + XG)),
                 (slice(HX + TX, EX), slice(EX + XG + G, EX + EG), slice(EX + EG + XG + G, EX + 2 * EG)))
        low, high = ([BK.at[x] for BK in (BK0, BK1) for x in side] for side in sides)
        if NS == 2:
            low, high = low + [LX.at[:, 0]], high + [LX.at[:, 1]]
        clear("gx", low + [E.at[x] for E in (E0, E1) for x in sides[0]] + [VE.at[:, 0:LH]],
              high + [E.at[x] for E in (E0, E1) for x in sides[1]] + [VE.at[:, LH + TX:]])
        for BK in (BK0, BK1):
            for x in sides[0] + sides[1]:
                BK[x, INNER, :] = jnp.zeros_like(BK[x, INNER, :])
        ends = slice(0, HY), slice(HY + TY, EY)
        low, high = ([ref.at[:, y] for ref in (E0, E1, BK0, BK1)] + [LX.at[:, :, :, y]] for y in ends)
        clear("gy", low + [YVD], high + [YVU])
        low, high = ([ref.at[x] for ref in (E0, E1, BK0, BK1)] for x in (slice(EX, EX + EG), slice(EX + EG, EX + 2 * EG)))
        clear("gz", low + [LX.at[:, :, HX, 0:TY], VRD], high + [LX.at[:, :, HX + XG, 0:TY], VRU])
        for end, L in ((0, HX), (shape["gz"] - 1, HX + XG)):
            @pl.when(jnp.logical_and(at["gz"] == end, odd))
            def _(L=L):
                LX[:, :, L, TY:, :] = jnp.zeros_like(LX[:, :, L, TY:, :])

    def send_faces():
        copies = [((1, 0, 0), vel.at[:, TX - LH:TX], VE.at[:, 0:LH, OY, :]),
                  ((-1, 0, 0), vel.at[:, 0:LH], VE.at[:, LH + TX:2 * LH + TX, OY, :])]
        for way, src, dst in copies:
            start(src, dst, way, 2 * EACH)
        VE[:, LH:LH + TX, OY, :] = vel[...]
        for c in range(3):
            for i in range(TX // 2):
                for h in range(2):
                    YSU[c, i, LH * h:LH * (h + 1), :] = vel[c, 2 * i + h, TY - LH:TY, :]
                    YSD[c, i, LH * h:LH * (h + 1), :] = vel[c, 2 * i + h, 0:LH, :]
            for g in range(TX // VPK):
                row = None
                for j in range(VPK):
                    turned = pltpu.roll(vel[c, VPK * g + j], (2 * LH * j + LH) % LANES, 1)
                    row = turned if row is None else jnp.where(lane2 // (2 * LH) == j, turned, row)
                SV[c, g] = row
        for way, src, dst in (((0, 1, 0), YSU, YVD), ((0, -1, 0), YSD, YVU),
                              ((0, 0, 1), SV, VRD), ((0, 0, -1), SV, VRU)):
            start(src, dst, way, 2 * EACH)

    def face_tiles(x, y, z):
        return (x * tiles_of(3 * LH, TY, LANES) + y * tiles_of(3 * TX // 2, 2 * LH, LANES)
                + z * tiles_of(3 * TX // VPK, TY, LANES))

    def regular():
        wait_for(recv.at[2 * EACH], face_tiles, AXES)
        for c in range(3):
            for i in range(TX // 2):
                for h in range(2):
                    VE[c, LH + 2 * i + h, HY - LH:HY, :] = YVD[c, i, LH * h:LH * (h + 1), :]
                    VE[c, LH + 2 * i + h, HY + TY:HY + TY + LH, :] = YVU[c, i, LH * h:LH * (h + 1), :]
        rows = lax.broadcasted_iota(jnp.int32, (2 * LANES, LANES), 0)
        cols = lax.broadcasted_iota(jnp.int32, (2 * LANES, LANES), 1)
        r = rows - LANES
        place = jnp.where(rows < LANES, rows, jnp.where(r < LH, r + LANES, r - LANES))
        known = jnp.logical_or(rows < LANES, jnp.logical_or(r < LH, r >= LANES - LH))
        gap = jnp.abs(place - cols)
        band = jnp.zeros((2 * LANES, LANES), jnp.float32)
        for k in range(5):
            tap = (3.0 if k == 0 else 1.0) * LAPLACE_TAPS[k]
            band = jnp.where(jnp.logical_and(known, gap == k), tap, band)
        for c in range(3):
            rims = []
            for g in range(TX // VPK):
                row = jnp.where(lane2 % (2 * LH) < LH, VRD[c, g], VRU[c, g])
                for j in range(VPK):
                    rims.append(pltpu.roll(row, (LANES - (2 * LH * j + LH)) % LANES, 1))
            rims = jnp.concatenate(rims, axis=0)
            own = vel[c].reshape(TX * TY, LANES)
            res = jnp.dot(jnp.concatenate([own, rims], axis=1), band,
                          preferred_element_type=jnp.float32,
                          precision=lax.Precision.HIGHEST).reshape(TX, TY, LANES)
            for k in range(1, 5):
                res = res + LAPLACE_TAPS[k] * (
                    VE[c, LH + k:LH + k + TX, OY, :] + VE[c, LH - k:LH - k + TX, OY, :]
                    + VE[c, LH:LH + TX, HY + k:HY + k + TY, :]
                    + VE[c, LH:LH + TX, HY - k:HY - k + TY, :])
            out[c] = (-REG_WEIGHT) * res

    met = False
    for i in reversed(range(NBX)):
        wait_for(arrive.at[i], lambda: tiles_of(3 * BX, TY, LANES) * 3 // 2, ())
        bx = column(i)
        for j in range(BX):
            E0[HX + bx * BX + j, OY, :] = product(0, bx, j)
        pack_column(E0, 0, bx)
        if not met and (i == NBX - 1 and NS == 1 or i == 0):
            pl.semaphore_wait(barrier, total)
            forward_x(E0, 0, 0)
            met = True
    for i in range(NBX):
        forward_rest(E0, 0, 0, column(i))

    clear_missing()
    send_faces()
    for copy in later:
        copy.wait()
    for i in range(NBX):
        for j in range(BX):
            E1[HX + column(i) * BX + j, OY, :] = product(1, column(i), j)
    YP[:, :, :, 0:TILE] = jnp.zeros_like(YP[:, :, :, 0:TILE])
    YP[:, :, :, TILE + BY:] = jnp.zeros_like(YP[:, :, :, TILE + BY:])
    XP[...] = jnp.zeros_like(XP)

    def enter(E, k, g, side):
        for j in range(HX):
            E[PK * g + j] = LX[k, side, j]
        unpack(LX[k, side, HX], LX[k, side, HX + XG], g)

    def forward(E, n, each):
        forward_pair(n, n)
        wait_rest(n)
        for i in range(NBX):
            g = XG + column(i)
            unpack(E[EX + g], E[EX + EG + g], g)
        for i in range(NBX):
            if i == 0:
                g = group_of(0)
                if NS == 2:
                    far_of(wait_late, n)
                    enter(E, n, g, 1 - up)
                else:
                    unpack(E[EX + g], E[EX + EG + g], g)
            if i == NBX - 1:
                near_of(wait_late, n)
                enter(E, n, group_of(EG - 1), place(up))
            each(i, column(i))

    def first(i, bx):
        for by in range(NBY):
            res = gather_block(E0, 0, bx, by)
            for m in range(BX):
                rows = slice(HY + by * BY, HY + (by + 1) * BY)
                E1[HX + bx * BX + m, rows, :] = E1[HX + bx * BX + m, rows, :] + res[m]
        pack_column(E1, 1, bx)
        if i == NBX - 1:
            forward_x(E1, 1, 1)
        forward_rest(E1, 1, 1, bx)

    forward(E0, 0, first)

    def second(i, bx):
        for by in range(NBY):
            spread_block(gather_block(E1, 1, bx, by), 1, i, bx, by)

    forward(E1, 1, second)

    def give_back(ACC, BK, k, n, meanwhile):
        collect(k, EG - 1, halo=place(up))
        if NS == 2:
            collect(k, 0, halo=1 - up)
        return_x(k, BK, n, 0)
        for q in range(XG, XG + G):
            collect(k, q, ACC)
        return_rest(ACC, BK, n)
        meanwhile()
        return_x(k, BK, n, 1)

    def backward(ACC, BK, n, each):
        wait_rest(n)
        for i in range(NBX):
            if i == 0:
                far_of(wait_back, n)
            if i == NBX - 1:
                near_of(wait_back, n)
            each(i, column(i), received(ACC, BK, i))

    give_back(ACC1, BK1, 1, 2, regular)

    def third(i, bx, layers):
        for j in range(BX):
            ADJ[bx * BX + j] = layers[j]
        for by in range(NBY):
            spread_block(blocks(layers, by), 0, i, bx, by)

    backward(ACC1, BK1, 2, third)
    def gauss():
        for c in range(3):
            out[c] = out[c] + STEP_SIZE * grad[1, c].astype(jnp.float32) * ADJ[...]

    give_back(ACC0, BK0, 0, 3, gauss)

    def fourth(i, bx, layers):
        for c in range(3):
            for j in range(BX):
                x = bx * BX + j
                out[c, x] = out[c, x] + STEP_SIZE * grad[0, c, x].astype(jnp.float32) * layers[j]

    backward(ACC0, BK0, 3, fourth)
    wait_sent()


def body(shape, velocity, gradients, shift_x, shift_y, shift_z, fractions):
    TX, TY, TZ = velocity.shape[1:]
    assert TZ == BZ == LANES and TX % VPK == 0 and TX % BX == 0 and TY % BY == 0
    assert shape["gy"] % 2 == 0 and TX // BX > 1
    assert BX == HX == PK and BY == HY == TILE and XG == 1
    EX, EY = TX + 2 * HX, TY + 2 * HY
    EG = EX // PK
    NS = 2 if shape["gx"] > 2 else 1
    NB = (TX // BX) * (TY // BY)
    most = (2 * STEPS + 1) * EX * EY * (LANES + 2 * HZ) // (TILE * LANES)

    vm = lambda *s: pltpu.VMEM(s, jnp.float32)
    vmem = pl.BlockSpec(memory_space=pltpu.VMEM)
    hbm = pl.BlockSpec(memory_space=pltpu.HBM)
    shift_x, shift_y, shift_z = (s.transpose(0, 1, 3, 2) for s in (shift_x, shift_y, shift_z))
    fractions = fractions.transpose(0, 2, 3, 4, 1)
    return pl.pallas_call(
        functools.partial(kernel, shape),
        out_shape=jax.ShapeDtypeStruct(velocity.shape, jnp.float32),
        in_specs=[hbm] * 6,
        out_specs=vmem,
        scratch_shapes=[
            pltpu.VMEM(velocity.shape, velocity.dtype), pltpu.VMEM(gradients.shape, gradients.dtype),
            *[pltpu.SMEM(s.shape, s.dtype) for s in (shift_x, shift_y, shift_z, fractions)],
            pltpu.SemaphoreType.DMA((TX // BX + 5,)),
            vm(EX + 2 * EG, EY, LANES), vm(EX + 2 * EG, EY, LANES),
            vm(2, NS, HX + 2 * XG, EY, LANES), vm(2, NS, HX + 2 * XG, EY, LANES),
            vm(2, NS, HX + 2 * XG, 2 * HY, LANES), vm(EX, EY, LANES),
            vm(NB, 2, BX + 3, 3 * TILE, LANES), vm(NB, 2, 2 * WX - BX, 5 * TILE, LANES),
            *[vm(EX + 2 * EG, EY, LANES) for _ in range(4)],
            vm(TX, TY, LANES),
            vm(2, 2, EG, EY, LANES),
            vm(3, TX + 2 * LH, EY, LANES),
            vm(3, TX // 2, 2 * LH, LANES), vm(3, TX // 2, 2 * LH, LANES),
            vm(3, TX // 2, 2 * LH, LANES), vm(3, TX // 2, 2 * LH, LANES),
            vm(3, TX // VPK, TY, LANES), vm(3, TX // VPK, TY, LANES), vm(3, TX // VPK, TY, LANES),
            vm(most, TILE, LANES),
            pltpu.SemaphoreType.DMA((1,)), pltpu.SemaphoreType.DMA((2 * (1 + 2 * NS) + 1,)),
        ],
        compiler_params=pltpu.CompilerParams(collective_id=0, has_side_effects=True,
                                             vmem_limit_bytes=24 << 20),
    )(*(pltpu.with_memory_space_constraint(x, pltpu.HBM) for x in (velocity, gradients, shift_x, shift_y, shift_z, fractions)))


def solution(mesh):
    in_specs = (
        P(None, "gx", "gy", "gz"),
        P(None, None, "gx", "gy", "gz"),
        P(None, "gx", "gy", "gz"),
        P(None, "gx", "gy", "gz"),
        P(None, "gx", "gy", "gz"),
        P(None, None, "gx", "gy", "gz"),
    )
    out_specs = P(None, "gx", "gy", "gz")
    return jax.shard_map(functools.partial(body, dict(mesh.shape)), mesh=mesh, in_specs=in_specs,
                         out_specs=out_specs, check_vma=False)
```

```python
import functools

import jax
import jax.numpy as jnp
from jax import lax
from jax.experimental import pallas as pl
from jax.experimental.pallas import tpu as pltpu
from jax.sharding import PartitionSpec as P

BX = 8
BY = 8
BZ = 128
RX = 6
RY = 6
RZ = 14
STEPS = 2

STEP_SIZE = 0.5
REG_WEIGHT = 0.1
LAPLACE_TAPS = (-205.0 / 72.0, 8.0 / 5.0, -1.0 / 5.0, 8.0 / 315.0, -1.0 / 560.0)

HX = RX + 2
HY = RY + 2
HZ = RZ + 2
LANES = 128
PK = LANES // HZ
XG = HX // PK
LH = 4
VPK = LANES // (2 * LH)
WX = BX + 2 * HX
WY = BY + 2 * HY
TILE = 8
MESH = pl.DeviceIdType.MESH
AXES = ("gx", "gy", "gz")
WAYS = sorted(((i, j, k) for i in (-1, 0, 1) for j in (-1, 0, 1) for k in (-1, 0, 1) if (i, j, k) != (0, 0, 0)),
              key=lambda d: (not d[0], sum(map(abs, d))))


def piece(way, own, halo):
    return {-1: (0, halo), 0: (halo, halo + own), 1: (halo + own, 2 * halo + own)}[way]


def border(way, own, halo):
    return {-1: (halo, 2 * halo), 0: (halo, halo + own), 1: (own, halo + own)}[way]


def kernel(shape, vel_in, grad_in, shx_in, shy_in, shz_in, frac_in, out,
           vel, grad, shx, shy, shz, frac, arrive,
           E0, E1, LX, HA, RL, U, YP, XP, ACC0, ACC1, BK0, BK1, ADJ, SP,
           VE, YSU, YSD, YVD, YVU, SV, VRD, VRU, BULK, send, recv):
    TX, TY, TZ = vel.shape[1:]
    NBX, NBY = TX // BX, TY // BY
    EX = TX + 2 * HX
    EY = TY + 2 * HY
    EG = EX // PK
    G = TX // PK
    OX = slice(HX, HX + TX)
    OY = slice(HY, HY + TY)
    NT = TY // TILE

    at = {a: lax.axis_index(a) for a in AXES}

    def has(way):
        ok = None
        for a, w in zip(AXES, way):
            if w:
                one = at[a] < shape[a] - 1 if w > 0 else at[a] > 0
                ok = one if ok is None else jnp.logical_and(ok, one)
        return ok

    def device(way):
        return {a: at[a] + w for a, w in zip(AXES, way) if w}

    up = (at["gx"] == 0).astype(jnp.int32)

    NS = 2 if shape["gx"] > 2 else 1
    even = 1 - lax.rem(at["gy"], 2)
    off = jnp.where(even == 1, at["gy"] > 0, at["gy"] < shape["gy"] - 1)

    odd = even == 0
    SEAM = pl.ds(0, 2 * HY), pl.ds(TY, 2 * HY)

    def place(h):
        return h if NS == 2 else 0

    def multiple(x):
        return pl.multiple_of(x, TILE)

    A = pl.ds(multiple(HY + even * (TY - HY)), HY)
    B = pl.ds(multiple(HY + (1 - even) * HY), TY - HY)
    OFF = pl.ds(multiple(HY + (1 - even) * (TY - HY)), HY)
    INNER = pl.ds(multiple(even * (HY + TY)), HY)
    OUTER = pl.ds(multiple((1 - even) * (HY + TY)), HY)

    def column(i):
        return i * up + (NBX - 1 - i) * (1 - up)

    def group_of(q):
        return q * up + (EG - 1 - q) * (1 - up)

    def part(ref, i):
        return ref.at[:, pl.ds(column(i) * BX, BX)]

    for i in reversed(range(NBX)):
        for src, dst in ((vel_in, vel), (grad_in.at[0], grad.at[0])):
            pltpu.make_async_copy(part(src, i), part(dst, i), arrive.at[i]).start()
    later = [pltpu.make_async_copy(a, b, arrive.at[NBX + m]) for m, (a, b) in enumerate((
        (shx_in, shx), (shy_in, shy), (shz_in, shz), (frac_in, frac), (grad_in.at[1], grad.at[1])))]
    barrier = pltpu.get_barrier_semaphore()
    total = jnp.int32(0)
    for way in WAYS:
        @pl.when(has(way))
        def _(way=way):
            pl.semaphore_signal(barrier, inc=1, device_id=device(way), device_id_type=MESH)
        total = total + has(way).astype(jnp.int32)

    def counts(a):
        if a == "even":
            return [(v, even == v) for v in range(2)]
        if a == "off":
            return [(v, off if v else jnp.logical_not(off)) for v in range(2)] if shape["gy"] > 2 else [(0, None)]
        n = (at[a] > 0).astype(jnp.int32) + (at[a] < shape[a] - 1).astype(jnp.int32)
        return [(v, n == v if shape[a] > 2 else None) for v in ((0,), (1,), (1, 2))[min(shape[a], 3) - 1]]

    def wait_for(sem, tiles, axes, also=None):
        combos = [((), also)]
        for a in axes:
            combos = [(vs + (v,), c if ok is None else ok if c is None else jnp.logical_and(c, ok))
                      for vs, c in combos for v, ok in counts(a)]
        for vs, ok in combos:
            n = tiles(*vs)
            if not n:
                continue
            wait = pltpu.make_async_copy(BULK.at[0:n], BULK.at[0:n], sem).wait
            if ok is None:
                wait()
            else:
                pl.when(ok)(wait)

    def tiles_of(x, y, z):
        return x * y * z // (TILE * LANES)

    EACH = 1 + 2 * NS
    SIDES = [] if shape["gx"] == 1 else [(up, None)] if NS == 1 else [(0, has((-1, 0, 0))), (1, has((1, 0, 0)))]

    def sem(n, kind=None, h=0):
        return EACH * (n % 2) + (0 if kind is None else 1 + kind * NS + place(h))

    def wait_rest(n):
        wait_for(recv.at[sem(n)], lambda y, z: tiles_of(TX, TY + HY * y, LANES + HZ * z) - tiles_of(TX, TY, LANES),
                 ("gy", "gz"))

    def wait_early(n, h, ok):
        wait_for(recv.at[sem(n, 0, h)], lambda z: 2 * tiles_of(HX, HY, LANES + HZ * z), ("gz",), both(ok, odd))

    def wait_late(n, h, ok):
        wait_for(recv.at[sem(n, 1, h)], lambda e, y, z: tiles_of(HX, TY - HY + HY * y, LANES + HZ * z)
                 + e * tiles_of(HX + 2 * XG, 2 * HY, LANES), ("even", "off", "gz"), ok)

    def wait_back(n, h, ok):
        wait_for(recv.at[sem(n, 0, h)], lambda y, z: tiles_of(HX, TY + HY * y, LANES + HZ * z), ("off", "gz"), ok)

    def wait_pair(n, h, ok):
        wait_for(recv.at[sem(n, 1, h)], lambda: tiles_of(HX + 2 * XG, 2 * HY, LANES), (), both(ok, odd))

    def far_of(wait, n):
        if NS == 2:
            wait(n, 1, jnp.logical_and(SIDES[1][1], up == 0))

    def near_of(wait, n):
        for h, ok in SIDES:
            wait(n, h, jnp.logical_and(ok, up == 1) if NS == 2 and h else ok)

    def wait_sent():
        def tiles(x, e, y, z):
            seam = tiles_of(HX + 2 * XG, 2 * HY, LANES)
            along = seam + tiles_of(HX, 2 * (TY + HY * y) + (-HY if e else HY), LANES + HZ * z)
            one = tiles_of(TX, TY + HY * (1 + y), LANES + HZ * z) - tiles_of(TX, TY, LANES)
            return STEPS * (2 * one + x * along) + face_tiles(x, 1 + y, z)

        wait_for(send.at[0], tiles, ("gx", "even", "off", "gz"))

    def start(src, dst, way, came):
        to_device(src, dst, device(way), has(way), came)

    def to_device(src, dst, where, ok, came):
        desc = pltpu.make_async_remote_copy(
            src_ref=src, dst_ref=dst, send_sem=send.at[0], recv_sem=recv.at[came],
            device_id=where, device_id_type=MESH)
        if ok is None:
            desc.start()
        else:
            pl.when(ok)(desc.start)

    def both(*oks):
        oks = [ok for ok in oks if ok is not None]
        return functools.reduce(jnp.logical_and, oks) if oks else None

    def beside(h, y=0, z=0):
        where = {"gx": at["gx"] + 2 * h - 1}
        if y is even:
            where["gy"] = at["gy"] + even
        elif y:
            where["gy"] = at["gy"] + (1 - 2 * even if y < 0 else 2 * even - 1)
        if z:
            where["gz"] = at["gz"] + z
        return where

    partner = {"gy": at["gy"] + 2 * even - 1}

    lane2 = lax.broadcasted_iota(jnp.int32, (1, LANES), 1)
    group = lane2 // HZ
    edge = jnp.logical_or(lane2 < HZ, lane2 >= LANES - HZ)

    def packed(layer):
        first = last = None
        for j in range(PK):
            turned = pltpu.roll(layer(j), HZ * j, 1) if j else layer(0)
            first = turned if j == 0 else jnp.where(group == j, turned, first)
            last = turned if j == 0 else jnp.where(group == j - 1, turned, last)
        return first, last

    def unpacked(first, last, j):
        both = jnp.where(group == j, first, last)
        return pltpu.roll(both, LANES - HZ * j, 1) if j else both

    def region(way, dim_of):
        (x0, x1) = dim_of(way[0], G if way[2] else TX, XG if way[2] else HX)
        (y0, y1) = dim_of(way[1], TY, HY)
        return slice(x0, x1), slice(y0, y1)

    def rim(ref, way):
        xs, ys = region(way, piece)
        base = {0: 0, -1: EX, 1: EX + EG}[way[2]]
        return ref.at[slice(base + xs.start, base + xs.stop), ys, :]

    def forward_x(E, k, n):
        for h, ok in SIDES:
            mine, g, into = pl.ds(HX + h * (TX - HX), HX), XG + h * (G - XG), LX.at[k, place(1 - h)]

            def send_rows(rows, where, y, ok, came):
                to_device(E.at[mine, rows, :], into.at[0:HX, where, :], beside(h, y), ok, came)
                for z in (-1, 1):
                    to_device(SP.at[k, (z + 1) // 2, g, rows, :], into.at[HX + (1 - z) // 2, where, :],
                              beside(h, y, z), both(ok, has((0, 0, z))), came)

            send_rows(A, pl.ds(multiple(HY * (1 - even)), HY), even, ok, sem(n, 0, 1 - h))
            send_rows(OFF, INNER, -1, both(ok, off), sem(n, 1, 1 - h))
            send_rows(B, B, 0, ok, sem(n, 1, 1 - h))

    def forward_pair(k, n):
        for h, ok in SIDES:
            wait_early(n, h, ok)
            to_device(LX.at[k, place(h), :, SEAM[0], :], LX.at[k, place(h), :, SEAM[1], :], partner, both(ok, odd),
                      sem(n, 1, h))

    def forward_rest(E, k, n, bx):
        for way in REST:
            ys, into = region(way, border)[1], region(tuple(-w for w in way), piece)[1]
            base = {0: HX, -1: EX + EG, 1: EX}[way[2]]
            if way[2]:
                src, dst = SP.at[k, (way[2] + 1) // 2, XG + bx, ys, :], E.at[base + XG + bx, into, :]
            else:
                src, dst = (E.at[pl.ds(HX + bx * BX, BX), rows, :] for rows in (ys, into))
            start(src, dst, way, sem(n))

    def return_x(k, BK, n, part):
        for h, ok in SIDES:
            mine, came = HA.at[k, place(h)], sem(n, 0, 1 - h)
            first = (1 - h) * (HX + TX)
            g = (1 - h) * (EG - 1)

            def send_rows(rows, into, y, ok):
                to_device(mine.at[0:HX, rows, :], BK.at[pl.ds(first, HX), into, :], beside(h, y), ok, came)
                for z in (-1, 1):
                    to_device(mine.at[HX + (z + 1) // 2, rows, :], BK.at[EX + EG * ((1 - z) // 2) + g, into, :],
                              beside(h, y, z), both(ok, has((0, 0, z))), came)

            if part == 0:
                to_device(mine.at[:, SEAM[1], :], RL.at[k, place(h)], partner, both(ok, even == 1), sem(n, 1, h))
                send_rows(OUTER, INNER, -1, both(ok, off))
                send_rows(B, B, 0, ok)
            else:
                wait_pair(n, h, ok)

                @pl.when(odd)
                def _(h=h):
                    for L in range(HX + 2 * XG):
                        HA[k, place(h), L, SEAM[0], :] = HA[k, place(h), L, SEAM[0], :] + RL[k, place(h), L]

                send_rows(pl.ds(0, HY), pl.ds(TY, HY), 1, both(ok, odd))
                send_rows(pl.ds(HY, HY), pl.ds(HY, HY), 0, both(ok, odd))

    def return_rest(ACC, BK, n):
        for way in REST:
            start(rim(ACC, way), rim(BK, tuple(-w for w in way)), way, sem(n))

    REST = [w for w in WAYS if not w[0]]

    def pack_column(E, k, bx):
        SP[k, 0, XG + bx, OY, :], SP[k, 1, XG + bx, OY, :] = packed(lambda j: E[HX + bx * BX + j, OY, :])

    def unpack(below, above, g):
        for j in range(PK):
            U[PK * g + j] = unpacked(above, below, j)

    def taps(k, d, bx, by):
        e = frac[k, bx, by, 0, d].astype(jnp.float32) * 0.125
        e2 = e * e
        e3 = e2 * e
        return (0.5 * (2.0 * e2 - e3 - e), 0.5 * (3.0 * e3 - 5.0 * e2 + 2.0),
                0.5 * (4.0 * e2 - 3.0 * e3 + e), 0.5 * (e3 - e2))

    def total_of(terms):
        return functools.reduce(lambda a, b: a + b, terms)

    def gather_block(E, k, bx, by):
        a, b, c = shx[k, bx, 0, by], shy[k, bx, 0, by], shz[k, bx, 0, by]
        wx, wy, wz = (taps(k, d, bx, by) for d in range(3))
        x0 = bx * BX + (a + HX - 1)
        y0 = by * BY + (b + HY - 1)
        along = []
        for ref in (E, U):
            rows = [total_of(wy[v] * ref[x0 + m, pl.ds(y0 + v, BY), :] for v in range(4)) for m in range(BX + 3)]
            along.append([total_of(wx[u] * rows[m + u] for u in range(4)) for m in range(BX)])
        own, rest = (jnp.concatenate(p, axis=0) for p in along)
        res = None
        for w in range(4):
            s = c + (w - 1)
            inside = jnp.logical_and(lane2 >= s, lane2 < LANES + s)
            term = wz[w] * pltpu.roll(jnp.where(inside, own, rest), lax.rem(LANES - s, LANES), 1)
            res = term if res is None else res + term
        return [res[BY * m:BY * (m + 1)] for m in range(BX)]

    def spread_block(vals, k, i, bx, by):
        n = i * NBY + by
        c = shz[k, bx, 0, by]
        wx, wy, wz = (taps(k, d, bx, by) for d in range(3))
        flat = jnp.concatenate(vals, axis=0)
        own = rest = None
        for w in range(4):
            s = c + (w - 1)
            inside = jnp.logical_and(lane2 >= s, lane2 < LANES + s)
            term = wz[w] * pltpu.roll(flat, lax.rem(LANES + s, LANES), 1)
            o, r = jnp.where(inside, term, 0.0), jnp.where(inside, 0.0, term)
            own, rest = (o, r) if own is None else (own + o, rest + r)
        for p, zs in enumerate((own, rest)):
            z = [zs[BY * m:BY * (m + 1)] for m in range(BX)]
            for m in range(BX + 3):
                YP[n, p, m, TILE:TILE + BY, :] = total_of(wx[u] * z[m - u] for u in range(4) if 0 <= m - u < BX)
            for m in range(BX + 3):
                XP[n, p, 2 * HX + m, 2 * TILE:2 * TILE + 2 * BY, :] = total_of(
                    wy[v] * YP[n, p, m, TILE - v:TILE - v + 2 * BY, :] for v in range(4))

    def collect(k, q, ACC=None, halo=None):
        g = group_of(q)
        found = []
        for i in range(NBX):
            if 0 <= q - i <= 2:
                bx = column(i)
                offset = BX * ((q - i) * up + (2 - q + i) * (1 - up))
                for by in range(NBY):
                    found.append((i * NBY + by, by, (HX + 1) - shx[k, bx, 0, by] + offset,
                                  (2 * TILE - HY + 1) - shy[k, bx, 0, by]))

        def layer(p, j):
            tiles = [None] * (EY // TILE)
            for n, by, x0, y0 in found:
                rows = XP[n, p, x0 + j, pl.ds(y0, WY), :]
                for r in range(WY // TILE):
                    one = rows[r * TILE:(r + 1) * TILE]
                    old = tiles[by + r]
                    tiles[by + r] = one if old is None else old + one
            return jnp.concatenate(tiles, axis=0)

        rims = [layer(1, j) for j in range(PK)]
        above, below = packed(lambda j: rims[j])
        for j in range(PK):
            if halo is not None:
                HA[k, halo, j] = layer(0, j)
            else:
                ACC[PK * g + j] = layer(0, j)
        if halo is not None:
            HA[k, halo, HX], HA[k, halo, HX + XG] = below, above
        else:
            ACC[EX + EG + g], ACC[EX + g] = above, below

    def received(ACC, BK, i):
        bx = column(i)
        halos = ([0] if i == 0 and NS == 2 else []) + ([EG - 1] if i == NBX - 1 else [])
        halos = [group_of(q) for q in halos]

        def rows(center, L):
            tiles = [center[L, HY + TILE * t:HY + TILE * (t + 1), :] for t in range(NT)]
            tiles[0] = tiles[0] + BK[L, 0:HY, :]
            tiles[-1] = tiles[-1] + BK[L, HY + TY:, :]
            return jnp.concatenate(tiles, axis=0)

        rims = []
        for base in (EX, EX + EG):
            rims.append(total_of([rows(BK, base + XG + bx)] + [rows(BK, base + g) for g in halos]))
        first, last = rims
        res = []
        for j in range(BX):
            one = total_of([rows(ACC, HX + bx * BX + j)] + [rows(BK, PK * g + j) for g in halos])
            res.append(one + jnp.where(edge, unpacked(first, last, j), 0.0))
        return res

    def blocks(layers, by):
        return [one[by * BY:(by + 1) * BY] for one in layers]

    def product(k, bx, j):
        return STEP_SIZE * total_of(grad[k, c, bx * BX + j].astype(jnp.float32) * vel[c, bx * BX + j] for c in range(3))

    def clear(a, first, last):
        for end, views in ((0, first), (shape[a] - 1, last)):
            @pl.when(at[a] == end)
            def _(views=views):
                for ref in views:
                    ref[...] = jnp.zeros_like(ref)

    def clear_missing():
        sides = ((slice(0, HX), slice(EX, EX + XG), slice(EX + EG, EX + EG + XG)),
                 (slice(HX + TX, EX), slice(EX + XG + G, EX + EG), slice(EX + EG + XG + G, EX + 2 * EG)))
        low, high = ([BK.at[x] for BK in (BK0, BK1) for x in side] for side in sides)
        if NS == 2:
            low, high = low + [LX.at[:, 0]], high + [LX.at[:, 1]]
        clear("gx", low + [E.at[x] for E in (E0, E1) for x in sides[0]] + [VE.at[:, 0:LH]],
              high + [E.at[x] for E in (E0, E1) for x in sides[1]] + [VE.at[:, LH + TX:]])
        for BK in (BK0, BK1):
            for x in sides[0] + sides[1]:
                BK[x, INNER, :] = jnp.zeros_like(BK[x, INNER, :])
        ends = slice(0, HY), slice(HY + TY, EY)
        low, high = ([ref.at[:, y] for ref in (E0, E1, BK0, BK1)] + [LX.at[:, :, :, y]] for y in ends)
        clear("gy", low + [YVD], high + [YVU])
        low, high = ([ref.at[x] for ref in (E0, E1, BK0, BK1)] for x in (slice(EX, EX + EG), slice(EX + EG, EX + 2 * EG)))
        clear("gz", low + [LX.at[:, :, HX, 0:TY], VRD], high + [LX.at[:, :, HX + XG, 0:TY], VRU])
        for end, L in ((0, HX), (shape["gz"] - 1, HX + XG)):
            @pl.when(jnp.logical_and(at["gz"] == end, odd))
            def _(L=L):
                LX[:, :, L, TY:, :] = jnp.zeros_like(LX[:, :, L, TY:, :])

    def send_faces():
        copies = [((1, 0, 0), vel.at[:, TX - LH:TX], VE.at[:, 0:LH, OY, :]),
                  ((-1, 0, 0), vel.at[:, 0:LH], VE.at[:, LH + TX:2 * LH + TX, OY, :])]
        for way, src, dst in copies:
            start(src, dst, way, 2 * EACH)
        VE[:, LH:LH + TX, OY, :] = vel[...]
        for c in range(3):
            for i in range(TX // 2):
                for h in range(2):
                    YSU[c, i, LH * h:LH * (h + 1), :] = vel[c, 2 * i + h, TY - LH:TY, :]
                    YSD[c, i, LH * h:LH * (h + 1), :] = vel[c, 2 * i + h, 0:LH, :]
            for g in range(TX // VPK):
                row = None
                for j in range(VPK):
                    turned = pltpu.roll(vel[c, VPK * g + j], (2 * LH * j + LH) % LANES, 1)
                    row = turned if row is None else jnp.where(lane2 // (2 * LH) == j, turned, row)
                SV[c, g] = row
        for way, src, dst in (((0, 1, 0), YSU, YVD), ((0, -1, 0), YSD, YVU),
                              ((0, 0, 1), SV, VRD), ((0, 0, -1), SV, VRU)):
            start(src, dst, way, 2 * EACH)

    def face_tiles(x, y, z):
        return (x * tiles_of(3 * LH, TY, LANES) + y * tiles_of(3 * TX // 2, 2 * LH, LANES)
                + z * tiles_of(3 * TX // VPK, TY, LANES))

    def regular():
        wait_for(recv.at[2 * EACH], face_tiles, AXES)
        for c in range(3):
            for i in range(TX // 2):
                for h in range(2):
                    VE[c, LH + 2 * i + h, HY - LH:HY, :] = YVD[c, i, LH * h:LH * (h + 1), :]
                    VE[c, LH + 2 * i + h, HY + TY:HY + TY + LH, :] = YVU[c, i, LH * h:LH * (h + 1), :]
        rows = lax.broadcasted_iota(jnp.int32, (2 * LANES, LANES), 0)
        cols = lax.broadcasted_iota(jnp.int32, (2 * LANES, LANES), 1)
        r = rows - LANES
        place = jnp.where(rows < LANES, rows, jnp.where(r < LH, r + LANES, r - LANES))
        known = jnp.logical_or(rows < LANES, jnp.logical_or(r < LH, r >= LANES - LH))
        gap = jnp.abs(place - cols)
        band = jnp.zeros((2 * LANES, LANES), jnp.float32)
        for k in range(5):
            tap = (3.0 if k == 0 else 1.0) * LAPLACE_TAPS[k]
            band = jnp.where(jnp.logical_and(known, gap == k), tap, band)
        for c in range(3):
            rims = []
            for g in range(TX // VPK):
                row = jnp.where(lane2 % (2 * LH) < LH, VRD[c, g], VRU[c, g])
                for j in range(VPK):
                    rims.append(pltpu.roll(row, (LANES - (2 * LH * j + LH)) % LANES, 1))
            rims = jnp.concatenate(rims, axis=0)
            own = vel[c].reshape(TX * TY, LANES)
            res = jnp.dot(jnp.concatenate([own, rims], axis=1), band,
                          preferred_element_type=jnp.float32,
                          precision=lax.Precision.HIGHEST).reshape(TX, TY, LANES)
            for k in range(1, 5):
                res = res + LAPLACE_TAPS[k] * (
                    VE[c, LH + k:LH + k + TX, OY, :] + VE[c, LH - k:LH - k + TX, OY, :]
                    + VE[c, LH:LH + TX, HY + k:HY + k + TY, :]
                    + VE[c, LH:LH + TX, HY - k:HY - k + TY, :])
            out[c] = (-REG_WEIGHT) * res

    met = False
    for i in reversed(range(NBX)):
        wait_for(arrive.at[i], lambda: tiles_of(3 * BX, TY, LANES) * 3 // 2, ())
        if i == NBX - 1:
            for copy in later:
                copy.start()
        bx = column(i)
        for j in range(BX):
            E0[HX + bx * BX + j, OY, :] = product(0, bx, j)
        pack_column(E0, 0, bx)
        if not met and (i == NBX - 1 and NS == 1 or i == 0):
            pl.semaphore_wait(barrier, total)
            forward_x(E0, 0, 0)
            met = True
    for i in range(NBX):
        forward_rest(E0, 0, 0, column(i))

    clear_missing()
    send_faces()
    for copy in later:
        copy.wait()
    for i in range(NBX):
        for j in range(BX):
            E1[HX + column(i) * BX + j, OY, :] = product(1, column(i), j)
    YP[:, :, :, 0:TILE] = jnp.zeros_like(YP[:, :, :, 0:TILE])
    YP[:, :, :, TILE + BY:] = jnp.zeros_like(YP[:, :, :, TILE + BY:])
    XP[...] = jnp.zeros_like(XP)

    def enter(E, k, g, side):
        for j in range(HX):
            E[PK * g + j] = LX[k, side, j]
        unpack(LX[k, side, HX], LX[k, side, HX + XG], g)

    def forward(E, n, each):
        forward_pair(n, n)
        wait_rest(n)
        for i in range(NBX):
            g = XG + column(i)
            unpack(E[EX + g], E[EX + EG + g], g)
        for i in range(NBX):
            if i == 0:
                g = group_of(0)
                if NS == 2:
                    far_of(wait_late, n)
                    enter(E, n, g, 1 - up)
                else:
                    unpack(E[EX + g], E[EX + EG + g], g)
            if i == NBX - 1:
                near_of(wait_late, n)
                enter(E, n, group_of(EG - 1), place(up))
            each(i, column(i))

    def first(i, bx):
        for by in range(NBY):
            res = gather_block(E0, 0, bx, by)
            for m in range(BX):
                rows = slice(HY + by * BY, HY + (by + 1) * BY)
                E1[HX + bx * BX + m, rows, :] = E1[HX + bx * BX + m, rows, :] + res[m]
        pack_column(E1, 1, bx)
        if i == NBX - 1:
            forward_x(E1, 1, 1)
        forward_rest(E1, 1, 1, bx)

    forward(E0, 0, first)

    def second(i, bx):
        for by in range(NBY):
            spread_block(gather_block(E1, 1, bx, by), 1, i, bx, by)

    forward(E1, 1, second)

    def give_back(ACC, BK, k, n):
        collect(k, EG - 1, halo=place(up))
        if NS == 2:
            collect(k, 0, halo=1 - up)
        return_x(k, BK, n, 0)
        for q in range(XG, XG + G):
            collect(k, q, ACC)
        return_rest(ACC, BK, n)
        return_x(k, BK, n, 1)

    def backward(ACC, BK, n, each):
        wait_rest(n)
        for i in range(NBX):
            if i == 0:
                far_of(wait_back, n)
            if i == NBX - 1:
                near_of(wait_back, n)
            each(i, column(i), received(ACC, BK, i))

    give_back(ACC1, BK1, 1, 2)
    regular()

    def third(i, bx, layers):
        for j in range(BX):
            ADJ[bx * BX + j] = layers[j]
        for by in range(NBY):
            spread_block(blocks(layers, by), 0, i, bx, by)

    backward(ACC1, BK1, 2, third)
    def gauss():
        for c in range(3):
            out[c] = out[c] + STEP_SIZE * grad[1, c].astype(jnp.float32) * ADJ[...]

    give_back(ACC0, BK0, 0, 3)
    gauss()

    def fourth(i, bx, layers):
        for c in range(3):
            for j in range(BX):
                x = bx * BX + j
                out[c, x] = out[c, x] + STEP_SIZE * grad[0, c, x].astype(jnp.float32) * layers[j]

    backward(ACC0, BK0, 3, fourth)
    wait_sent()


def body(shape, velocity, gradients, shift_x, shift_y, shift_z, fractions):
    TX, TY, TZ = velocity.shape[1:]
    assert TZ == BZ == LANES and TX % VPK == 0 and TX % BX == 0 and TY % BY == 0
    assert shape["gy"] % 2 == 0 and TX // BX > 1
    assert BX == HX == PK and BY == HY == TILE and XG == 1
    EX, EY = TX + 2 * HX, TY + 2 * HY
    EG = EX // PK
    NS = 2 if shape["gx"] > 2 else 1
    NB = (TX // BX) * (TY // BY)
    most = (2 * STEPS + 1) * EX * EY * (LANES + 2 * HZ) // (TILE * LANES)

    vm = lambda *s: pltpu.VMEM(s, jnp.float32)
    vmem = pl.BlockSpec(memory_space=pltpu.VMEM)
    hbm = pl.BlockSpec(memory_space=pltpu.HBM)
    shift_x, shift_y, shift_z = (s.transpose(0, 1, 3, 2) for s in (shift_x, shift_y, shift_z))
    fractions = fractions.transpose(0, 2, 3, 4, 1)
    return pl.pallas_call(
        functools.partial(kernel, shape),
        out_shape=jax.ShapeDtypeStruct(velocity.shape, jnp.float32),
        in_specs=[hbm] * 6,
        out_specs=vmem,
        scratch_shapes=[
            pltpu.VMEM(velocity.shape, velocity.dtype), pltpu.VMEM(gradients.shape, gradients.dtype),
            *[pltpu.SMEM(s.shape, s.dtype) for s in (shift_x, shift_y, shift_z, fractions)],
            pltpu.SemaphoreType.DMA((TX // BX + 5,)),
            vm(EX + 2 * EG, EY, LANES), vm(EX + 2 * EG, EY, LANES),
            vm(2, NS, HX + 2 * XG, EY, LANES), vm(2, NS, HX + 2 * XG, EY, LANES),
            vm(2, NS, HX + 2 * XG, 2 * HY, LANES), vm(EX, EY, LANES),
            vm(NB, 2, BX + 3, 3 * TILE, LANES), vm(NB, 2, 2 * WX - BX, 5 * TILE, LANES),
            *[vm(EX + 2 * EG, EY, LANES) for _ in range(4)],
            vm(TX, TY, LANES),
            vm(2, 2, EG, EY, LANES),
            vm(3, TX + 2 * LH, EY, LANES),
            vm(3, TX // 2, 2 * LH, LANES), vm(3, TX // 2, 2 * LH, LANES),
            vm(3, TX // 2, 2 * LH, LANES), vm(3, TX // 2, 2 * LH, LANES),
            vm(3, TX // VPK, TY, LANES), vm(3, TX // VPK, TY, LANES), vm(3, TX // VPK, TY, LANES),
            vm(most, TILE, LANES),
            pltpu.SemaphoreType.DMA((1,)), pltpu.SemaphoreType.DMA((2 * (1 + 2 * NS) + 1,)),
        ],
        compiler_params=pltpu.CompilerParams(collective_id=0, has_side_effects=True,
                                             vmem_limit_bytes=24 << 20),
    )(*(pltpu.with_memory_space_constraint(x, pltpu.HBM) for x in (velocity, gradients, shift_x, shift_y, shift_z, fractions)))


def solution(mesh):
    in_specs = (
        P(None, "gx", "gy", "gz"),
        P(None, None, "gx", "gy", "gz"),
        P(None, "gx", "gy", "gz"),
        P(None, "gx", "gy", "gz"),
        P(None, "gx", "gy", "gz"),
        P(None, None, "gx", "gy", "gz"),
    )
    out_specs = P(None, "gx", "gy", "gz")
    return jax.shard_map(functools.partial(body, dict(mesh.shape)), mesh=mesh, in_specs=in_specs,
                         out_specs=out_specs, check_vma=False)
```

```python
import functools

import jax
import jax.numpy as jnp
from jax import lax
from jax.experimental import pallas as pl
from jax.experimental.pallas import tpu as pltpu
from jax.sharding import PartitionSpec as P

BX = 8
BY = 8
BZ = 128
RX = 6
RY = 6
RZ = 14
STEPS = 2

STEP_SIZE = 0.5
REG_WEIGHT = 0.1
LAPLACE_TAPS = (-205.0 / 72.0, 8.0 / 5.0, -1.0 / 5.0, 8.0 / 315.0, -1.0 / 560.0)

HX = RX + 2
HY = RY + 2
HZ = RZ + 2
LANES = 128
PK = LANES // HZ
XG = HX // PK
LH = 4
VPK = LANES // (2 * LH)
WX = BX + 2 * HX
WY = BY + 2 * HY
TILE = 8
MESH = pl.DeviceIdType.MESH
AXES = ("gx", "gy", "gz")
WAYS = sorted(((i, j, k) for i in (-1, 0, 1) for j in (-1, 0, 1) for k in (-1, 0, 1) if (i, j, k) != (0, 0, 0)),
              key=lambda d: (not d[0], sum(map(abs, d))))


def piece(way, own, halo):
    return {-1: (0, halo), 0: (halo, halo + own), 1: (halo + own, 2 * halo + own)}[way]


def border(way, own, halo):
    return {-1: (halo, 2 * halo), 0: (halo, halo + own), 1: (own, halo + own)}[way]


def kernel(shape, vel_in, grad_in, shx_in, shy_in, shz_in, frac_in, out,
           vel, grad, shx, shy, shz, frac, arrive,
           E0, E1, LX, HA, RL, U, YP, XP, ACC0, ACC1, BK0, BK1, ADJ, SP,
           VE, YSU, YSD, YVD, YVU, SV, VRD, VRU, BULK, send, recv):
    TX, TY, TZ = vel.shape[1:]
    NBX, NBY = TX // BX, TY // BY
    EX = TX + 2 * HX
    EY = TY + 2 * HY
    EG = EX // PK
    G = TX // PK
    OX = slice(HX, HX + TX)
    OY = slice(HY, HY + TY)
    NT = TY // TILE

    at = {a: lax.axis_index(a) for a in AXES}

    def has(way):
        ok = None
        for a, w in zip(AXES, way):
            if w:
                one = at[a] < shape[a] - 1 if w > 0 else at[a] > 0
                ok = one if ok is None else jnp.logical_and(ok, one)
        return ok

    def device(way):
        return {a: at[a] + w for a, w in zip(AXES, way) if w}

    up = (at["gx"] == 0).astype(jnp.int32)

    NS = 2 if shape["gx"] > 2 else 1
    even = 1 - lax.rem(at["gy"], 2)
    off = jnp.where(even == 1, at["gy"] > 0, at["gy"] < shape["gy"] - 1)

    odd = even == 0
    SEAM = pl.ds(0, 2 * HY), pl.ds(TY, 2 * HY)

    def place(h):
        return h if NS == 2 else 0

    def multiple(x):
        return pl.multiple_of(x, TILE)

    A = pl.ds(multiple(HY + even * (TY - HY)), HY)
    B = pl.ds(multiple(HY + (1 - even) * HY), TY - HY)
    OFF = pl.ds(multiple(HY + (1 - even) * (TY - HY)), HY)
    INNER = pl.ds(multiple(even * (HY + TY)), HY)
    OUTER = pl.ds(multiple((1 - even) * (HY + TY)), HY)

    def column(i):
        return i * up + (NBX - 1 - i) * (1 - up)

    def group_of(q):
        return q * up + (EG - 1 - q) * (1 - up)

    def part(ref, i):
        return ref.at[:, pl.ds(column(i) * BX, BX)]

    for i in reversed(range(NBX)):
        for src, dst in ((vel_in, vel), (grad_in.at[0], grad.at[0])):
            pltpu.make_async_copy(part(src, i), part(dst, i), arrive.at[i]).start()
    later = [pltpu.make_async_copy(a, b, arrive.at[NBX + m]) for m, (a, b) in enumerate((
        (shx_in, shx), (shy_in, shy), (shz_in, shz), (frac_in, frac), (grad_in.at[1], grad.at[1])))]
    barrier = pltpu.get_barrier_semaphore()
    total = jnp.int32(0)
    for way in WAYS:
        @pl.when(has(way))
        def _(way=way):
            pl.semaphore_signal(barrier, inc=1, device_id=device(way), device_id_type=MESH)
        total = total + has(way).astype(jnp.int32)

    def counts(a):
        if a == "even":
            return [(v, even == v) for v in range(2)]
        if a == "off":
            return [(v, off if v else jnp.logical_not(off)) for v in range(2)] if shape["gy"] > 2 else [(0, None)]
        n = (at[a] > 0).astype(jnp.int32) + (at[a] < shape[a] - 1).astype(jnp.int32)
        return [(v, n == v if shape[a] > 2 else None) for v in ((0,), (1,), (1, 2))[min(shape[a], 3) - 1]]

    def wait_for(sem, tiles, axes, also=None):
        combos = [((), also)]
        for a in axes:
            combos = [(vs + (v,), c if ok is None else ok if c is None else jnp.logical_and(c, ok))
                      for vs, c in combos for v, ok in counts(a)]
        for vs, ok in combos:
            n = tiles(*vs)
            if not n:
                continue
            wait = pltpu.make_async_copy(BULK.at[0:n], BULK.at[0:n], sem).wait
            if ok is None:
                wait()
            else:
                pl.when(ok)(wait)

    def tiles_of(x, y, z):
        return x * y * z // (TILE * LANES)

    EACH = 1 + 2 * NS
    SIDES = [] if shape["gx"] == 1 else [(up, None)] if NS == 1 else [(0, has((-1, 0, 0))), (1, has((1, 0, 0)))]

    def sem(n, kind=None, h=0):
        return EACH * (n % 2) + (0 if kind is None else 1 + kind * NS + place(h))

    def wait_rest(n):
        wait_for(recv.at[sem(n)], lambda y, z: tiles_of(TX, TY + HY * y, LANES + HZ * z) - tiles_of(TX, TY, LANES),
                 ("gy", "gz"))

    def wait_early(n, h, ok):
        wait_for(recv.at[sem(n, 0, h)], lambda z: 2 * tiles_of(HX, HY, LANES + HZ * z), ("gz",), both(ok, odd))

    def wait_late(n, h, ok):
        wait_for(recv.at[sem(n, 1, h)], lambda e, y, z: tiles_of(HX, TY - HY + HY * y, LANES + HZ * z)
                 + e * tiles_of(HX + 2 * XG, 2 * HY, LANES), ("even", "off", "gz"), ok)

    def wait_back(n, h, ok):
        wait_for(recv.at[sem(n, 0, h)], lambda y, z: tiles_of(HX, TY + HY * y, LANES + HZ * z), ("off", "gz"), ok)

    def wait_pair(n, h, ok):
        wait_for(recv.at[sem(n, 1, h)], lambda: tiles_of(HX + 2 * XG, 2 * HY, LANES), (), both(ok, odd))

    def far_of(wait, n):
        if NS == 2:
            wait(n, 1, jnp.logical_and(SIDES[1][1], up == 0))

    def near_of(wait, n):
        for h, ok in SIDES:
            wait(n, h, jnp.logical_and(ok, up == 1) if NS == 2 and h else ok)

    def wait_sent():
        def tiles(x, e, y, z):
            seam = tiles_of(HX + 2 * XG, 2 * HY, LANES)
            along = seam + tiles_of(HX, 2 * (TY + HY * y) + (-HY if e else HY), LANES + HZ * z)
            one = tiles_of(TX, TY + HY * (1 + y), LANES + HZ * z) - tiles_of(TX, TY, LANES)
            return STEPS * (2 * one + x * along) + face_tiles(x, 1 + y, z)

        wait_for(send.at[0], tiles, ("gx", "even", "off", "gz"))

    def start(src, dst, way, came):
        to_device(src, dst, device(way), has(way), came)

    def to_device(src, dst, where, ok, came):
        desc = pltpu.make_async_remote_copy(
            src_ref=src, dst_ref=dst, send_sem=send.at[0], recv_sem=recv.at[came],
            device_id=where, device_id_type=MESH)
        if ok is None:
            desc.start()
        else:
            pl.when(ok)(desc.start)

    def both(*oks):
        oks = [ok for ok in oks if ok is not None]
        return functools.reduce(jnp.logical_and, oks) if oks else None

    def beside(h, y=0, z=0):
        where = {"gx": at["gx"] + 2 * h - 1}
        if y is even:
            where["gy"] = at["gy"] + even
        elif y:
            where["gy"] = at["gy"] + (1 - 2 * even if y < 0 else 2 * even - 1)
        if z:
            where["gz"] = at["gz"] + z
        return where

    partner = {"gy": at["gy"] + 2 * even - 1}

    lane2 = lax.broadcasted_iota(jnp.int32, (1, LANES), 1)
    group = lane2 // HZ
    edge = jnp.logical_or(lane2 < HZ, lane2 >= LANES - HZ)

    def packed(layer):
        first = last = None
        for j in range(PK):
            turned = pltpu.roll(layer(j), HZ * j, 1) if j else layer(0)
            first = turned if j == 0 else jnp.where(group == j, turned, first)
            last = turned if j == 0 else jnp.where(group == j - 1, turned, last)
        return first, last

    def unpacked(first, last, j):
        both = jnp.where(group == j, first, last)
        return pltpu.roll(both, LANES - HZ * j, 1) if j else both

    def region(way, dim_of):
        (x0, x1) = dim_of(way[0], G if way[2] else TX, XG if way[2] else HX)
        (y0, y1) = dim_of(way[1], TY, HY)
        return slice(x0, x1), slice(y0, y1)

    def rim(ref, way):
        xs, ys = region(way, piece)
        base = {0: 0, -1: EX, 1: EX + EG}[way[2]]
        return ref.at[slice(base + xs.start, base + xs.stop), ys, :]

    def forward_x(E, k, n, part):
        for h, ok in SIDES:
            mine, g, into = pl.ds(HX + h * (TX - HX), HX), XG + h * (G - XG), LX.at[k, place(1 - h)]

            def send_rows(rows, where, y, ok, came, parts=(0, 1)):
                if 0 in parts:
                    to_device(E.at[mine, rows, :], into.at[0:HX, where, :], beside(h, y), ok, came)
                if 1 not in parts:
                    return
                for z in (-1, 1):
                    to_device(SP.at[k, (z + 1) // 2, g, rows, :], into.at[HX + (1 - z) // 2, where, :],
                              beside(h, y, z), both(ok, has((0, 0, z))), came)

            send_rows(A, pl.ds(multiple(HY * (1 - even)), HY), even, ok, sem(n, 0, 1 - h), (part,))
            if part == 0:
                continue
            send_rows(OFF, INNER, -1, both(ok, off), sem(n, 1, 1 - h))
            send_rows(B, B, 0, ok, sem(n, 1, 1 - h))

    def forward_pair(k, n):
        for h, ok in SIDES:
            wait_early(n, h, ok)
            to_device(LX.at[k, place(h), :, SEAM[0], :], LX.at[k, place(h), :, SEAM[1], :], partner, both(ok, odd),
                      sem(n, 1, h))

    def forward_rest(E, k, n, bx):
        for way in REST:
            ys, into = region(way, border)[1], region(tuple(-w for w in way), piece)[1]
            base = {0: HX, -1: EX + EG, 1: EX}[way[2]]
            if way[2]:
                src, dst = SP.at[k, (way[2] + 1) // 2, XG + bx, ys, :], E.at[base + XG + bx, into, :]
            else:
                src, dst = (E.at[pl.ds(HX + bx * BX, BX), rows, :] for rows in (ys, into))
            start(src, dst, way, sem(n))

    def return_x(k, BK, n, part):
        for h, ok in SIDES:
            mine, came = HA.at[k, place(h)], sem(n, 0, 1 - h)
            first = (1 - h) * (HX + TX)
            g = (1 - h) * (EG - 1)

            def send_rows(rows, into, y, ok):
                to_device(mine.at[0:HX, rows, :], BK.at[pl.ds(first, HX), into, :], beside(h, y), ok, came)
                for z in (-1, 1):
                    to_device(mine.at[HX + (z + 1) // 2, rows, :], BK.at[EX + EG * ((1 - z) // 2) + g, into, :],
                              beside(h, y, z), both(ok, has((0, 0, z))), came)

            if part == 0:
                to_device(mine.at[:, SEAM[1], :], RL.at[k, place(h)], partner, both(ok, even == 1), sem(n, 1, h))
                send_rows(OUTER, INNER, -1, both(ok, off))
                send_rows(B, B, 0, ok)
            else:
                wait_pair(n, h, ok)

                @pl.when(odd)
                def _(h=h):
                    for L in range(HX + 2 * XG):
                        HA[k, place(h), L, SEAM[0], :] = HA[k, place(h), L, SEAM[0], :] + RL[k, place(h), L]

                send_rows(pl.ds(0, HY), pl.ds(TY, HY), 1, both(ok, odd))
                send_rows(pl.ds(HY, HY), pl.ds(HY, HY), 0, both(ok, odd))

    def return_rest(ACC, BK, n):
        for way in REST:
            start(rim(ACC, way), rim(BK, tuple(-w for w in way)), way, sem(n))

    REST = [w for w in WAYS if not w[0]]

    def pack_column(E, k, bx):
        SP[k, 0, XG + bx, OY, :], SP[k, 1, XG + bx, OY, :] = packed(lambda j: E[HX + bx * BX + j, OY, :])

    def unpack(below, above, g):
        for j in range(PK):
            U[PK * g + j] = unpacked(above, below, j)

    def taps(k, d, bx, by):
        e = frac[k, bx, by, 0, d].astype(jnp.float32) * 0.125
        e2 = e * e
        e3 = e2 * e
        return (0.5 * (2.0 * e2 - e3 - e), 0.5 * (3.0 * e3 - 5.0 * e2 + 2.0),
                0.5 * (4.0 * e2 - 3.0 * e3 + e), 0.5 * (e3 - e2))

    def total_of(terms):
        return functools.reduce(lambda a, b: a + b, terms)

    def gather_block(E, k, bx, by):
        a, b, c = shx[k, bx, 0, by], shy[k, bx, 0, by], shz[k, bx, 0, by]
        wx, wy, wz = (taps(k, d, bx, by) for d in range(3))
        x0 = bx * BX + (a + HX - 1)
        y0 = by * BY + (b + HY - 1)
        along = []
        for ref in (E, U):
            rows = [total_of(wy[v] * ref[x0 + m, pl.ds(y0 + v, BY), :] for v in range(4)) for m in range(BX + 3)]
            along.append([total_of(wx[u] * rows[m + u] for u in range(4)) for m in range(BX)])
        own, rest = (jnp.concatenate(p, axis=0) for p in along)
        res = None
        for w in range(4):
            s = c + (w - 1)
            inside = jnp.logical_and(lane2 >= s, lane2 < LANES + s)
            term = wz[w] * pltpu.roll(jnp.where(inside, own, rest), lax.rem(LANES - s, LANES), 1)
            res = term if res is None else res + term
        return [res[BY * m:BY * (m + 1)] for m in range(BX)]

    def spread_block(vals, k, i, bx, by):
        n = i * NBY + by
        c = shz[k, bx, 0, by]
        wx, wy, wz = (taps(k, d, bx, by) for d in range(3))
        flat = jnp.concatenate(vals, axis=0)
        own = rest = None
        for w in range(4):
            s = c + (w - 1)
            inside = jnp.logical_and(lane2 >= s, lane2 < LANES + s)
            term = wz[w] * pltpu.roll(flat, lax.rem(LANES + s, LANES), 1)
            o, r = jnp.where(inside, term, 0.0), jnp.where(inside, 0.0, term)
            own, rest = (o, r) if own is None else (own + o, rest + r)
        for p, zs in enumerate((own, rest)):
            z = [zs[BY * m:BY * (m + 1)] for m in range(BX)]
            for m in range(BX + 3):
                YP[n, p, m, TILE:TILE + BY, :] = total_of(wx[u] * z[m - u] for u in range(4) if 0 <= m - u < BX)
            for m in range(BX + 3):
                XP[n, p, 2 * HX + m, 2 * TILE:2 * TILE + 2 * BY, :] = total_of(
                    wy[v] * YP[n, p, m, TILE - v:TILE - v + 2 * BY, :] for v in range(4))

    def collect(k, q, ACC=None, halo=None):
        g = group_of(q)
        found = []
        for i in range(NBX):
            if 0 <= q - i <= 2:
                bx = column(i)
                offset = BX * ((q - i) * up + (2 - q + i) * (1 - up))
                for by in range(NBY):
                    found.append((i * NBY + by, by, (HX + 1) - shx[k, bx, 0, by] + offset,
                                  (2 * TILE - HY + 1) - shy[k, bx, 0, by]))

        def layer(p, j):
            tiles = [None] * (EY // TILE)
            for n, by, x0, y0 in found:
                rows = XP[n, p, x0 + j, pl.ds(y0, WY), :]
                for r in range(WY // TILE):
                    one = rows[r * TILE:(r + 1) * TILE]
                    old = tiles[by + r]
                    tiles[by + r] = one if old is None else old + one
            return jnp.concatenate(tiles, axis=0)

        rims = [layer(1, j) for j in range(PK)]
        above, below = packed(lambda j: rims[j])
        for j in range(PK):
            if halo is not None:
                HA[k, halo, j] = layer(0, j)
            else:
                ACC[PK * g + j] = layer(0, j)
        if halo is not None:
            HA[k, halo, HX], HA[k, halo, HX + XG] = below, above
        else:
            ACC[EX + EG + g], ACC[EX + g] = above, below

    def received(ACC, BK, i):
        bx = column(i)
        halos = ([0] if i == 0 and NS == 2 else []) + ([EG - 1] if i == NBX - 1 else [])
        halos = [group_of(q) for q in halos]

        def rows(center, L):
            tiles = [center[L, HY + TILE * t:HY + TILE * (t + 1), :] for t in range(NT)]
            tiles[0] = tiles[0] + BK[L, 0:HY, :]
            tiles[-1] = tiles[-1] + BK[L, HY + TY:, :]
            return jnp.concatenate(tiles, axis=0)

        rims = []
        for base in (EX, EX + EG):
            rims.append(total_of([rows(BK, base + XG + bx)] + [rows(BK, base + g) for g in halos]))
        first, last = rims
        res = []
        for j in range(BX):
            one = total_of([rows(ACC, HX + bx * BX + j)] + [rows(BK, PK * g + j) for g in halos])
            res.append(one + jnp.where(edge, unpacked(first, last, j), 0.0))
        return res

    def blocks(layers, by):
        return [one[by * BY:(by + 1) * BY] for one in layers]

    def product(k, bx, j):
        return STEP_SIZE * total_of(grad[k, c, bx * BX + j].astype(jnp.float32) * vel[c, bx * BX + j] for c in range(3))

    def clear(a, first, last):
        for end, views in ((0, first), (shape[a] - 1, last)):
            @pl.when(at[a] == end)
            def _(views=views):
                for ref in views:
                    ref[...] = jnp.zeros_like(ref)

    def clear_missing():
        sides = ((slice(0, HX), slice(EX, EX + XG), slice(EX + EG, EX + EG + XG)),
                 (slice(HX + TX, EX), slice(EX + XG + G, EX + EG), slice(EX + EG + XG + G, EX + 2 * EG)))
        low, high = ([BK.at[x] for BK in (BK0, BK1) for x in side] for side in sides)
        if NS == 2:
            low, high = low + [LX.at[:, 0]], high + [LX.at[:, 1]]
        clear("gx", low + [E.at[x] for E in (E0, E1) for x in sides[0]] + [VE.at[:, 0:LH]],
              high + [E.at[x] for E in (E0, E1) for x in sides[1]] + [VE.at[:, LH + TX:]])
        for BK in (BK0, BK1):
            for x in sides[0] + sides[1]:
                BK[x, INNER, :] = jnp.zeros_like(BK[x, INNER, :])
        ends = slice(0, HY), slice(HY + TY, EY)
        low, high = ([ref.at[:, y] for ref in (E0, E1, BK0, BK1)] + [LX.at[:, :, :, y]] for y in ends)
        clear("gy", low + [YVD], high + [YVU])
        low, high = ([ref.at[x] for ref in (E0, E1, BK0, BK1)] for x in (slice(EX, EX + EG), slice(EX + EG, EX + 2 * EG)))
        clear("gz", low + [LX.at[:, :, HX, 0:TY], VRD], high + [LX.at[:, :, HX + XG, 0:TY], VRU])
        for end, L in ((0, HX), (shape["gz"] - 1, HX + XG)):
            @pl.when(jnp.logical_and(at["gz"] == end, odd))
            def _(L=L):
                LX[:, :, L, TY:, :] = jnp.zeros_like(LX[:, :, L, TY:, :])

    def send_faces():
        copies = [((1, 0, 0), vel.at[:, TX - LH:TX], VE.at[:, 0:LH, OY, :]),
                  ((-1, 0, 0), vel.at[:, 0:LH], VE.at[:, LH + TX:2 * LH + TX, OY, :])]
        for way, src, dst in copies:
            start(src, dst, way, 2 * EACH)
        VE[:, LH:LH + TX, OY, :] = vel[...]
        for c in range(3):
            for i in range(TX // 2):
                for h in range(2):
                    YSU[c, i, LH * h:LH * (h + 1), :] = vel[c, 2 * i + h, TY - LH:TY, :]
                    YSD[c, i, LH * h:LH * (h + 1), :] = vel[c, 2 * i + h, 0:LH, :]
            for g in range(TX // VPK):
                row = None
                for j in range(VPK):
                    turned = pltpu.roll(vel[c, VPK * g + j], (2 * LH * j + LH) % LANES, 1)
                    row = turned if row is None else jnp.where(lane2 // (2 * LH) == j, turned, row)
                SV[c, g] = row
        for way, src, dst in (((0, 1, 0), YSU, YVD), ((0, -1, 0), YSD, YVU),
                              ((0, 0, 1), SV, VRD), ((0, 0, -1), SV, VRU)):
            start(src, dst, way, 2 * EACH)

    def face_tiles(x, y, z):
        return (x * tiles_of(3 * LH, TY, LANES) + y * tiles_of(3 * TX // 2, 2 * LH, LANES)
                + z * tiles_of(3 * TX // VPK, TY, LANES))

    def regular():
        wait_for(recv.at[2 * EACH], face_tiles, AXES)
        for c in range(3):
            for i in range(TX // 2):
                for h in range(2):
                    VE[c, LH + 2 * i + h, HY - LH:HY, :] = YVD[c, i, LH * h:LH * (h + 1), :]
                    VE[c, LH + 2 * i + h, HY + TY:HY + TY + LH, :] = YVU[c, i, LH * h:LH * (h + 1), :]
        rows = lax.broadcasted_iota(jnp.int32, (2 * LANES, LANES), 0)
        cols = lax.broadcasted_iota(jnp.int32, (2 * LANES, LANES), 1)
        r = rows - LANES
        place = jnp.where(rows < LANES, rows, jnp.where(r < LH, r + LANES, r - LANES))
        known = jnp.logical_or(rows < LANES, jnp.logical_or(r < LH, r >= LANES - LH))
        gap = jnp.abs(place - cols)
        band = jnp.zeros((2 * LANES, LANES), jnp.float32)
        for k in range(5):
            tap = (3.0 if k == 0 else 1.0) * LAPLACE_TAPS[k]
            band = jnp.where(jnp.logical_and(known, gap == k), tap, band)
        for c in range(3):
            rims = []
            for g in range(TX // VPK):
                row = jnp.where(lane2 % (2 * LH) < LH, VRD[c, g], VRU[c, g])
                for j in range(VPK):
                    rims.append(pltpu.roll(row, (LANES - (2 * LH * j + LH)) % LANES, 1))
            rims = jnp.concatenate(rims, axis=0)
            own = vel[c].reshape(TX * TY, LANES)
            res = jnp.dot(jnp.concatenate([own, rims], axis=1), band,
                          preferred_element_type=jnp.float32,
                          precision=lax.Precision.HIGHEST).reshape(TX, TY, LANES)
            for k in range(1, 5):
                res = res + LAPLACE_TAPS[k] * (
                    VE[c, LH + k:LH + k + TX, OY, :] + VE[c, LH - k:LH - k + TX, OY, :]
                    + VE[c, LH:LH + TX, HY + k:HY + k + TY, :]
                    + VE[c, LH:LH + TX, HY - k:HY - k + TY, :])
            out[c] = (-REG_WEIGHT) * res

    met = False
    for i in reversed(range(NBX)):
        wait_for(arrive.at[i], lambda: tiles_of(3 * BX, TY, LANES) * 3 // 2, ())
        if i == NBX - 1:
            for copy in later:
                copy.start()
        bx = column(i)
        for j in range(BX):
            E0[HX + bx * BX + j, OY, :] = product(0, bx, j)
        meet = not met and (i == NBX - 1 and NS == 1 or i == 0)
        if meet:
            pl.semaphore_wait(barrier, total)
            forward_x(E0, 0, 0, 0)
        pack_column(E0, 0, bx)
        if meet:
            forward_x(E0, 0, 0, 1)
            met = True
    for i in range(NBX):
        forward_rest(E0, 0, 0, column(i))

    clear_missing()
    send_faces()
    for copy in later:
        copy.wait()
    for i in range(NBX):
        for j in range(BX):
            E1[HX + column(i) * BX + j, OY, :] = product(1, column(i), j)
    YP[:, :, :, 0:TILE] = jnp.zeros_like(YP[:, :, :, 0:TILE])
    YP[:, :, :, TILE + BY:] = jnp.zeros_like(YP[:, :, :, TILE + BY:])
    XP[...] = jnp.zeros_like(XP)

    def enter(E, k, g, side):
        for j in range(HX):
            E[PK * g + j] = LX[k, side, j]
        unpack(LX[k, side, HX], LX[k, side, HX + XG], g)

    def forward(E, n, each):
        forward_pair(n, n)
        wait_rest(n)
        for i in range(NBX):
            g = XG + column(i)
            unpack(E[EX + g], E[EX + EG + g], g)
        for i in range(NBX):
            if i == 0:
                g = group_of(0)
                if NS == 2:
                    far_of(wait_late, n)
                    enter(E, n, g, 1 - up)
                else:
                    unpack(E[EX + g], E[EX + EG + g], g)
            if i == NBX - 1:
                near_of(wait_late, n)
                enter(E, n, group_of(EG - 1), place(up))
            each(i, column(i))

    def first(i, bx):
        for by in range(NBY):
            res = gather_block(E0, 0, bx, by)
            for m in range(BX):
                rows = slice(HY + by * BY, HY + (by + 1) * BY)
                E1[HX + bx * BX + m, rows, :] = E1[HX + bx * BX + m, rows, :] + res[m]
        if i == NBX - 1:
            forward_x(E1, 1, 1, 0)
        pack_column(E1, 1, bx)
        if i == NBX - 1:
            forward_x(E1, 1, 1, 1)
        forward_rest(E1, 1, 1, bx)

    forward(E0, 0, first)

    def second(i, bx):
        for by in range(NBY):
            spread_block(gather_block(E1, 1, bx, by), 1, i, bx, by)

    forward(E1, 1, second)

    def give_back(ACC, BK, k, n):
        collect(k, EG - 1, halo=place(up))
        if NS == 2:
            collect(k, 0, halo=1 - up)
        return_x(k, BK, n, 0)
        for q in range(XG, XG + G):
            collect(k, q, ACC)
        return_rest(ACC, BK, n)
        return_x(k, BK, n, 1)

    def backward(ACC, BK, n, each):
        wait_rest(n)
        for i in range(NBX):
            if i == 0:
                far_of(wait_back, n)
            if i == NBX - 1:
                near_of(wait_back, n)
            each(i, column(i), received(ACC, BK, i))

    give_back(ACC1, BK1, 1, 2)
    regular()

    def third(i, bx, layers):
        for j in range(BX):
            ADJ[bx * BX + j] = layers[j]
        for by in range(NBY):
            spread_block(blocks(layers, by), 0, i, bx, by)

    backward(ACC1, BK1, 2, third)
    def gauss():
        for c in range(3):
            out[c] = out[c] + STEP_SIZE * grad[1, c].astype(jnp.float32) * ADJ[...]

    give_back(ACC0, BK0, 0, 3)
    gauss()

    def fourth(i, bx, layers):
        for c in range(3):
            for j in range(BX):
                x = bx * BX + j
                out[c, x] = out[c, x] + STEP_SIZE * grad[0, c, x].astype(jnp.float32) * layers[j]

    backward(ACC0, BK0, 3, fourth)
    wait_sent()


def body(shape, velocity, gradients, shift_x, shift_y, shift_z, fractions):
    TX, TY, TZ = velocity.shape[1:]
    assert TZ == BZ == LANES and TX % VPK == 0 and TX % BX == 0 and TY % BY == 0
    assert shape["gy"] % 2 == 0 and TX // BX > 1
    assert BX == HX == PK and BY == HY == TILE and XG == 1
    EX, EY = TX + 2 * HX, TY + 2 * HY
    EG = EX // PK
    NS = 2 if shape["gx"] > 2 else 1
    NB = (TX // BX) * (TY // BY)
    most = (2 * STEPS + 1) * EX * EY * (LANES + 2 * HZ) // (TILE * LANES)

    vm = lambda *s: pltpu.VMEM(s, jnp.float32)
    vmem = pl.BlockSpec(memory_space=pltpu.VMEM)
    hbm = pl.BlockSpec(memory_space=pltpu.HBM)
    shift_x, shift_y, shift_z = (s.transpose(0, 1, 3, 2) for s in (shift_x, shift_y, shift_z))
    fractions = fractions.transpose(0, 2, 3, 4, 1)
    return pl.pallas_call(
        functools.partial(kernel, shape),
        out_shape=jax.ShapeDtypeStruct(velocity.shape, jnp.float32),
        in_specs=[hbm] * 6,
        out_specs=vmem,
        scratch_shapes=[
            pltpu.VMEM(velocity.shape, velocity.dtype), pltpu.VMEM(gradients.shape, gradients.dtype),
            *[pltpu.SMEM(s.shape, s.dtype) for s in (shift_x, shift_y, shift_z, fractions)],
            pltpu.SemaphoreType.DMA((TX // BX + 5,)),
            vm(EX + 2 * EG, EY, LANES), vm(EX + 2 * EG, EY, LANES),
            vm(2, NS, HX + 2 * XG, EY, LANES), vm(2, NS, HX + 2 * XG, EY, LANES),
            vm(2, NS, HX + 2 * XG, 2 * HY, LANES), vm(EX, EY, LANES),
            vm(NB, 2, BX + 3, 3 * TILE, LANES), vm(NB, 2, 2 * WX - BX, 5 * TILE, LANES),
            *[vm(EX + 2 * EG, EY, LANES) for _ in range(4)],
            vm(TX, TY, LANES),
            vm(2, 2, EG, EY, LANES),
            vm(3, TX + 2 * LH, EY, LANES),
            vm(3, TX // 2, 2 * LH, LANES), vm(3, TX // 2, 2 * LH, LANES),
            vm(3, TX // 2, 2 * LH, LANES), vm(3, TX // 2, 2 * LH, LANES),
            vm(3, TX // VPK, TY, LANES), vm(3, TX // VPK, TY, LANES), vm(3, TX // VPK, TY, LANES),
            vm(most, TILE, LANES),
            pltpu.SemaphoreType.DMA((1,)), pltpu.SemaphoreType.DMA((2 * (1 + 2 * NS) + 1,)),
        ],
        compiler_params=pltpu.CompilerParams(collective_id=0, has_side_effects=True,
                                             vmem_limit_bytes=24 << 20),
    )(*(pltpu.with_memory_space_constraint(x, pltpu.HBM) for x in (velocity, gradients, shift_x, shift_y, shift_z, fractions)))


def solution(mesh):
    in_specs = (
        P(None, "gx", "gy", "gz"),
        P(None, None, "gx", "gy", "gz"),
        P(None, "gx", "gy", "gz"),
        P(None, "gx", "gy", "gz"),
        P(None, "gx", "gy", "gz"),
        P(None, None, "gx", "gy", "gz"),
    )
    out_specs = P(None, "gx", "gy", "gz")
    return jax.shard_map(functools.partial(body, dict(mesh.shape)), mesh=mesh, in_specs=in_specs,
                         out_specs=out_specs, check_vma=False)
```
